32 devices in a mesh: gx: 4 (over y, core), gy: 8 (over z, x).
Axes of the slice: x: 2, y: 2, z: 4, core: 2. Of those that a mesh axis runs over, the one named last changes fastest.
Arguments:
- density: float32 [80, 80, 384], P('gx', 'gy'), may hold values from 1e-06 to 0.5
- charge: float32 [80, 80, 384], P('gx', 'gy'), may hold values from -6 to 6
Outputs:
- solution_field: float32 [80, 80, 384], P('gx', 'gy')
- residual: float32 [80, 80, 384], P('gx', 'gy')
The draws below stay inside these ranges and needn't reach their ends.
All inputs are finite; a program needn't handle non-finite values.
Results may differ from the reference program's by a relative error of at most 0.0003.
Values sent between devices are 32-bit elements; how exact they have to be, the bound alone decides.
No kernel may reach another device: no remote copies, remote signals or barrier semaphores. Data moves between devices by JAX's collectives and lax.ppermute only.
A program may use at most 64 MiB of HBM per device.

```python
import math
import jax
import jax.numpy as jnp

NZ = 384
ITERS = 1
NX = 80
NY = 80


def block_scale(rng, dims, split, smallest, high):
    def one(axis_at, blocks):
        steps = jax.random.uniform(jax.random.fold_in(jax.random.fold_in(rng, 6), axis_at), (blocks,), jnp.float32, smallest / len(split), high / len(split))
        return jnp.repeat(jnp.exp(steps), dims[axis_at] // blocks).reshape((-1,) + (1,) * (len(dims) - axis_at - 1))

    factor_of = one(*split[0])
    for cut in split[1:]:
        factor_of = factor_of * one(*cut)
    return factor_of


def normal_values(key, shape, deviation, bound, pieces=(), kind=jnp.bfloat16):
    factor_of = block_scale(key, shape, pieces, -0.22, 0.18) if pieces else 1.0
    result = jax.random.normal(key, shape, jnp.float32) * deviation * factor_of
    return jnp.minimum(jnp.maximum(result, -bound), bound).astype(kind)


def setup_inputs(seed: int = 0) -> dict:
    seeds = jax.random.split(jax.random.key(seed), 3)
    density = jnp.clip(jnp.exp(math.log(0.5) - 13.122363 * jax.random.uniform(seeds[0], (NX, NY, NZ), jnp.float32) ** block_scale(seeds[0], (NX, NY, NZ), ((0, 4), (1, 8)), -0.2, 0.2)), 9.999999974752427e-07, 0.5)
    charge = normal_values(seeds[1], (NX, NY, NZ), 1.0, 6.0, ((0, 4), (1, 8)), jnp.float32)
    return {"density": density, "charge": charge}


EPS_SOLVENT = 78.3
RHO_UPPER = 5e-3
RHO_LOWER = 1e-4
KAPPA_SCALE = 0.1
EPS_PRECOND = 20.0
SHIFT_PRECOND = 0.05


def permittivity(density):
    upper = math.log(RHO_UPPER)
    lower = math.log(RHO_LOWER)
    fraction = jnp.clip((upper - jnp.log(density)) / (upper - lower), 0.0, 1.0)
    exponent = fraction - jnp.sin(2.0 * math.pi * fraction) / (2.0 * math.pi)
    return jnp.exp(exponent * math.log(EPS_SOLVENT))


def shifted(values, offset, axis_dim):
    return jnp.roll(values, -offset, axis_dim)


def divergence_term(field, eps, axis_dim):
    grad = (27.0 * (shifted(field, 1, axis_dim) - field) - (shifted(field, 2, axis_dim) - shifted(field, -1, axis_dim))) / 24.0
    flux = (0.5 * (eps + shifted(eps, 1, axis_dim))) * grad
    return (27.0 * (flux - shifted(flux, -1, axis_dim)) - (shifted(flux, 1, axis_dim) - shifted(flux, -2, axis_dim))) / 24.0


def operate(field, eps, kappa):
    total = divergence_term(field, eps, 0) + divergence_term(field, eps, 1) + divergence_term(field, eps, 2)
    return kappa * field - total


def spectrum(length):
    halfang = jnp.arange(length, dtype=jnp.float32) * (math.pi / length)
    return ((27.0 * jnp.sin(halfang) - jnp.sin(3.0 * halfang)) / 12.0) ** 2


def precondition(field):
    symbol = EPS_PRECOND * (spectrum(NX)[:, None, None] + spectrum(NY)[None, :, None] + spectrum(NZ)[None, None, :]) + SHIFT_PRECOND
    return jnp.real(jnp.fft.ifftn(jnp.fft.fftn(field) / symbol)).astype(field.dtype)


def reference(density, charge):
    eps = permittivity(density)
    kappa = KAPPA_SCALE * (eps - 1.0) / (EPS_SOLVENT - 1.0)
    rhs = (4.0 * math.pi) * charge
    solution_field = jnp.zeros_like(rhs)
    residual = rhs
    precond = precondition(residual)
    direction = precond
    inner_now = jnp.sum(residual * precond)
    for stepno in range(ITERS):
        image = operate(direction, eps, kappa)
        alpha = inner_now / jnp.sum(direction * image)
        solution_field = solution_field + alpha * direction
        residual = residual - alpha * image
        if stepno + 1 < ITERS:
            precond = precondition(residual)
            inner_next = jnp.sum(residual * precond)
            direction = precond + (inner_next / inner_now) * direction
            inner_now = inner_next
    return solution_field, residual
```

```python
import math

import jax
import jax.numpy as jnp
import ml_dtypes
import numpy as np
from jax import lax
from jax.experimental import pallas as pl
from jax.experimental.pallas import tpu as pltpu
from jax.sharding import PartitionSpec as P

EPS_SOLVENT = 78.3
RHO_UPPER = 0.005
RHO_LOWER = 0.0001
KAPPA_SCALE = 0.1
EPS_PRECOND = 20.0
SHIFT_PRECOND = 0.05
HIGHEST = lax.Precision.HIGHEST
LANES = 128
HALO = 3
VMEM_LIMIT = 48 << 20


def extended(block, sides, width):
    for axis, dim in sides:
        count = lax.axis_size(axis)
        forward = [(i, i + 1) for i in range(count - 1)]
        forward.append((count - 1, 0))
        backward = [(target, source) for source, target in forward]
        low = lax.ppermute(
            lax.slice_in_dim(block, block.shape[dim] - width, None, axis=dim), axis, forward
        )
        high = lax.ppermute(lax.slice_in_dim(block, 0, width, axis=dim), axis, backward)
        block = jnp.concatenate([low, block, high], axis=dim)
    return block


def permittivity(density):
    upper = math.log(RHO_UPPER)
    lower = math.log(RHO_LOWER)
    fraction = jnp.clip((upper - jnp.log(density)) / (upper - lower), 0.0, 1.0)
    exponent = fraction - jnp.sin(2.0 * math.pi * fraction) / (2.0 * math.pi)
    return jnp.exp(exponent * math.log(EPS_SOLVENT))


def hartley(length):
    indices = jnp.arange(length, dtype=jnp.int32)
    product = indices[:, None] * indices[None, :] % length
    angles = product.astype(jnp.float32) * (2.0 * math.pi / length)
    return jnp.cos(angles) + jnp.sin(angles)


def spectrum(wavenum, length):
    halfang = wavenum.astype(jnp.float32) * (math.pi / length)
    return ((27.0 * jnp.sin(halfang) - jnp.sin(3.0 * halfang)) / 12.0) ** 2


def cutout(values, offset, length, dimen):
    return lax.slice_in_dim(values, offset, offset + length, axis=dimen)


def padded_term(padded, faces, count, dimen):
    nfaces = count + 3
    grad = (
        27.0 * (cutout(padded, 2, nfaces, dimen) - cutout(padded, 1, nfaces, dimen))
        - (cutout(padded, 3, nfaces, dimen) - cutout(padded, 0, nfaces, dimen))
    ) / 24.0
    flux = faces * grad
    return (
        27.0 * (cutout(flux, 2, count, dimen) - cutout(flux, 1, count, dimen))
        - (cutout(flux, 3, count, dimen) - cutout(flux, 0, count, dimen))
    ) / 24.0


def rolled_term(field, faces):
    grad = (
        27.0 * (jnp.roll(field, -1, 2) - field) - (jnp.roll(field, -2, 2) - jnp.roll(field, 1, 2))
    ) / 24.0
    flux = faces * grad
    return (
        27.0 * (flux - jnp.roll(flux, 1, 2)) - (jnp.roll(flux, -1, 2) - jnp.roll(flux, 2, 2))
    ) / 24.0


def operate(field, faces_x, faces_y, faces_z, kappa):
    cellsx = field.shape[0]
    cellsy = field.shape[1]
    padded = extended(field, (("gx", 0), ("gy", 1)), 3)
    term_x = padded_term(padded[:, 3 : 3 + cellsy], faces_x, cellsx, 0)
    term_y = padded_term(padded[3 : 3 + cellsx], faces_y, cellsy, 1)
    term_z = rolled_term(field, faces_z)
    return kappa * field - (term_x + term_y + term_z)


def precondition(field):
    cellsx, cellsy, length_z = field.shape
    size_x = cellsx * lax.axis_size("gx")
    size_y = cellsy * lax.axis_size("gy")
    hart_x = hartley(size_x)
    hart_y = hartley(size_y)
    hart_z = hartley(length_z)
    scaling = float(size_x * size_y * length_z)
    forward = jnp.dot(field, hart_z, precision=HIGHEST)
    zpiece = length_z // lax.axis_size("gx")
    xpiece = size_x // lax.axis_size("gy")
    lines_x = lax.all_to_all(forward, "gx", split_axis=2, concat_axis=0, tiled=True)
    along_x = jnp.einsum("xyk,xa->yka", lines_x, hart_x, precision=HIGHEST)
    lines_y = lax.all_to_all(along_x, "gy", split_axis=2, concat_axis=0, tiled=True)
    along_y = jnp.einsum("ykb,yc->kbc", lines_y, hart_y, precision=HIGHEST)
    wave_z = lax.axis_index("gx") * zpiece + jnp.arange(zpiece, dtype=jnp.int32)
    wave_x = lax.axis_index("gy") * xpiece + jnp.arange(xpiece, dtype=jnp.int32)
    wave_y = jnp.arange(size_y, dtype=jnp.int32)
    symbol = (
        EPS_PRECOND
        * (
            spectrum(wave_z, length_z)[:, None, None]
            + spectrum(wave_x, size_x)[None, :, None]
            + spectrum(wave_y, size_y)[None, None, :]
        )
        + SHIFT_PRECOND
    )
    scaled = along_y / (symbol * scaling)
    back_y = jnp.einsum("kbc,cy->ykb", scaled, hart_y, precision=HIGHEST)
    lines_back = lax.all_to_all(back_y, "gy", split_axis=0, concat_axis=2, tiled=True)
    back_x = jnp.einsum("yka,ax->xyk", lines_back, hart_x, precision=HIGHEST)
    bricks = lax.all_to_all(back_x, "gx", split_axis=0, concat_axis=2, tiled=True)
    return jnp.dot(bricks, hart_z, precision=HIGHEST)


def residual_inner(residual, precond):
    return lax.psum(jnp.sum(residual * precond), ("gx", "gy"))


def local_lines(density, charge):
    eps = permittivity(density)
    kappa = KAPPA_SCALE * (eps - 1.0) / (EPS_SOLVENT - 1.0)
    cellsx = eps.shape[0]
    cellsy = eps.shape[1]
    eps_padded = extended(eps, (("gx", 0), ("gy", 1)), 2)
    strip_x = eps_padded[:, 2 : 2 + cellsy]
    faces_x = 0.5 * (strip_x[:-1] + strip_x[1:])
    strip_y = eps_padded[2 : 2 + cellsx]
    faces_y = 0.5 * (strip_y[:, :-1] + strip_y[:, 1:])
    faces_z = 0.5 * (eps + jnp.roll(eps, -1, 2))
    rhs = 4.0 * math.pi * charge
    residual = rhs
    precond = precondition(residual)
    inner_now = residual_inner(residual, precond)
    image = operate(precond, faces_x, faces_y, faces_z, kappa)
    alpha = inner_now / lax.psum(jnp.sum(precond * image), ("gx", "gy"))
    solution_field = alpha * precond
    residual = residual - alpha * image
    return (solution_field, residual)


def cas_table(rows, columns, length):
    angle = (np.outer(rows, columns) % length).astype(np.float64) * (2.0 * np.pi / length)
    return np.cos(angle) + np.sin(angle)


def symbol_table(length):
    halfang = np.arange(length, dtype=np.float64) * (np.pi / length)
    return ((27.0 * np.sin(halfang) - np.sin(3.0 * halfang)) / 12.0) ** 2


def halves(table):
    high = table.astype(ml_dtypes.bfloat16)
    low = (table - high.astype(np.float64)).astype(ml_dtypes.bfloat16)
    return high, low


def split(values):
    high = values.astype(jnp.bfloat16)
    low = (values - high.astype(jnp.float32)).astype(jnp.bfloat16)
    return high, low


def mul(left, right):
    return jnp.dot(left, right, preferred_element_type=jnp.float32)


def mul_t(left, right):
    return lax.dot_general(
        left, right, (((1,), (1,)), ((), ())), preferred_element_type=jnp.float32
    )


class Plan:
    def __init__(self, cellsx, cellsy, length_z, count_x, count_y):
        self.cx, self.cy, self.nz = cellsx, cellsy, length_z
        self.gx, self.gy = count_x, count_y
        self.nd = count_x * count_y
        self.nx, self.ny = cellsx * count_x, cellsy * count_y
        self.kz = length_z // self.nd
        self.xp = -(-cellsx // 8) * 8
        self.xe = cellsx + 2 * HALO
        self.rows = -(-(self.xe + cellsx) // 8) * 8
        self.xep = -(-self.xe // 8) * 8
        self.group = LANES // max(self.kz, 1)
        self.chunks = -(-self.nd // self.group)

    def fits(self):
        return (
            self.nz % self.nd == 0
            and self.nz % LANES == 0
            and self.cy * self.kz <= LANES
            and (self.cy * self.kz) % 8 == 0
            and 2 * HALO * self.kz <= LANES
            and self.cx >= HALO
            and self.cy >= HALO
            and self.nx <= LANES
            and self.ny % 16 == 0
            and self.gx * self.xep <= LANES
        )

    def z_columns(self):
        wave = np.arange(self.nz)
        place = (wave // self.kz // self.group) * LANES + (
            wave // self.kz % self.group
        ) * self.kz + wave % self.kz
        return place

    def z_forward(self):
        table = np.zeros((self.nz, self.chunks * LANES))
        table[:, self.z_columns()] = cas_table(np.arange(self.nz), np.arange(self.nz), self.nz)
        return halves(table)

    def z_backward(self):
        high, low = self.z_forward()
        return np.ascontiguousarray(high.T), np.ascontiguousarray(low.T)

    def x_forward(self):
        table = np.zeros((LANES, self.gx * self.xp))
        for g in range(self.gx):
            table[: self.nx, g * self.xp : g * self.xp + self.cx] = cas_table(
                np.arange(self.nx), g * self.cx + np.arange(self.cx), self.nx
            )
        high, low = halves(table)
        return np.concatenate([high, low, high], axis=1)

    def y_table(self):
        high, low = halves(cas_table(np.arange(self.ny), np.arange(self.ny), self.ny))
        return np.concatenate([high, low, high], axis=1)

    def x_backward(self):
        extended_rows = np.zeros((self.gx * self.xep, LANES))
        own_rows = np.zeros((self.gx * self.xp, LANES))
        for g in range(self.gx):
            x = (g * self.cx - HALO + np.arange(self.xe)) % self.nx
            extended_rows[g * self.xep : g * self.xep + self.xe, : self.nx] = cas_table(
                x, np.arange(self.nx), self.nx
            )
            x = g * self.cx + np.arange(self.cx)
            own_rows[g * self.xp : g * self.xp + self.cx, : self.nx] = cas_table(
                x, np.arange(self.nx), self.nx
            )
        high, low = halves(np.concatenate([extended_rows, own_rows], axis=0))
        return np.concatenate([high, low, high], axis=1)

    def scales(self):
        lam_x, lam_y, lam_z = symbol_table(self.nx), symbol_table(self.ny), symbol_table(self.nz)
        plane = np.full((self.ny, LANES), 1e30)
        plane[:, : self.nx] = lam_x[None, :] + lam_y[:, None]
        return plane.astype(np.float32), lam_z.reshape(self.nd, self.kz).astype(np.float32)


def call(kernel, outs, args, scratch=(), flops=0):
    vmem = pl.BlockSpec(memory_space=pltpu.VMEM)
    nbytes = sum(int(np.prod(a.shape)) * a.dtype.itemsize for a in (*args, *outs))
    return pl.pallas_call(
        kernel,
        out_shape=tuple(outs),
        in_specs=[vmem] * len(args),
        out_specs=tuple([vmem] * len(outs)),
        scratch_shapes=list(scratch),
        compiler_params=pltpu.CompilerParams(vmem_limit_bytes=VMEM_LIMIT),
        cost_estimate=pl.CostEstimate(flops=flops, bytes_accessed=nbytes, transcendentals=0),
    )(*args)


def lane_index(rows):
    return lax.broadcasted_iota(jnp.int32, (rows, LANES), 1)


def moved(values, shift):
    shift = shift % LANES
    return values if shift == 0 else pltpu.roll(values, shift, 1)


def forward_kernel(plan, charge, high_z, low_z, out):
    p = plan
    gap = jnp.zeros((p.xp - p.cx, p.nz), jnp.float32)
    rows = []
    for y in range(p.cy):
        rows.append(charge[y])
        if p.xp > p.cx:
            rows.append(gap)
    high, low = split(jnp.concatenate(rows, axis=0))
    spec = mul(high, high_z[...]) + mul(low, high_z[...]) + mul(high, low_z[...])
    lane = lane_index(p.xp)
    for target in range(p.nd):
        chunk, slot = divmod(target, p.group)
        block = jnp.zeros((p.xp, LANES), jnp.float32)
        for y in range(p.cy):
            part = spec[y * p.xp : (y + 1) * p.xp, chunk * LANES : (chunk + 1) * LANES]
            part = moved(part, (y - slot) * p.kz)
            block = jnp.where((lane >= y * p.kz) & (lane < (y + 1) * p.kz), part, block)
        out[target] = block


def plane_kernel(plan, lines, x_fwd, y_both, x_bwd, plane, waves, out, turned, planes):
    p = plan
    step = p.cy * p.kz
    field = jnp.concatenate(
        [
            jnp.concatenate([lines[gx * p.gy + gy] for gx in range(p.gx)], axis=0)
            for gy in range(p.gy)
        ],
        axis=1,
    )
    high, low = split(field)
    along_x = mul(x_fwd[...], jnp.concatenate([high, high, low], axis=0))
    for gy in range(p.gy):
        turned[pl.ds(gy * step, LANES), :] = along_x[:, gy * LANES : (gy + 1) * LANES].T
    field = jnp.concatenate(
        [turned[pl.ds(k, p.ny, stride=p.kz), :] for k in range(p.kz)], axis=1
    )
    high, low = split(field)
    along_y = mul(y_both[...], jnp.concatenate([high, high, low], axis=0))
    total = 4.0 * math.pi / float(p.nx * p.ny * p.nz)
    scaled = []
    for k in range(p.kz):
        symbol = EPS_PRECOND * (plane[...] + waves[k]) + SHIFT_PRECOND
        scaled.append(along_y[:, k * LANES : (k + 1) * LANES] * (total / symbol))
    high, low = split(jnp.concatenate(scaled, axis=1))
    back_y = mul(y_both[...], jnp.concatenate([high, high, low], axis=0))
    edge = HALO * p.kz
    base = -(-edge // 8) * 8
    for k in range(p.kz):
        planes[pl.ds(base + k, p.ny, stride=p.kz), :] = back_y[:, k * LANES : (k + 1) * LANES]
    planes[pl.ds(base - edge, edge), :] = planes[pl.ds(base + p.ny * p.kz - edge, edge), :]
    planes[pl.ds(base + p.ny * p.kz, edge), :] = planes[pl.ds(base, edge), :]
    cut = p.gx * p.xep
    for gy in range(p.gy):
        start = base + gy * step
        high, low = split(planes[pl.ds(start, LANES), :])
        ext = mul_t(x_bwd[:cut, :], jnp.concatenate([high, high, low], axis=1))
        sides = jnp.concatenate(
            [
                planes[pl.ds(start - edge, edge), :],
                planes[pl.ds(start + step, edge), :],
                jnp.zeros((LANES - 2 * edge, LANES), jnp.float32),
            ],
            axis=0,
        )
        high, low = split(sides)
        own = mul_t(x_bwd[cut:, :], jnp.concatenate([high, high, low], axis=1))
        for gx in range(p.gx):
            out[gx * p.gy + gy, : p.xe] = ext[gx * p.xep : gx * p.xep + p.xe]
            out[gx * p.gy + gy, p.xe : p.xe + p.cx] = own[gx * p.xp : gx * p.xp + p.cx]
            rest = p.rows - p.xe - p.cx
            if rest:
                out[gx * p.gy + gy, p.xe + p.cx :] = jnp.zeros((rest, LANES), jnp.float32)


def stencil_kernel(
    plan, blocks, high_z, low_z, charge, eps, ex_low, ex_high, ey_low, ey_high,
    pre, image, sums, z_high, z_low, field, eps_x, eps_y,
):
    p = plan
    lane = lane_index(p.xep)
    for chunk in range(p.chunks):
        count = min(p.group, p.nd - chunk * p.group)
        for y in range(p.cy + 2 * HALO):
            inner = HALO <= y < HALO + p.cy
            if inner:
                first, rows, piece = 0, p.xep, y - HALO
                at = piece * p.xep
            else:
                piece = y if y < HALO else y - p.cy
                first, rows = p.xe, p.xp
                at = p.cy * p.xep + piece * p.xp
            line = jnp.zeros((rows, LANES), jnp.float32)
            for slot in range(count):
                part = blocks[chunk * p.group + slot, first : min(first + rows, p.rows), :]
                if part.shape[0] < rows:
                    part = jnp.concatenate(
                        [part, jnp.zeros((rows - part.shape[0], LANES), jnp.float32)], axis=0
                    )
                part = moved(part, (slot - piece) * p.kz)
                here = lane[:rows]
                line = jnp.where((here >= slot * p.kz) & (here < (slot + 1) * p.kz), part, line)
            high, low = split(line)
            z_high[at : at + rows, chunk * LANES : (chunk + 1) * LANES] = high
            z_low[at : at + rows, chunk * LANES : (chunk + 1) * LANES] = low
    whole = (
        mul(z_high[...], high_z[...]) + mul(z_low[...], high_z[...]) + mul(z_high[...], low_z[...])
    )
    for y in range(p.cy):
        field[HALO + y] = whole[y * p.xep : (y + 1) * p.xep]
    for piece in range(2 * HALO):
        at = p.cy * p.xep + piece * p.xp
        y = piece if piece < HALO else piece + p.cy
        field[y, HALO : HALO + p.cx] = whole[at : at + p.cx]
    eps_x[:, 0:2, :] = ex_low[...]
    eps_x[:, 2 : 2 + p.cx, :] = eps[...]
    eps_x[:, 2 + p.cx : 4 + p.cx, :] = ex_high[...]
    eps_y[0:2] = ey_low[...]
    eps_y[2 : 2 + p.cy] = eps[...]
    eps_y[2 + p.cy : 4 + p.cy] = ey_high[...]

    def stretch(flux_at):
        return 27.0 * (flux_at(2) - flux_at(1)) - (flux_at(3) - flux_at(0))

    rz = jnp.zeros((p.cx, LANES), jnp.float32)
    dot = jnp.zeros((p.cx, LANES), jnp.float32)
    faces_y = {}

    def face_y(y):
        if y not in faces_y:
            val = [field[y + i, HALO : HALO + p.cx, :] for i in range(4)]
            grad = 27.0 * (val[2] - val[1]) - (val[3] - val[0])
            faces_y[y] = (eps_y[y] + eps_y[y + 1]) * grad
        return faces_y[y]

    for y in range(p.cy):
        line = field[HALO + y]
        val = [line[i : i + p.cx + 3] for i in range(4)]
        grad = 27.0 * (val[2] - val[1]) - (val[3] - val[0])
        eps_line = eps_x[y]
        flux = (eps_line[0 : p.cx + 3] + eps_line[1 : p.cx + 4]) * grad
        term = stretch(lambda i: flux[i : i + p.cx])
        term = term + stretch(lambda i: face_y(y + i))
        here = line[HALO : HALO + p.cx]
        eps_here = eps[y]
        n = p.nz
        grad = 27.0 * (pltpu.roll(here, n - 1, 1) - here) - (
            pltpu.roll(here, n - 2, 1) - pltpu.roll(here, 1, 1)
        )
        flux = (eps_here + pltpu.roll(eps_here, n - 1, 1)) * grad
        term = term + (
            27.0 * (flux - pltpu.roll(flux, 1, 1))
            - (pltpu.roll(flux, n - 1, 1) - pltpu.roll(flux, 2, 1))
        )
        result = (KAPPA_SCALE / (EPS_SOLVENT - 1.0)) * (eps_here - 1.0) * here - term * (0.5 / 576.0)
        pre[y] = here
        image[y] = result
        one = charge[y] * here
        two = result * here
        for c in range(n // LANES):
            rz = rz + one[:, c * LANES : (c + 1) * LANES]
            dot = dot + two[:, c * LANES : (c + 1) * LANES]
    rz = jnp.sum(rz, axis=0, keepdims=True)
    dot = jnp.sum(dot, axis=0, keepdims=True)
    half = LANES // 2
    rz = rz + pltpu.roll(rz, half, 1)
    dot = dot + pltpu.roll(dot, half, 1)
    both = jnp.where(lane_index(1) < half, rz, dot)
    sums[...] = jnp.broadcast_to(both[None], sums.shape)


def update_kernel(plan, sums, charge, pre, image, solution_field, residual):
    p = plan
    half = LANES // 2
    total = jnp.sum(sums[...], axis=0)
    lane = lane_index(1)
    rz = jnp.sum(jnp.where(lane < half, total, 0.0), axis=1, keepdims=True)
    dot = jnp.sum(jnp.where(lane < half, 0.0, total), axis=1, keepdims=True)
    alpha = jnp.broadcast_to((4.0 * math.pi) * rz / dot, (p.cx, p.nz))
    for y in range(p.cy):
        solution_field[y] = alpha * pre[y]
        residual[y] = (4.0 * math.pi) * charge[y] - alpha * image[y]


def local_planes(plan, density, charge):
    p = plan
    axes = ("gx", "gy")
    f32 = jnp.float32

    def shape(*dims, kind=f32):
        return jax.ShapeDtypeStruct(dims, kind)

    density = density.transpose(1, 0, 2)
    charge = charge.transpose(1, 0, 2)
    high_z, low_z = p.z_forward()
    (lines,) = call(
        lambda *refs: forward_kernel(p, *refs),
        [shape(p.nd, p.xp, LANES)],
        [charge, jnp.asarray(high_z), jnp.asarray(low_z)],
    )
    lines = lax.all_to_all(lines, axes, 0, 0)
    eps = permittivity(density)
    fwd_x = [(i, (i + 1) % p.gx) for i in range(p.gx)]
    fwd_y = [(i, (i + 1) % p.gy) for i in range(p.gy)]
    ex_low = lax.ppermute(eps[:, p.cx - 2 :], "gx", fwd_x)
    ex_high = lax.ppermute(eps[:, :2], "gx", [(b, a) for a, b in fwd_x])
    ey_low = lax.ppermute(eps[p.cy - 2 :], "gy", fwd_y)
    ey_high = lax.ppermute(eps[:2], "gy", [(b, a) for a, b in fwd_y])
    plane, waves = p.scales()
    me = lax.axis_index("gx") * p.gy + lax.axis_index("gy")
    mine = lax.dynamic_slice_in_dim(jnp.asarray(waves), me, 1, axis=0)
    mine = jnp.broadcast_to(mine.reshape(p.kz, 1, 1), (p.kz, 1, LANES))
    edge = -(-HALO * p.kz // 8) * 8
    (blocks,) = call(
        lambda *refs: plane_kernel(p, *refs),
        [shape(p.nd, p.rows, LANES)],
        [
            lines,
            jnp.asarray(p.x_forward()),
            jnp.asarray(p.y_table()),
            jnp.asarray(p.x_backward()),
            jnp.asarray(plane),
            mine,
        ],
        [
            pltpu.VMEM((p.ny * p.kz + LANES, LANES), f32),
            pltpu.VMEM((2 * edge + p.ny * p.kz + LANES, LANES), f32),
        ],
    )
    blocks = lax.all_to_all(blocks, axes, 0, 0)
    back_high, back_low = p.z_backward()
    nrows = p.cy * p.xep + 2 * HALO * p.xp
    pre, image, sums = call(
        lambda *refs: stencil_kernel(p, *refs),
        [shape(p.cy, p.cx, p.nz), shape(p.cy, p.cx, p.nz), shape(p.nd, 1, LANES)],
        [
            blocks, jnp.asarray(back_high), jnp.asarray(back_low), charge,
            eps, ex_low, ex_high, ey_low, ey_high,
        ],
        [
            pltpu.VMEM((nrows, p.chunks * LANES), jnp.bfloat16),
            pltpu.VMEM((nrows, p.chunks * LANES), jnp.bfloat16),
            pltpu.VMEM((p.cy + 2 * HALO, p.xep, p.nz), f32),
            pltpu.VMEM((p.cy, p.cx + 4, p.nz), f32),
            pltpu.VMEM((p.cy + 4, p.cx, p.nz), f32),
        ],
    )
    sums = lax.all_to_all(sums, axes, 0, 0)
    solution_field, residual = call(
        lambda *refs: update_kernel(p, *refs),
        [shape(p.cy, p.cx, p.nz), shape(p.cy, p.cx, p.nz)],
        [sums, charge, pre, image],
    )
    return solution_field.transpose(1, 0, 2), residual.transpose(1, 0, 2)


def local(density, charge):
    cellsx, cellsy, length_z = charge.shape
    plan = Plan(cellsx, cellsy, length_z, lax.axis_size("gx"), lax.axis_size("gy"))
    if plan.fits():
        return local_planes(plan, density, charge)
    return local_lines(density, charge)


def solution(mesh):
    placed = (P("gx", "gy", None), P("gx", "gy", None))
    return jax.shard_map(
        local,
        mesh=mesh,
        in_specs=placed,
        out_specs=(P("gx", "gy", None), P("gx", "gy", None)),
        check_vma=False,
    )
```

```python
import math

import jax
import jax.numpy as jnp
import ml_dtypes
import numpy as np
from jax import lax
from jax.experimental import pallas as pl
from jax.experimental.pallas import tpu as pltpu
from jax.sharding import PartitionSpec as P

EPS_SOLVENT = 78.3
RHO_UPPER = 0.005
RHO_LOWER = 0.0001
KAPPA_SCALE = 0.1
EPS_PRECOND = 20.0
SHIFT_PRECOND = 0.05
HIGHEST = lax.Precision.HIGHEST
LANES = 128
HALO = 3
VMEM_LIMIT = 48 << 20


def extended(block, sides, width):
    for axis, dim in sides:
        count = lax.axis_size(axis)
        forward = [(i, i + 1) for i in range(count - 1)]
        forward.append((count - 1, 0))
        backward = [(target, source) for source, target in forward]
        low = lax.ppermute(
            lax.slice_in_dim(block, block.shape[dim] - width, None, axis=dim), axis, forward
        )
        high = lax.ppermute(lax.slice_in_dim(block, 0, width, axis=dim), axis, backward)
        block = jnp.concatenate([low, block, high], axis=dim)
    return block


def permittivity(density):
    upper = math.log(RHO_UPPER)
    lower = math.log(RHO_LOWER)
    fraction = jnp.clip((upper - jnp.log(density)) / (upper - lower), 0.0, 1.0)
    exponent = fraction - jnp.sin(2.0 * math.pi * fraction) / (2.0 * math.pi)
    return jnp.exp(exponent * math.log(EPS_SOLVENT))


def hartley(length):
    indices = jnp.arange(length, dtype=jnp.int32)
    product = indices[:, None] * indices[None, :] % length
    angles = product.astype(jnp.float32) * (2.0 * math.pi / length)
    return jnp.cos(angles) + jnp.sin(angles)


def spectrum(wavenum, length):
    halfang = wavenum.astype(jnp.float32) * (math.pi / length)
    return ((27.0 * jnp.sin(halfang) - jnp.sin(3.0 * halfang)) / 12.0) ** 2


def cutout(values, offset, length, dimen):
    return lax.slice_in_dim(values, offset, offset + length, axis=dimen)


def padded_term(padded, faces, count, dimen):
    nfaces = count + 3
    grad = (
        27.0 * (cutout(padded, 2, nfaces, dimen) - cutout(padded, 1, nfaces, dimen))
        - (cutout(padded, 3, nfaces, dimen) - cutout(padded, 0, nfaces, dimen))
    ) / 24.0
    flux = faces * grad
    return (
        27.0 * (cutout(flux, 2, count, dimen) - cutout(flux, 1, count, dimen))
        - (cutout(flux, 3, count, dimen) - cutout(flux, 0, count, dimen))
    ) / 24.0


def rolled_term(field, faces):
    grad = (
        27.0 * (jnp.roll(field, -1, 2) - field) - (jnp.roll(field, -2, 2) - jnp.roll(field, 1, 2))
    ) / 24.0
    flux = faces * grad
    return (
        27.0 * (flux - jnp.roll(flux, 1, 2)) - (jnp.roll(flux, -1, 2) - jnp.roll(flux, 2, 2))
    ) / 24.0


def operate(field, faces_x, faces_y, faces_z, kappa):
    cellsx = field.shape[0]
    cellsy = field.shape[1]
    padded = extended(field, (("gx", 0), ("gy", 1)), 3)
    term_x = padded_term(padded[:, 3 : 3 + cellsy], faces_x, cellsx, 0)
    term_y = padded_term(padded[3 : 3 + cellsx], faces_y, cellsy, 1)
    term_z = rolled_term(field, faces_z)
    return kappa * field - (term_x + term_y + term_z)


def precondition(field):
    cellsx, cellsy, length_z = field.shape
    size_x = cellsx * lax.axis_size("gx")
    size_y = cellsy * lax.axis_size("gy")
    hart_x = hartley(size_x)
    hart_y = hartley(size_y)
    hart_z = hartley(length_z)
    scaling = float(size_x * size_y * length_z)
    forward = jnp.dot(field, hart_z, precision=HIGHEST)
    zpiece = length_z // lax.axis_size("gx")
    xpiece = size_x // lax.axis_size("gy")
    lines_x = lax.all_to_all(forward, "gx", split_axis=2, concat_axis=0, tiled=True)
    along_x = jnp.einsum("xyk,xa->yka", lines_x, hart_x, precision=HIGHEST)
    lines_y = lax.all_to_all(along_x, "gy", split_axis=2, concat_axis=0, tiled=True)
    along_y = jnp.einsum("ykb,yc->kbc", lines_y, hart_y, precision=HIGHEST)
    wave_z = lax.axis_index("gx") * zpiece + jnp.arange(zpiece, dtype=jnp.int32)
    wave_x = lax.axis_index("gy") * xpiece + jnp.arange(xpiece, dtype=jnp.int32)
    wave_y = jnp.arange(size_y, dtype=jnp.int32)
    symbol = (
        EPS_PRECOND
        * (
            spectrum(wave_z, length_z)[:, None, None]
            + spectrum(wave_x, size_x)[None, :, None]
            + spectrum(wave_y, size_y)[None, None, :]
        )
        + SHIFT_PRECOND
    )
    scaled = along_y / (symbol * scaling)
    back_y = jnp.einsum("kbc,cy->ykb", scaled, hart_y, precision=HIGHEST)
    lines_back = lax.all_to_all(back_y, "gy", split_axis=0, concat_axis=2, tiled=True)
    back_x = jnp.einsum("yka,ax->xyk", lines_back, hart_x, precision=HIGHEST)
    bricks = lax.all_to_all(back_x, "gx", split_axis=0, concat_axis=2, tiled=True)
    return jnp.dot(bricks, hart_z, precision=HIGHEST)


def residual_inner(residual, precond):
    return lax.psum(jnp.sum(residual * precond), ("gx", "gy"))


def local_lines(density, charge):
    eps = permittivity(density)
    kappa = KAPPA_SCALE * (eps - 1.0) / (EPS_SOLVENT - 1.0)
    cellsx = eps.shape[0]
    cellsy = eps.shape[1]
    eps_padded = extended(eps, (("gx", 0), ("gy", 1)), 2)
    strip_x = eps_padded[:, 2 : 2 + cellsy]
    faces_x = 0.5 * (strip_x[:-1] + strip_x[1:])
    strip_y = eps_padded[2 : 2 + cellsx]
    faces_y = 0.5 * (strip_y[:, :-1] + strip_y[:, 1:])
    faces_z = 0.5 * (eps + jnp.roll(eps, -1, 2))
    rhs = 4.0 * math.pi * charge
    residual = rhs
    precond = precondition(residual)
    inner_now = residual_inner(residual, precond)
    image = operate(precond, faces_x, faces_y, faces_z, kappa)
    alpha = inner_now / lax.psum(jnp.sum(precond * image), ("gx", "gy"))
    solution_field = alpha * precond
    residual = residual - alpha * image
    return (solution_field, residual)


def cas_table(rows, columns, length):
    angle = (np.outer(rows, columns) % length).astype(np.float64) * (2.0 * np.pi / length)
    return np.cos(angle) + np.sin(angle)


def symbol_table(length):
    halfang = np.arange(length, dtype=np.float64) * (np.pi / length)
    return ((27.0 * np.sin(halfang) - np.sin(3.0 * halfang)) / 12.0) ** 2


def halves(table):
    high = table.astype(ml_dtypes.bfloat16)
    low = (table - high.astype(np.float64)).astype(ml_dtypes.bfloat16)
    return high, low


def thirds(table):
    high, low = halves(table)
    return np.concatenate([high, low, high], axis=1)


def split(values):
    high = values.astype(jnp.bfloat16)
    low = (values - high.astype(jnp.float32)).astype(jnp.bfloat16)
    return high, low


def stacked(values, axis):
    high, low = split(values)
    return jnp.concatenate([high, high, low], axis=axis)


def mul(left, right):
    return jnp.dot(left, right, preferred_element_type=jnp.float32)


def mul_t(left, right):
    return lax.dot_general(
        left, right, (((1,), (1,)), ((), ())), preferred_element_type=jnp.float32
    )


def padded_rows(values, rows):
    if values.shape[0] == rows:
        return values
    gap = jnp.zeros((rows - values.shape[0],) + values.shape[1:], values.dtype)
    return jnp.concatenate([values, gap], axis=0)


def up(size, step):
    return -(-size // step) * step


STENCIL = tuple(EPS_PRECOND * c / 576.0 for c in (-783.0, 54.0, -1.0))


class Plan:
    def __init__(self, shape, count_x, count_y):
        size_x, size_y, self.nz = shape
        self.gx, self.gl = count_x, count_y // 2
        self.nx, self.ny = size_x, size_y // 2
        self.cx, self.cy = size_x // count_x, size_y // count_y
        self.ng = self.gx * self.gl
        self.even = count_y % 2 == 0 and self.cy % 2 == 0 and self.ng > 0
        self.kz = self.nz // max(self.ng, 1)
        self.yq = self.cy // 2
        self.xp = up(self.cx, 8)
        self.xe = self.cx + 2 * HALO
        self.xw = up(self.xe, 8)
        self.yp = up(self.ny, 16)
        self.step = self.yq * self.kz
        self.edge = HALO * self.kz
        self.group = LANES // max(self.kz, 1)
        self.chunks = -(-self.ng // self.group)
        self.deep = self.chunks * LANES
        self.extra = self.cx // self.yq if self.yq else 0
        self.rows = up(2 * self.xe + self.cx + self.extra, 8)
        self.lines = self.cy * self.xw + (2 * HALO - 1) * self.xp + self.yq * 8

    def fits(self):
        return (
            self.even
            and self.nz % (self.ng * 8) == 0
            and self.nz % LANES == 0
            and self.yq == 2 * HALO - 1
            and self.cx == 4 * self.yq
            and self.step <= LANES
            and self.step % 8 == 0
            and self.nx <= LANES
            and 2 * (LANES - self.nx) >= self.nx
            and self.nx % 16 == 0
            and self.ny >= 2 * HALO
            and self.gx * self.xw <= LANES
        )

    def z_forward(self):
        wave = np.arange(self.nz)
        owner = wave // self.kz
        place = owner // self.group * LANES + owner % self.group * self.kz + wave % self.kz
        table = np.zeros((self.nz, self.deep))
        table[:, place] = cas_table(wave, wave, self.nz)
        return halves(table)

    def z_backward(self):
        return tuple(np.ascontiguousarray(part.T) for part in self.z_forward())

    def x_forward(self):
        table = np.zeros((LANES, self.nx))
        table[: self.nx] = cas_table(np.arange(self.nx), np.arange(self.nx), self.nx)
        return thirds(table)

    def y_both(self):
        table = np.zeros((self.ny, self.yp))
        table[:, : self.ny] = cas_table(np.arange(self.ny), np.arange(self.ny), self.ny)
        return thirds(table)

    def ends(self):
        low = np.arange(HALO)
        return np.concatenate([low, self.ny - 1 - low])

    def y_ends(self):
        table = np.zeros((8, self.yp))
        table[: 2 * HALO, : self.ny] = cas_table(self.ends(), np.arange(self.ny), self.ny)
        return thirds(table)

    def y_sources(self):
        columns = cas_table(np.arange(self.ny), self.ends(), self.ny).T
        wide = np.broadcast_to(columns[:, :, None], (2 * HALO, self.ny, LANES))
        return np.ascontiguousarray(wide).astype(np.float32)

    def x_backward(self):
        wide = np.zeros((self.gx * self.xw, LANES))
        own = np.zeros((self.gx * self.xp, LANES))
        waves = np.arange(self.nx)
        for g in range(self.gx):
            x = (g * self.cx - HALO + np.arange(self.xe)) % self.nx
            wide[g * self.xw : g * self.xw + self.xe, : self.nx] = cas_table(x, waves, self.nx)
            x = g * self.cx + np.arange(self.cx)
            own[g * self.xp : g * self.xp + self.cx, : self.nx] = cas_table(x, waves, self.nx)
        scale = 4.0 * np.pi / (self.nx * self.nz)
        return thirds(np.concatenate([wide, own], axis=0) * scale)

    def plane(self):
        plane = np.full((self.ny, LANES), 1e30)
        plane[:, : self.nx] = symbol_table(self.nx)[None, :] + symbol_table(self.ny)[:, None]
        return plane.astype(np.float32)

    def waves(self):
        return symbol_table(self.nz).reshape(self.ng, self.kz).astype(np.float32)

    def joins(self):
        lam_x, lam_y, lam_z = symbol_table(self.nx), symbol_table(self.ny), symbol_table(self.nz)
        total = EPS_PRECOND * (lam_z[:, None, None] + lam_x[None, :, None] + lam_y) + SHIFT_PRECOND
        green = np.real(np.fft.ifft(1.0 / total, axis=-1))
        i = np.arange(HALO)
        near = green[..., np.abs(i[:, None] - i[None, :])]
        far = green[..., i[:, None] + i[None, :] + 1]
        band = np.zeros((HALO, HALO))
        for row in range(HALO):
            for column in range(HALO - row):
                band[row, column] = STENCIL[row + column]
        eye = np.eye(HALO)
        even = np.linalg.inv(eye - 2.0 * (near + far) @ band)
        odd = np.linalg.inv(eye + 2.0 * (near - far) @ band)
        both = np.stack([even, odd], axis=2).reshape(self.nz, self.nx, 2 * HALO * HALO)
        table = np.zeros((self.ng, 2 * HALO * HALO, self.kz, LANES), np.float32)
        table[..., : self.nx] = both.reshape(self.ng, self.kz, self.nx, -1).transpose(0, 3, 1, 2)
        return table


VMEM_SPEC = pl.BlockSpec(memory_space=pltpu.VMEM)
ANY_SPEC = pl.BlockSpec(memory_space=pl.ANY)


def call(kernel, outs, args, scratch=(), specs=None):
    nbytes = sum(int(np.prod(a.shape)) * a.dtype.itemsize for a in (*args, *outs))
    return pl.pallas_call(
        kernel,
        out_shape=tuple(outs),
        in_specs=specs or [VMEM_SPEC] * len(args),
        out_specs=tuple([VMEM_SPEC] * len(outs)),
        scratch_shapes=list(scratch),
        compiler_params=pltpu.CompilerParams(vmem_limit_bytes=VMEM_LIMIT),
        cost_estimate=pl.CostEstimate(flops=0, bytes_accessed=nbytes, transcendentals=0),
    )(*args)


def lane_index(rows):
    return lax.broadcasted_iota(jnp.int32, (rows, LANES), 1)


def moved(values, shift):
    shift = shift % LANES
    return values if shift == 0 else pltpu.roll(values, shift, 1)


def between(lane, slot, width):
    return (lane >= slot * width) & (lane < (slot + 1) * width)


def forward_kernel(p, charge_in, high_in, low_in, out, charge, high_z, low_z, sems):
    copies = [
        pltpu.make_async_copy(source, target, sems.at[i])
        for i, (source, target) in enumerate(
            ((charge_in, charge), (high_in, high_z), (low_in, low_z))
        )
    ]
    for copy in copies:
        copy.start()
    copies[0].wait()
    rows = [padded_rows(charge[y], p.xp) for y in range(p.cy)]
    high, low = split(jnp.concatenate(rows, axis=0))
    copies[1].wait()
    spec = mul(high, high_z[...]) + mul(low, high_z[...])
    copies[2].wait()
    spec = spec + mul(high, low_z[...])
    lane = lane_index(p.xp)
    for target in range(p.ng):
        chunk, slot = divmod(target, p.group)
        for part in range(2):
            block = jnp.zeros((p.xp, LANES), jnp.float32)
            for i in range(p.yq):
                y = part * p.yq + i
                piece = spec[y * p.xp : (y + 1) * p.xp, chunk * LANES : (chunk + 1) * LANES]
                block = jnp.where(between(lane, i, p.kz), moved(piece, (i - slot) * p.kz), block)
            out[target, part * p.cx : (part + 1) * p.cx] = block[: p.cx]


def table_kernel(p, plane, waves, out):
    for k in range(p.kz):
        symbol = EPS_PRECOND * (plane[...] + waves[k]) + SHIFT_PRECOND
        out[:, k * LANES : (k + 1) * LANES] = 1.0 / (float(p.ny) * symbol)


def lanes_of(values, k):
    return values[:, k * LANES : (k + 1) * LANES]


def solve_kernel(p, blocks, x_fwd, y_both, y_ends, table, spectrum_out, own, sent, turned, ends):
    columns = []
    for gl in range(p.gl):
        for part in range(2):
            pieces = [
                blocks[gx * p.gl + gl, part * p.cx : (part + 1) * p.cx] for gx in range(p.gx)
            ]
            columns.append(jnp.concatenate(pieces, axis=0))
    along_x = mul(x_fwd[...], stacked(jnp.concatenate(columns, axis=1), 0))
    for b in range(2 * p.gl):
        turned[pl.ds(b * p.step, LANES), :] = lanes_of(along_x, b).T
    field = jnp.concatenate(
        [turned[pl.ds(k, p.ny, stride=p.kz), :] for k in range(p.kz)], axis=1
    )
    along_y = mul(y_both[...], stacked(padded_rows(field, p.yp), 0))
    solved = along_y * table[...]
    spectrum_out[...] = solved
    at_ends = mul(y_ends[...], stacked(padded_rows(solved, p.yp), 0))
    for k in range(p.kz):
        ends[pl.ds(k, 8, stride=p.kz), :] = lanes_of(at_ends, k)
    own[...] = ends[pl.ds(0, 2 * HALO * p.kz), :]
    piece = [ends[pl.ds(j * p.kz, p.kz), :] for j in range(2 * HALO)]
    lane = lane_index(p.kz)
    free = LANES - p.nx
    for i in range(4):
        spare = moved(piece[4 + i // 2], p.nx if i % 2 == 0 else p.nx - free)
        sent[pl.ds(i * p.kz, p.kz), :] = jnp.where(lane < p.nx, piece[i], spare)


def return_kernel(
    p, spectrum_in, own, received, table, joins, y_both, y_sources, x_bwd,
    out, sources, planes,
):
    lane = lane_index(p.kz)
    free = LANES - p.nx
    part = [received[pl.ds(i * p.kz, p.kz), :] for i in range(4)]
    other = [jnp.where(lane < p.nx, value, 0.0) for value in part]
    for i in range(2):
        first = moved(part[2 * i], -p.nx)
        second = moved(part[2 * i + 1], free - p.nx)
        other.append(jnp.where(lane < free, first, jnp.where(lane < p.nx, second, 0.0)))
    mine = [own[pl.ds(j * p.kz, p.kz), :] for j in range(2 * HALO)]
    jump = [mine[j] - other[j] for j in range(2 * HALO)]
    even = [jump[j] + jump[HALO + j] for j in range(HALO)]
    odd = [jump[j] - jump[HALO + j] for j in range(HALO)]

    def mixed(base, vector):
        return [
            sum(joins[base + HALO * i + j] * vector[j] for j in range(HALO)) for i in range(HALO)
        ]

    even_full, odd_full = mixed(0, even), mixed(HALO * HALO, odd)
    low_full = [0.5 * (e + o) for e, o in zip(even_full, odd_full)]
    high_full = [0.5 * (e - o) for e, o in zip(even_full, odd_full)]
    far_low = [other[j] - 0.5 * (low_full[j] - jump[j]) for j in range(HALO)]
    far_high = [other[HALO + j] - 0.5 * (high_full[j] - jump[HALO + j]) for j in range(HALO)]
    for i in range(HALO):
        sources[pl.ds(i * p.kz, p.kz), :] = sum(
            STENCIL[i + j] * high_full[j] for j in range(HALO - i)
        )
        sources[pl.ds((HALO + i) * p.kz, p.kz), :] = sum(
            STENCIL[i + j] * low_full[j] for j in range(HALO - i)
        )
    whole = []
    for k in range(p.kz):
        added = sum(y_sources[j] * sources[pl.ds(j * p.kz + k, 1), :] for j in range(2 * HALO))
        whole.append(
            spectrum_in[:, k * LANES : (k + 1) * LANES]
            + added * table[:, k * LANES : (k + 1) * LANES]
        )
    back_y = mul(y_both[...], stacked(padded_rows(jnp.concatenate(whole, axis=1), p.yp), 0))
    base = p.edge
    for k in range(p.kz):
        planes[pl.ds(base + k, p.ny, stride=p.kz), :] = lanes_of(back_y, k)
    after = base + p.ny * p.kz
    for i in range(HALO):
        planes[pl.ds(base - (i + 1) * p.kz, p.kz), :] = far_high[i]
        planes[pl.ds(after + i * p.kz, p.kz), :] = far_low[i]
    cut = p.gx * p.xw
    wide_rows = x_bwd[:cut, :]
    own_rows = x_bwd[cut:, :]
    gap = jnp.zeros((LANES - p.step, LANES), jnp.float32)
    slots = lane_index(p.extra)
    rest = p.rows - 2 * p.xe - p.cx - p.extra
    for gl in range(p.gl):
        start = base + gl * 2 * p.step
        end = start + 2 * p.step
        last = planes[pl.ds(end + p.edge - p.kz, p.kz), :]
        both = jnp.concatenate(
            [planes[pl.ds(start, LANES), :], planes[pl.ds(start + p.step, LANES), :]], axis=0
        )
        wide = mul_t(wide_rows, stacked(both, 1))
        sides = jnp.concatenate(
            [
                planes[pl.ds(start - p.edge, p.edge), :],
                planes[pl.ds(end, p.edge - p.kz), :],
                gap,
                *[last] * p.yq,
                gap,
            ],
            axis=0,
        )
        side = mul_t(own_rows, stacked(sides, 1))
        for gx in range(p.gx):
            target = gx * p.gl + gl
            for half in range(2):
                out[target, half * p.xe : (half + 1) * p.xe] = wide[
                    gx * p.xw : gx * p.xw + p.xe, half * LANES : (half + 1) * LANES
                ]
            at, line = 2 * p.xe, gx * p.xp
            out[target, at : at + p.cx] = side[line : line + p.cx, :LANES]
            at += p.cx
            extra = jnp.zeros((p.extra, LANES), jnp.float32)
            for q in range(p.yq):
                value = side[line + q * p.extra : line + (q + 1) * p.extra, LANES:]
                extra = jnp.where(between(slots, q, p.kz), value, extra)
            out[target, at : at + p.extra] = extra
            if rest:
                out[target, at + p.extra :] = jnp.zeros((rest, LANES), jnp.float32)


def stencil_kernel(
    p, blocks, high_z, low_z, charge, eps, ex_low, ex_high, ey_low, ey_high,
    pre, image, sums, lines, field, eps_x, eps_y,
):
    lane = lane_index(p.xw)
    windows, at = [], 0
    for y in range(p.cy):
        half = y // p.yq
        windows.append((half * p.xe // 8 * 8, p.xw, y % p.yq, at))
        at += p.xw
    side = 2 * p.xe
    for h in range(2 * HALO - 1):
        windows.append((side // 8 * 8, p.xp, h, at))
        at += p.xp
    tail = side + p.cx
    for q in range(p.yq):
        windows.append((tail // 8 * 8, 8, q, at))
        at += 8
    for chunk in range(p.chunks):
        count = min(p.group, p.ng - chunk * p.group)
        for first, rows, piece, at in windows:
            here = lane[:rows]
            line = jnp.zeros((rows, LANES), jnp.float32)
            for slot in range(count):
                part = blocks[chunk * p.group + slot, first : first + rows, :]
                part = moved(part, (slot - piece) * p.kz)
                line = jnp.where(between(here, slot, p.kz), part, line)
            lines[at : at + rows, chunk * LANES : (chunk + 1) * LANES] = line
    high, low = split(lines[...])
    whole = mul(high, high_z[...]) + mul(low, high_z[...]) + mul(high, low_z[...])
    for y in range(p.cy):
        first, rows, piece, at = windows[y]
        off = (y // p.yq) * p.xe - first
        field[HALO + y, : p.xe] = whole[at + off : at + off + p.xe]
    for h in range(2 * HALO - 1):
        first, rows, piece, at = windows[p.cy + h]
        off = side - first
        y = h if h < HALO else h + p.cy
        field[y, HALO : HALO + p.cx] = whole[at + off : at + off + p.cx]
    for q in range(p.yq):
        first, rows, piece, at = windows[p.cy + 2 * HALO - 1 + q]
        off = tail - first
        field[p.cy + 2 * HALO - 1, HALO + q * p.extra : HALO + (q + 1) * p.extra] = whole[
            at + off : at + off + p.extra
        ]
    eps_x[:, 0:2, :] = ex_low[...]
    eps_x[:, 2 : 2 + p.cx, :] = eps[...]
    eps_x[:, 2 + p.cx : 4 + p.cx, :] = ex_high[...]
    eps_y[0:2] = ey_low[...]
    eps_y[2 : 2 + p.cy] = eps[...]
    eps_y[2 + p.cy : 4 + p.cy] = ey_high[...]

    def stretch(flux_at):
        return 27.0 * (flux_at(2) - flux_at(1)) - (flux_at(3) - flux_at(0))

    rz = jnp.zeros((p.cx, LANES), jnp.float32)
    dot = jnp.zeros((p.cx, LANES), jnp.float32)
    faces_y = {}

    def face_y(y):
        if y not in faces_y:
            val = [field[y + i, HALO : HALO + p.cx, :] for i in range(4)]
            grad = 27.0 * (val[2] - val[1]) - (val[3] - val[0])
            faces_y[y] = (eps_y[y] + eps_y[y + 1]) * grad
        return faces_y[y]

    for y in range(p.cy):
        line = field[HALO + y]
        val = [line[i : i + p.cx + 3] for i in range(4)]
        grad = 27.0 * (val[2] - val[1]) - (val[3] - val[0])
        eps_line = eps_x[y]
        flux = (eps_line[0 : p.cx + 3] + eps_line[1 : p.cx + 4]) * grad
        term = stretch(lambda i: flux[i : i + p.cx])
        term = term + stretch(lambda i: face_y(y + i))
        here = line[HALO : HALO + p.cx]
        eps_here = eps[y]
        n = p.nz
        grad = 27.0 * (pltpu.roll(here, n - 1, 1) - here) - (
            pltpu.roll(here, n - 2, 1) - pltpu.roll(here, 1, 1)
        )
        flux = (eps_here + pltpu.roll(eps_here, n - 1, 1)) * grad
        term = term + (
            27.0 * (flux - pltpu.roll(flux, 1, 1))
            - (pltpu.roll(flux, n - 1, 1) - pltpu.roll(flux, 2, 1))
        )
        result = (KAPPA_SCALE / (EPS_SOLVENT - 1.0)) * (eps_here - 1.0) * here - term * (0.5 / 576.0)
        pre[y] = here
        image[y] = result
        one = charge[y] * here
        two = result * here
        for c in range(n // LANES):
            rz = rz + one[:, c * LANES : (c + 1) * LANES]
            dot = dot + two[:, c * LANES : (c + 1) * LANES]
    rz = jnp.sum(rz, axis=0, keepdims=True)
    dot = jnp.sum(dot, axis=0, keepdims=True)
    half = LANES // 2
    rz = rz + pltpu.roll(rz, half, 1)
    dot = dot + pltpu.roll(dot, half, 1)
    both = jnp.where(lane_index(1) < half, rz, dot)
    sums[...] = jnp.broadcast_to(both[None], sums.shape)


def update_kernel(p, sums, charge, pre, image, solution_field, residual):
    half = LANES // 2
    total = jnp.sum(sums[...], axis=0)
    lane = lane_index(1)
    rz = jnp.sum(jnp.where(lane < half, total, 0.0), axis=1, keepdims=True)
    dot = jnp.sum(jnp.where(lane < half, 0.0, total), axis=1, keepdims=True)
    alpha = jnp.broadcast_to((4.0 * math.pi) * rz / dot, (p.cx, p.nz))
    for y in range(p.cy):
        solution_field[y] = alpha * pre[y]
        residual[y] = (4.0 * math.pi) * charge[y] - alpha * image[y]


def local_planes(p, density, charge):
    group = ("gx", "gl")
    along_y = ("gh", "gl")
    f32, bf16 = jnp.float32, jnp.bfloat16

    def shape(*dims):
        return jax.ShapeDtypeStruct(dims, f32)

    def ring(count):
        return [(i, (i + 1) % count) for i in range(count)]

    def back(pairs):
        return [(target, source) for source, target in pairs]

    density = density.transpose(1, 0, 2)
    charge = charge.transpose(1, 0, 2)
    high_z, low_z = p.z_forward()
    (blocks,) = call(
        lambda *refs: forward_kernel(p, *refs),
        [shape(p.ng, 2 * p.cx, LANES)],
        [charge, jnp.asarray(high_z), jnp.asarray(low_z)],
        [
            pltpu.VMEM((p.cy, p.cx, p.nz), f32),
            pltpu.VMEM((p.nz, p.deep), bf16),
            pltpu.VMEM((p.nz, p.deep), bf16),
            pltpu.SemaphoreType.DMA((3,)),
        ],
        specs=[ANY_SPEC] * 3,
    )
    blocks = lax.all_to_all(blocks, group, 0, 0)
    eps = permittivity(density)
    ex_low = lax.ppermute(eps[:, p.cx - 2 :], "gx", ring(p.gx))
    ex_high = lax.ppermute(eps[:, :2], "gx", back(ring(p.gx)))
    ey_low = lax.ppermute(eps[p.cy - 2 :], along_y, ring(2 * p.gl))
    ey_high = lax.ppermute(eps[:2], along_y, back(ring(2 * p.gl)))
    me = lax.axis_index("gx") * p.gl + lax.axis_index("gl")
    waves = lax.dynamic_slice_in_dim(jnp.asarray(p.waves()), me, 1, axis=0)
    waves = jnp.broadcast_to(waves.reshape(p.kz, 1, 1), (p.kz, 1, LANES))
    joins = lax.dynamic_index_in_dim(jnp.asarray(p.joins()), me, 0, keepdims=False)
    (table,) = call(
        lambda *refs: table_kernel(p, *refs),
        [shape(p.ny, p.kz * LANES)],
        [jnp.asarray(p.plane()), waves],
    )
    y_both = jnp.asarray(p.y_both())
    spectrum_half, own, sent = call(
        lambda *refs: solve_kernel(p, *refs),
        [shape(p.ny, p.kz * LANES), shape(2 * HALO * p.kz, LANES), shape(4 * p.kz, LANES)],
        [blocks, jnp.asarray(p.x_forward()), y_both, jnp.asarray(p.y_ends()), table],
        [pltpu.VMEM((p.ny * p.kz + LANES, LANES), f32), pltpu.VMEM((8 * p.kz, LANES), f32)],
    )
    received = lax.ppermute(sent, "gh", [(0, 1), (1, 0)])
    (blocks,) = call(
        lambda *refs: return_kernel(p, *refs),
        [shape(p.ng, p.rows, LANES)],
        [
            spectrum_half, own, received, table, joins, y_both,
            jnp.asarray(p.y_sources()), jnp.asarray(p.x_backward()),
        ],
        [
            pltpu.VMEM((2 * HALO * p.kz, LANES), f32),
            pltpu.VMEM((p.ny * p.kz + 2 * p.edge, LANES), f32),
        ],
    )
    blocks = lax.all_to_all(blocks, group, 0, 0)
    back_high, back_low = p.z_backward()
    pre, image, sums = call(
        lambda *refs: stencil_kernel(p, *refs),
        [shape(p.cy, p.cx, p.nz), shape(p.cy, p.cx, p.nz), shape(2 * p.ng, 1, LANES)],
        [
            blocks, jnp.asarray(back_high), jnp.asarray(back_low), charge,
            eps, ex_low, ex_high, ey_low, ey_high,
        ],
        [
            pltpu.VMEM((p.lines, p.deep), f32),
            pltpu.VMEM((p.cy + 2 * HALO, p.xw, p.nz), f32),
            pltpu.VMEM((p.cy, p.cx + 4, p.nz), f32),
            pltpu.VMEM((p.cy + 4, p.cx, p.nz), f32),
        ],
    )
    sums = lax.all_to_all(sums, ("gx", "gh", "gl"), 0, 0)
    solution_field, residual = call(
        lambda *refs: update_kernel(p, *refs),
        [shape(p.cy, p.cx, p.nz), shape(p.cy, p.cx, p.nz)],
        [sums, charge, pre, image],
    )
    return solution_field.transpose(1, 0, 2), residual.transpose(1, 0, 2)


def solution(mesh):
    count_x, count_y = mesh.shape["gx"], mesh.shape["gy"]

    def run(density, charge):
        plan = Plan(charge.shape, count_x, count_y)
        if plan.fits():
            split_mesh = jax.sharding.Mesh(
                mesh.devices.reshape(count_x, 2, count_y // 2), ("gx", "gh", "gl")
            )
            spec = P("gx", ("gh", "gl"), None)
            body, over = (lambda *args: local_planes(plan, *args)), split_mesh
        else:
            spec = P("gx", "gy", None)
            body, over = local_lines, mesh
        return jax.shard_map(
            body, mesh=over, in_specs=(spec, spec), out_specs=(spec, spec), check_vma=False
        )(density, charge)

    return run
```

```python
import math

import jax
import jax.numpy as jnp
import ml_dtypes
import numpy as np
from jax import lax
from jax.experimental import pallas as pl
from jax.experimental.pallas import tpu as pltpu
from jax.sharding import PartitionSpec as P

EPS_SOLVENT = 78.3
RHO_UPPER = 0.005
RHO_LOWER = 0.0001
KAPPA_SCALE = 0.1
EPS_PRECOND = 20.0
SHIFT_PRECOND = 0.05
HIGHEST = lax.Precision.HIGHEST
LANES = 128
HALO = 3
VMEM_LIMIT = 48 << 20


def extended(block, sides, width):
    for axis, dim in sides:
        count = lax.axis_size(axis)
        forward = [(i, i + 1) for i in range(count - 1)]
        forward.append((count - 1, 0))
        backward = [(target, source) for source, target in forward]
        low = lax.ppermute(
            lax.slice_in_dim(block, block.shape[dim] - width, None, axis=dim), axis, forward
        )
        high = lax.ppermute(lax.slice_in_dim(block, 0, width, axis=dim), axis, backward)
        block = jnp.concatenate([low, block, high], axis=dim)
    return block


def permittivity(density):
    upper = math.log(RHO_UPPER)
    lower = math.log(RHO_LOWER)
    fraction = jnp.clip((upper - jnp.log(density)) / (upper - lower), 0.0, 1.0)
    exponent = fraction - jnp.sin(2.0 * math.pi * fraction) / (2.0 * math.pi)
    return jnp.exp(exponent * math.log(EPS_SOLVENT))


def hartley(length):
    indices = jnp.arange(length, dtype=jnp.int32)
    product = indices[:, None] * indices[None, :] % length
    angles = product.astype(jnp.float32) * (2.0 * math.pi / length)
    return jnp.cos(angles) + jnp.sin(angles)


def spectrum(wavenum, length):
    halfang = wavenum.astype(jnp.float32) * (math.pi / length)
    return ((27.0 * jnp.sin(halfang) - jnp.sin(3.0 * halfang)) / 12.0) ** 2


def cutout(values, offset, length, dimen):
    return lax.slice_in_dim(values, offset, offset + length, axis=dimen)


def padded_term(padded, faces, count, dimen):
    nfaces = count + 3
    grad = (
        27.0 * (cutout(padded, 2, nfaces, dimen) - cutout(padded, 1, nfaces, dimen))
        - (cutout(padded, 3, nfaces, dimen) - cutout(padded, 0, nfaces, dimen))
    ) / 24.0
    flux = faces * grad
    return (
        27.0 * (cutout(flux, 2, count, dimen) - cutout(flux, 1, count, dimen))
        - (cutout(flux, 3, count, dimen) - cutout(flux, 0, count, dimen))
    ) / 24.0


def rolled_term(field, faces):
    grad = (
        27.0 * (jnp.roll(field, -1, 2) - field) - (jnp.roll(field, -2, 2) - jnp.roll(field, 1, 2))
    ) / 24.0
    flux = faces * grad
    return (
        27.0 * (flux - jnp.roll(flux, 1, 2)) - (jnp.roll(flux, -1, 2) - jnp.roll(flux, 2, 2))
    ) / 24.0


def operate(field, faces_x, faces_y, faces_z, kappa):
    cellsx = field.shape[0]
    cellsy = field.shape[1]
    padded = extended(field, (("gx", 0), ("gy", 1)), 3)
    term_x = padded_term(padded[:, 3 : 3 + cellsy], faces_x, cellsx, 0)
    term_y = padded_term(padded[3 : 3 + cellsx], faces_y, cellsy, 1)
    term_z = rolled_term(field, faces_z)
    return kappa * field - (term_x + term_y + term_z)


def precondition(field):
    cellsx, cellsy, length_z = field.shape
    size_x = cellsx * lax.axis_size("gx")
    size_y = cellsy * lax.axis_size("gy")
    hart_x = hartley(size_x)
    hart_y = hartley(size_y)
    hart_z = hartley(length_z)
    scaling = float(size_x * size_y * length_z)
    forward = jnp.dot(field, hart_z, precision=HIGHEST)
    zpiece = length_z // lax.axis_size("gx")
    xpiece = size_x // lax.axis_size("gy")
    lines_x = lax.all_to_all(forward, "gx", split_axis=2, concat_axis=0, tiled=True)
    along_x = jnp.einsum("xyk,xa->yka", lines_x, hart_x, precision=HIGHEST)
    lines_y = lax.all_to_all(along_x, "gy", split_axis=2, concat_axis=0, tiled=True)
    along_y = jnp.einsum("ykb,yc->kbc", lines_y, hart_y, precision=HIGHEST)
    wave_z = lax.axis_index("gx") * zpiece + jnp.arange(zpiece, dtype=jnp.int32)
    wave_x = lax.axis_index("gy") * xpiece + jnp.arange(xpiece, dtype=jnp.int32)
    wave_y = jnp.arange(size_y, dtype=jnp.int32)
    symbol = (
        EPS_PRECOND
        * (
            spectrum(wave_z, length_z)[:, None, None]
            + spectrum(wave_x, size_x)[None, :, None]
            + spectrum(wave_y, size_y)[None, None, :]
        )
        + SHIFT_PRECOND
    )
    scaled = along_y / (symbol * scaling)
    back_y = jnp.einsum("kbc,cy->ykb", scaled, hart_y, precision=HIGHEST)
    lines_back = lax.all_to_all(back_y, "gy", split_axis=0, concat_axis=2, tiled=True)
    back_x = jnp.einsum("yka,ax->xyk", lines_back, hart_x, precision=HIGHEST)
    bricks = lax.all_to_all(back_x, "gx", split_axis=0, concat_axis=2, tiled=True)
    return jnp.dot(bricks, hart_z, precision=HIGHEST)


def residual_inner(residual, precond):
    return lax.psum(jnp.sum(residual * precond), ("gx", "gy"))


def local_lines(density, charge):
    eps = permittivity(density)
    kappa = KAPPA_SCALE * (eps - 1.0) / (EPS_SOLVENT - 1.0)
    cellsx = eps.shape[0]
    cellsy = eps.shape[1]
    eps_padded = extended(eps, (("gx", 0), ("gy", 1)), 2)
    strip_x = eps_padded[:, 2 : 2 + cellsy]
    faces_x = 0.5 * (strip_x[:-1] + strip_x[1:])
    strip_y = eps_padded[2 : 2 + cellsx]
    faces_y = 0.5 * (strip_y[:, :-1] + strip_y[:, 1:])
    faces_z = 0.5 * (eps + jnp.roll(eps, -1, 2))
    rhs = 4.0 * math.pi * charge
    residual = rhs
    precond = precondition(residual)
    inner_now = residual_inner(residual, precond)
    image = operate(precond, faces_x, faces_y, faces_z, kappa)
    alpha = inner_now / lax.psum(jnp.sum(precond * image), ("gx", "gy"))
    solution_field = alpha * precond
    residual = residual - alpha * image
    return (solution_field, residual)


def cas_table(rows, columns, length):
    angle = (np.outer(rows, columns) % length).astype(np.float64) * (2.0 * np.pi / length)
    return np.cos(angle) + np.sin(angle)


def symbol_table(length):
    halfang = np.arange(length, dtype=np.float64) * (np.pi / length)
    return ((27.0 * np.sin(halfang) - np.sin(3.0 * halfang)) / 12.0) ** 2


def halves(table):
    high = table.astype(ml_dtypes.bfloat16)
    low = (table - high.astype(np.float64)).astype(ml_dtypes.bfloat16)
    return high, low


def thirds(table):
    high, low = halves(table)
    return np.concatenate([high, low, high], axis=1)


def split(values):
    high = values.astype(jnp.bfloat16)
    low = (values - high.astype(jnp.float32)).astype(jnp.bfloat16)
    return high, low


def stacked(values, axis):
    high, low = split(values)
    return jnp.concatenate([high, high, low], axis=axis)


def mul(left, right):
    return jnp.dot(left, right, preferred_element_type=jnp.float32)


def mul_t(left, right):
    return lax.dot_general(
        left, right, (((1,), (1,)), ((), ())), preferred_element_type=jnp.float32
    )


def padded_rows(values, rows):
    if values.shape[0] == rows:
        return values
    gap = jnp.zeros((rows - values.shape[0],) + values.shape[1:], values.dtype)
    return jnp.concatenate([values, gap], axis=0)


def up(size, step):
    return -(-size // step) * step


STENCIL = tuple(EPS_PRECOND * c / 576.0 for c in (-783.0, 54.0, -1.0))


class Plan:
    def __init__(self, shape, count_x, count_y):
        size_x, size_y, self.nz = shape
        self.gx, self.gl = count_x, count_y // 2
        self.nx, self.ny = size_x, size_y // 2
        self.cx, self.cy = size_x // count_x, size_y // count_y
        self.ng = self.gx * self.gl
        self.even = count_y % 2 == 0 and self.cy % 2 == 0 and self.ng > 0
        self.kz = self.nz // max(self.ng, 1)
        self.yq = self.cy // 2
        self.xp = up(self.cx, 8)
        self.xe = self.cx + 2 * HALO
        self.xw = up(self.xe, 8)
        self.yp = up(self.ny, 16)
        self.step = self.yq * self.kz
        self.edge = HALO * self.kz
        self.group = LANES // max(self.kz, 1)
        self.chunks = -(-self.ng // self.group)
        self.deep = self.chunks * LANES
        self.extra = self.cx // self.yq if self.yq else 0
        self.rows = up(2 * self.xe + self.cx + self.extra, 8)
        self.mirror = self.nx // 2 + 1
        self.lines = self.cy * self.xw + (2 * HALO - 1) * self.xp + self.yq * 8

    def fits(self):
        return (
            self.even
            and self.nz % (self.ng * 8) == 0
            and self.nz % LANES == 0
            and self.yq == 2 * HALO - 1
            and self.cx == 4 * self.yq
            and self.step <= LANES
            and self.step % 8 == 0
            and self.nx <= LANES
            and 2 * (LANES - self.nx) >= self.nx
            and 3 * self.mirror <= LANES
            and self.ny % 8 == 0
            and self.nx % 16 == 0
            and self.ny >= 2 * HALO
            and self.gx * self.xw <= LANES
        )

    def z_forward(self):
        wave = np.arange(self.nz)
        owner = wave // self.kz
        place = owner // self.group * LANES + owner % self.group * self.kz + wave % self.kz
        table = np.zeros((self.nz, self.deep))
        table[:, place] = cas_table(wave, wave, self.nz)
        return halves(table)

    def x_waves(self):
        return np.concatenate([np.arange(self.mirror), np.arange(self.nx - 1, self.mirror - 1, -1)])

    def x_forward(self):
        table = np.zeros((LANES, self.nx))
        table[: self.nx] = cas_table(self.x_waves(), np.arange(self.nx), self.nx)
        return thirds(table)

    def y_both(self):
        table = np.zeros((self.ny, self.yp))
        table[:, : self.ny] = cas_table(np.arange(self.ny), np.arange(self.ny), self.ny)
        return thirds(table)

    def ends(self):
        low = np.arange(HALO)
        return np.concatenate([low, self.ny - 1 - low])

    def y_ends(self):
        table = np.zeros((8, self.yp))
        table[: 2 * HALO, : self.ny] = cas_table(self.ends(), np.arange(self.ny), self.ny)
        return thirds(table)

    def y_sources(self):
        columns = cas_table(np.arange(self.ny), self.ends(), self.ny).T
        wide = np.broadcast_to(columns[:, :, None], (2 * HALO, self.ny, LANES))
        return np.ascontiguousarray(wide).astype(np.float32)

    def x_backward(self):
        wide = np.zeros((self.gx * self.xw, LANES))
        own = np.zeros((self.gx * self.xp, LANES))
        waves = self.x_waves()
        for g in range(self.gx):
            x = (g * self.cx - HALO + np.arange(self.xe)) % self.nx
            wide[g * self.xw : g * self.xw + self.xe, : self.nx] = cas_table(x, waves, self.nx)
            x = g * self.cx + np.arange(self.cx)
            own[g * self.xp : g * self.xp + self.cx, : self.nx] = cas_table(x, waves, self.nx)
        scale = 4.0 * np.pi / (self.nx * self.nz)
        return thirds(np.concatenate([wide, own], axis=0) * scale)

    def plane(self):
        plane = np.full((self.ny, LANES), 1e30)
        lam_x = symbol_table(self.nx)[self.x_waves()]
        plane[:, : self.nx] = lam_x[None, :] + symbol_table(self.ny)[:, None]
        return plane.astype(np.float32)

    def coarse_pack(self):
        parts = [self.x_forward(), self.y_both(), self.y_ends(), self.x_backward()]
        width = max(part.shape[1] for part in parts)
        self.places, rows = [], 0
        for part in parts:
            self.places.append((rows, part.shape))
            rows = up(rows + part.shape[0], 16)
        table = np.zeros((rows, width), ml_dtypes.bfloat16)
        for (row, shape), part in zip(self.places, parts):
            table[row : row + shape[0], : shape[1]] = part
        return table

    def fine_pack(self):
        parts = [self.plane(), self.y_sources(), self.joins()]
        return np.concatenate([part.reshape(-1, LANES) for part in parts], axis=0)

    def coarse(self, ref, which):
        row, shape = self.places[which]
        return ref[row : row + shape[0], : shape[1]]

    def join_rows(self, ref, row):
        me = lax.axis_index("gx") * self.gl + lax.axis_index("gl")
        size = (2 * HALO + 1) * self.kz
        start = (2 * HALO + 1) * self.ny + me * size + row * self.kz
        return ref[pl.ds(pl.multiple_of(start, 8), self.kz), :]

    def joins(self):
        lam_x = symbol_table(self.nx)[: self.mirror]
        lam_y, lam_z = symbol_table(self.ny), symbol_table(self.nz)
        total = EPS_PRECOND * (lam_z[:, None, None] + lam_x[None, :, None] + lam_y) + SHIFT_PRECOND
        green = np.real(np.fft.ifft(1.0 / total, axis=-1))
        i = np.arange(HALO)
        near = green[..., np.abs(i[:, None] - i[None, :])]
        far = green[..., i[:, None] + i[None, :] + 1]
        band = np.zeros((HALO, HALO))
        for row in range(HALO):
            for column in range(HALO - row):
                band[row, column] = STENCIL[row + column]
        eye = np.eye(HALO)
        even = np.linalg.inv(eye - 2.0 * (near + far) @ band)
        odd = np.linalg.inv(eye + 2.0 * (near - far) @ band)
        both = np.stack([even, odd], axis=2).reshape(self.ng, self.kz, self.mirror, 2 * HALO, HALO)
        both = both.transpose(0, 3, 1, 4, 2).reshape(self.ng, 2 * HALO, self.kz, HALO * self.mirror)
        table = np.zeros((self.ng, 2 * HALO + 1, self.kz, LANES), np.float32)
        table[:, : 2 * HALO, :, : HALO * self.mirror] = both
        table[:, 2 * HALO] = lam_z.reshape(self.ng, self.kz, 1)
        return table


VMEM_SPEC = pl.BlockSpec(memory_space=pltpu.VMEM)
ANY_SPEC = pl.BlockSpec(memory_space=pl.ANY)


def call(kernel, outs, args, scratch=(), specs=None, limit=VMEM_LIMIT, flops=0):
    nbytes = sum(int(np.prod(a.shape)) * a.dtype.itemsize for a in (*args, *outs))
    return pl.pallas_call(
        kernel,
        out_shape=tuple(outs),
        in_specs=specs or [VMEM_SPEC] * len(args),
        out_specs=tuple([VMEM_SPEC] * len(outs)),
        scratch_shapes=list(scratch),
        compiler_params=pltpu.CompilerParams(vmem_limit_bytes=limit),
        cost_estimate=pl.CostEstimate(flops=flops, bytes_accessed=nbytes, transcendentals=0),
    )(*args)


def lane_index(rows):
    return lax.broadcasted_iota(jnp.int32, (rows, LANES), 1)


def moved(values, shift):
    shift = shift % LANES
    return values if shift == 0 else pltpu.roll(values, shift, 1)


def between(lane, slot, width):
    return (lane >= slot * width) & (lane < (slot + 1) * width)


def fetched(pairs, sems):
    copies = [
        pltpu.make_async_copy(source, target, sems.at[i])
        for i, (source, target) in enumerate(pairs)
    ]
    for copy in copies:
        copy.start()
    return copies


def forward_kernel(p, charge_in, high_in, low_in, out, charge, high_z, low_z, sems):
    copies = fetched(((charge_in, charge), (high_in, high_z), (low_in, low_z)), sems)
    copies[0].wait()
    rows = [padded_rows(charge[y], p.xp) for y in range(p.cy)]
    high, low = split(jnp.concatenate(rows, axis=0))
    copies[1].wait()
    spec = mul(high, high_z[...]) + mul(low, high_z[...])
    copies[2].wait()
    spec = spec + mul(high, low_z[...])
    lane = lane_index(p.xp)
    for target in range(p.ng):
        chunk, slot = divmod(target, p.group)
        for part in range(2):
            block = jnp.zeros((p.xp, LANES), jnp.float32)
            for i in range(p.yq):
                y = part * p.yq + i
                piece = spec[y * p.xp : (y + 1) * p.xp, chunk * LANES : (chunk + 1) * LANES]
                block = jnp.where(between(lane, i, p.kz), moved(piece, (i - slot) * p.kz), block)
            out[target, part * p.cx : (part + 1) * p.cx] = block[: p.cx]


def table_kernel(p, fine, out):
    plane = fine[: p.ny, :]
    waves = p.join_rows(fine, 2 * HALO)
    for k in range(p.kz):
        symbol = EPS_PRECOND * (plane + waves[k : k + 1]) + SHIFT_PRECOND
        out[:, k * LANES : (k + 1) * LANES] = 1.0 / (float(p.ny) * symbol)


def lanes_of(values, k):
    return values[:, k * LANES : (k + 1) * LANES]


def solve_kernel(p, blocks, coarse, table, spectrum_out, own, sent, turned, ends):
    x_fwd, y_both, y_ends = (p.coarse(coarse, i) for i in range(3))
    columns = []
    for gl in range(p.gl):
        for part in range(2):
            pieces = [
                blocks[gx * p.gl + gl, part * p.cx : (part + 1) * p.cx] for gx in range(p.gx)
            ]
            columns.append(jnp.concatenate(pieces, axis=0))
    along_x = mul(x_fwd, stacked(jnp.concatenate(columns, axis=1), 0))
    for b in range(2 * p.gl):
        turned[pl.ds(b * p.step, LANES), :] = lanes_of(along_x, b).T
    field = jnp.concatenate(
        [turned[pl.ds(k, p.ny, stride=p.kz), :] for k in range(p.kz)], axis=1
    )
    along_y = mul(y_both, stacked(padded_rows(field, p.yp), 0))
    solved = along_y * table[...]
    spectrum_out[...] = solved
    at_ends = mul(y_ends, stacked(padded_rows(solved, p.yp), 0))
    for k in range(p.kz):
        ends[pl.ds(k, 8, stride=p.kz), :] = lanes_of(at_ends, k)
    own[...] = ends[pl.ds(0, 2 * HALO * p.kz), :]
    piece = [ends[pl.ds(j * p.kz, p.kz), :] for j in range(2 * HALO)]
    lane = lane_index(p.kz)
    free = LANES - p.nx
    for i in range(4):
        spare = moved(piece[4 + i // 2], p.nx if i % 2 == 0 else p.nx - free)
        sent[pl.ds(i * p.kz, p.kz), :] = jnp.where(lane < p.nx, piece[i], spare)


def return_kernel(
    p, spectrum_in, own, received, table, fine, coarse,
    out, sources, planes,
):
    y_both, x_bwd = p.coarse(coarse, 1), p.coarse(coarse, 3)
    y_sources = [fine[(j + 1) * p.ny : (j + 2) * p.ny, :] for j in range(2 * HALO)]
    lane = lane_index(p.kz)
    free = LANES - p.nx
    part = [received[pl.ds(i * p.kz, p.kz), :] for i in range(4)]
    other = [jnp.where(lane < p.nx, value, 0.0) for value in part]
    for i in range(2):
        first = moved(part[2 * i], -p.nx)
        second = moved(part[2 * i + 1], free - p.nx)
        other.append(jnp.where(lane < free, first, jnp.where(lane < p.nx, second, 0.0)))
    mine = [own[pl.ds(j * p.kz, p.kz), :] for j in range(2 * HALO)]
    jump = [mine[j] - other[j] for j in range(2 * HALO)]
    even = [jump[j] + jump[HALO + j] for j in range(HALO)]
    odd = [jump[j] - jump[HALO + j] for j in range(HALO)]

    def mixed(base, vector):
        results = []
        for i in range(HALO):
            packed = p.join_rows(fine, base + i)
            total = 0.0
            for j in range(HALO):
                first = moved(packed, -j * p.mirror)
                second = moved(packed, p.mirror - 1 - j * p.mirror)
                total = total + jnp.where(lane < p.mirror, first, second) * vector[j]
            results.append(total)
        return results

    even_full, odd_full = mixed(0, even), mixed(HALO, odd)
    low_full = [0.5 * (e + o) for e, o in zip(even_full, odd_full)]
    high_full = [0.5 * (e - o) for e, o in zip(even_full, odd_full)]
    far_low = [other[j] - 0.5 * (low_full[j] - jump[j]) for j in range(HALO)]
    far_high = [other[HALO + j] - 0.5 * (high_full[j] - jump[HALO + j]) for j in range(HALO)]
    for i in range(HALO):
        sources[pl.ds(i * p.kz, p.kz), :] = sum(
            STENCIL[i + j] * high_full[j] for j in range(HALO - i)
        )
        sources[pl.ds((HALO + i) * p.kz, p.kz), :] = sum(
            STENCIL[i + j] * low_full[j] for j in range(HALO - i)
        )
    whole = []
    for k in range(p.kz):
        added = sum(y_sources[j] * sources[pl.ds(j * p.kz + k, 1), :] for j in range(2 * HALO))
        whole.append(
            spectrum_in[:, k * LANES : (k + 1) * LANES]
            + added * table[:, k * LANES : (k + 1) * LANES]
        )
    back_y = mul(y_both, stacked(padded_rows(jnp.concatenate(whole, axis=1), p.yp), 0))
    base = p.edge
    for k in range(p.kz):
        planes[pl.ds(base + k, p.ny, stride=p.kz), :] = lanes_of(back_y, k)
    after = base + p.ny * p.kz
    for i in range(HALO):
        planes[pl.ds(base - (i + 1) * p.kz, p.kz), :] = far_high[i]
        planes[pl.ds(after + i * p.kz, p.kz), :] = far_low[i]
    cut = p.gx * p.xw
    wide_rows = x_bwd[:cut, :]
    own_rows = x_bwd[cut:, :]
    gap = jnp.zeros((LANES - p.step, LANES), jnp.float32)
    slots = lane_index(p.extra)
    rest = p.rows - 2 * p.xe - p.cx - p.extra
    for gl in range(p.gl):
        start = base + gl * 2 * p.step
        end = start + 2 * p.step
        last = planes[pl.ds(end + p.edge - p.kz, p.kz), :]
        both = jnp.concatenate(
            [planes[pl.ds(start, LANES), :], planes[pl.ds(start + p.step, LANES), :]], axis=0
        )
        wide = mul_t(wide_rows, stacked(both, 1))
        sides = jnp.concatenate(
            [
                planes[pl.ds(start - p.edge, p.edge), :],
                planes[pl.ds(end, p.edge - p.kz), :],
                gap,
                *[last] * p.yq,
                gap,
            ],
            axis=0,
        )
        side = mul_t(own_rows, stacked(sides, 1))
        for gx in range(p.gx):
            target = gx * p.gl + gl
            for half in range(2):
                out[target, half * p.xe : (half + 1) * p.xe] = wide[
                    gx * p.xw : gx * p.xw + p.xe, half * LANES : (half + 1) * LANES
                ]
            at, line = 2 * p.xe, gx * p.xp
            out[target, at : at + p.cx] = side[line : line + p.cx, :LANES]
            at += p.cx
            extra = jnp.zeros((p.extra, LANES), jnp.float32)
            for q in range(p.yq):
                value = side[line + q * p.extra : line + (q + 1) * p.extra, LANES:]
                extra = jnp.where(between(slots, q, p.kz), value, extra)
            out[target, at : at + p.extra] = extra
            if rest:
                out[target, at + p.extra :] = jnp.zeros((rest, LANES), jnp.float32)


def stencil_kernel(
    p, blocks, high_z, low_z, charge, eps, ex_low, ex_high, ey_low, ey_high,
    pre, image, sums, lines, field, eps_x, eps_y,
):
    lane = lane_index(p.xw)
    windows, at = [], 0
    for y in range(p.cy):
        half = y // p.yq
        windows.append((half * p.xe // 8 * 8, p.xw, y % p.yq, at))
        at += p.xw
    side = 2 * p.xe
    for h in range(2 * HALO - 1):
        windows.append((side // 8 * 8, p.xp, h, at))
        at += p.xp
    tail = side + p.cx
    for q in range(p.yq):
        windows.append((tail // 8 * 8, 8, q, at))
        at += 8
    for chunk in range(p.chunks):
        count = min(p.group, p.ng - chunk * p.group)
        for first, rows, piece, at in windows:
            here = lane[:rows]
            line = jnp.zeros((rows, LANES), jnp.float32)
            for slot in range(count):
                part = blocks[chunk * p.group + slot, first : first + rows, :]
                part = moved(part, (slot - piece) * p.kz)
                line = jnp.where(between(here, slot, p.kz), part, line)
            lines[at : at + rows, chunk * LANES : (chunk + 1) * LANES] = line
    high, low = split(lines[...])
    whole = mul_t(high, high_z[...]) + mul_t(low, high_z[...]) + mul_t(high, low_z[...])
    for y in range(p.cy):
        first, rows, piece, at = windows[y]
        off = (y // p.yq) * p.xe - first
        field[HALO + y, : p.xe] = whole[at + off : at + off + p.xe]
    for h in range(2 * HALO - 1):
        first, rows, piece, at = windows[p.cy + h]
        off = side - first
        y = h if h < HALO else h + p.cy
        field[y, HALO : HALO + p.cx] = whole[at + off : at + off + p.cx]
    for q in range(p.yq):
        first, rows, piece, at = windows[p.cy + 2 * HALO - 1 + q]
        off = tail - first
        field[p.cy + 2 * HALO - 1, HALO + q * p.extra : HALO + (q + 1) * p.extra] = whole[
            at + off : at + off + p.extra
        ]
    eps_x[:, 0:2, :] = ex_low[...]
    eps_x[:, 2 : 2 + p.cx, :] = eps[...]
    eps_x[:, 2 + p.cx : 4 + p.cx, :] = ex_high[...]
    eps_y[0:2] = ey_low[...]
    eps_y[2 : 2 + p.cy] = eps[...]
    eps_y[2 + p.cy : 4 + p.cy] = ey_high[...]

    def stretch(flux_at):
        return 27.0 * (flux_at(2) - flux_at(1)) - (flux_at(3) - flux_at(0))

    rz = jnp.zeros((p.cx, LANES), jnp.float32)
    dot = jnp.zeros((p.cx, LANES), jnp.float32)
    faces_y = {}

    def face_y(y):
        if y not in faces_y:
            val = [field[y + i, HALO : HALO + p.cx, :] for i in range(4)]
            grad = 27.0 * (val[2] - val[1]) - (val[3] - val[0])
            faces_y[y] = (eps_y[y] + eps_y[y + 1]) * grad
        return faces_y[y]

    for y in range(p.cy):
        line = field[HALO + y]
        val = [line[i : i + p.cx + 3] for i in range(4)]
        grad = 27.0 * (val[2] - val[1]) - (val[3] - val[0])
        eps_line = eps_x[y]
        flux = (eps_line[0 : p.cx + 3] + eps_line[1 : p.cx + 4]) * grad
        term = stretch(lambda i: flux[i : i + p.cx])
        term = term + stretch(lambda i: face_y(y + i))
        here = line[HALO : HALO + p.cx]
        eps_here = eps[y]
        n = p.nz
        grad = 27.0 * (pltpu.roll(here, n - 1, 1) - here) - (
            pltpu.roll(here, n - 2, 1) - pltpu.roll(here, 1, 1)
        )
        flux = (eps_here + pltpu.roll(eps_here, n - 1, 1)) * grad
        term = term + (
            27.0 * (flux - pltpu.roll(flux, 1, 1))
            - (pltpu.roll(flux, n - 1, 1) - pltpu.roll(flux, 2, 1))
        )
        result = (KAPPA_SCALE / (EPS_SOLVENT - 1.0)) * (eps_here - 1.0) * here - term * (0.5 / 576.0)
        pre[y] = here
        image[y] = result
        one = charge[y] * here
        two = result * here
        for c in range(n // LANES):
            rz = rz + one[:, c * LANES : (c + 1) * LANES]
            dot = dot + two[:, c * LANES : (c + 1) * LANES]
    rz = jnp.sum(rz, axis=0, keepdims=True)
    dot = jnp.sum(dot, axis=0, keepdims=True)
    half = LANES // 2
    rz = rz + pltpu.roll(rz, half, 1)
    dot = dot + pltpu.roll(dot, half, 1)
    both = jnp.where(lane_index(1) < half, rz, dot)
    sums[...] = jnp.broadcast_to(both[None], sums.shape)


def update_kernel(p, sums, charge, pre, image, solution_field, residual):
    half = LANES // 2
    total = jnp.sum(sums[...], axis=0)
    lane = lane_index(1)
    rz = jnp.sum(jnp.where(lane < half, total, 0.0), axis=1, keepdims=True)
    dot = jnp.sum(jnp.where(lane < half, 0.0, total), axis=1, keepdims=True)
    alpha = jnp.broadcast_to((4.0 * math.pi) * rz / dot, (p.cx, p.nz))
    for y in range(p.cy):
        solution_field[y] = alpha * pre[y]
        residual[y] = (4.0 * math.pi) * charge[y] - alpha * image[y]


def local_planes(p, density, charge):
    group = ("gx", "gl")
    along_y = ("gh", "gl")
    f32 = jnp.float32

    def shape(*dims):
        return jax.ShapeDtypeStruct(dims, f32)

    def ring(count):
        return [(i, (i + 1) % count) for i in range(count)]

    def back(pairs):
        return [(target, source) for source, target in pairs]

    density = density.transpose(1, 0, 2)
    charge = charge.transpose(1, 0, 2)
    high_z, low_z = (jnp.asarray(part) for part in p.z_forward())
    coarse, fine = jnp.asarray(p.coarse_pack()), jnp.asarray(p.fine_pack())
    (blocks,) = call(
        lambda *refs: forward_kernel(p, *refs),
        [shape(p.ng, 2 * p.cx, LANES)],
        [charge, high_z, low_z],
        [
            pltpu.VMEM((p.cy, p.cx, p.nz), f32),
            pltpu.VMEM((p.nz, p.deep), jnp.bfloat16),
            pltpu.VMEM((p.nz, p.deep), jnp.bfloat16),
            pltpu.SemaphoreType.DMA((3,)),
        ],
        specs=[ANY_SPEC] * 3,
        limit=None,
    )
    blocks = lax.all_to_all(blocks, group, 0, 0)
    (table,) = call(
        lambda *refs: table_kernel(p, *refs), [shape(p.ny, p.kz * LANES)], [fine]
    )
    eps = permittivity(density)
    blocks, eps, table = lax.optimization_barrier(
        (blocks, eps, table)
    )
    spectrum_half, own, sent = call(
        lambda *refs: solve_kernel(p, *refs),
        [shape(p.ny, p.kz * LANES), shape(2 * HALO * p.kz, LANES), shape(4 * p.kz, LANES)],
        [blocks, coarse, table],
        [pltpu.VMEM((p.ny * p.kz + LANES, LANES), f32), pltpu.VMEM((8 * p.kz, LANES), f32)],
    )
    sent, eps = lax.optimization_barrier((sent, eps))
    received = lax.ppermute(sent, "gh", [(0, 1), (1, 0)])
    ex_low = lax.ppermute(eps[:, p.cx - 2 :], "gx", ring(p.gx))
    ex_high = lax.ppermute(eps[:, :2], "gx", back(ring(p.gx)))
    ey_low = lax.ppermute(eps[p.cy - 2 :], along_y, ring(2 * p.gl))
    ey_high = lax.ppermute(eps[:2], along_y, back(ring(2 * p.gl)))
    received, ex_low, ex_high, ey_low, ey_high = lax.optimization_barrier(
        (received, ex_low, ex_high, ey_low, ey_high)
    )
    (blocks,) = call(
        lambda *refs: return_kernel(p, *refs),
        [shape(p.ng, p.rows, LANES)],
        [
            spectrum_half, own, received, table, fine, coarse,
        ],
        [
            pltpu.VMEM((2 * HALO * p.kz, LANES), f32),
            pltpu.VMEM((p.ny * p.kz + 2 * p.edge, LANES), f32),
        ],
    )
    blocks = lax.all_to_all(blocks, group, 0, 0)
    pre, image, sums = call(
        lambda *refs: stencil_kernel(p, *refs),
        [shape(p.cy, p.cx, p.nz), shape(p.cy, p.cx, p.nz), shape(2 * p.ng, 1, LANES)],
        [
            blocks, high_z, low_z, charge, eps, ex_low, ex_high, ey_low, ey_high,
        ],
        [
            pltpu.VMEM((p.lines, p.deep), f32),
            pltpu.VMEM((p.cy + 2 * HALO, p.xw, p.nz), f32),
            pltpu.VMEM((p.cy, p.cx + 4, p.nz), f32),
            pltpu.VMEM((p.cy + 4, p.cx, p.nz), f32),
        ],
    )
    sums = lax.all_to_all(sums, ("gx", "gh", "gl"), 0, 0)
    solution_field, residual = call(
        lambda *refs: update_kernel(p, *refs),
        [shape(p.cy, p.cx, p.nz), shape(p.cy, p.cx, p.nz)],
        [sums, charge, pre, image],
    )
    return solution_field.transpose(1, 0, 2), residual.transpose(1, 0, 2)


def solution(mesh):
    count_x, count_y = mesh.shape["gx"], mesh.shape["gy"]

    def run(density, charge):
        plan = Plan(charge.shape, count_x, count_y)
        if plan.fits():
            split_mesh = jax.sharding.Mesh(
                mesh.devices.reshape(count_x, 2, count_y // 2), ("gx", "gh", "gl")
            )
            spec = P("gx", ("gh", "gl"), None)
            body, over = (lambda *args: local_planes(plan, *args)), split_mesh
        else:
            spec = P("gx", "gy", None)
            body, over = local_lines, mesh
        return jax.shard_map(
            body, mesh=over, in_specs=(spec, spec), out_specs=(spec, spec), check_vma=False
        )(density, charge)

    return run
```

```python
import math

import jax
import jax.numpy as jnp
import ml_dtypes
import numpy as np
from jax import lax
from jax.experimental import pallas as pl
from jax.experimental.pallas import tpu as pltpu
from jax.sharding import PartitionSpec as P

EPS_SOLVENT = 78.3
RHO_UPPER = 0.005
RHO_LOWER = 0.0001
KAPPA_SCALE = 0.1
EPS_PRECOND = 20.0
SHIFT_PRECOND = 0.05
HIGHEST = lax.Precision.HIGHEST
LANES = 128
HALO = 3
VMEM_LIMIT = 48 << 20


def extended(block, sides, width):
    for axis, dim in sides:
        count = lax.axis_size(axis)
        forward = [(i, i + 1) for i in range(count - 1)]
        forward.append((count - 1, 0))
        backward = [(target, source) for source, target in forward]
        low = lax.ppermute(
            lax.slice_in_dim(block, block.shape[dim] - width, None, axis=dim), axis, forward
        )
        high = lax.ppermute(lax.slice_in_dim(block, 0, width, axis=dim), axis, backward)
        block = jnp.concatenate([low, block, high], axis=dim)
    return block


def permittivity(density):
    upper = math.log(RHO_UPPER)
    lower = math.log(RHO_LOWER)
    fraction = jnp.clip((upper - jnp.log(density)) / (upper - lower), 0.0, 1.0)
    exponent = fraction - jnp.sin(2.0 * math.pi * fraction) / (2.0 * math.pi)
    return jnp.exp(exponent * math.log(EPS_SOLVENT))


def hartley(length):
    indices = jnp.arange(length, dtype=jnp.int32)
    product = indices[:, None] * indices[None, :] % length
    angles = product.astype(jnp.float32) * (2.0 * math.pi / length)
    return jnp.cos(angles) + jnp.sin(angles)


def spectrum(wavenum, length):
    halfang = wavenum.astype(jnp.float32) * (math.pi / length)
    return ((27.0 * jnp.sin(halfang) - jnp.sin(3.0 * halfang)) / 12.0) ** 2


def cutout(values, offset, length, dimen):
    return lax.slice_in_dim(values, offset, offset + length, axis=dimen)


def padded_term(padded, faces, count, dimen):
    nfaces = count + 3
    grad = (
        27.0 * (cutout(padded, 2, nfaces, dimen) - cutout(padded, 1, nfaces, dimen))
        - (cutout(padded, 3, nfaces, dimen) - cutout(padded, 0, nfaces, dimen))
    ) / 24.0
    flux = faces * grad
    return (
        27.0 * (cutout(flux, 2, count, dimen) - cutout(flux, 1, count, dimen))
        - (cutout(flux, 3, count, dimen) - cutout(flux, 0, count, dimen))
    ) / 24.0


def rolled_term(field, faces):
    grad = (
        27.0 * (jnp.roll(field, -1, 2) - field) - (jnp.roll(field, -2, 2) - jnp.roll(field, 1, 2))
    ) / 24.0
    flux = faces * grad
    return (
        27.0 * (flux - jnp.roll(flux, 1, 2)) - (jnp.roll(flux, -1, 2) - jnp.roll(flux, 2, 2))
    ) / 24.0


def operate(field, faces_x, faces_y, faces_z, kappa):
    cellsx = field.shape[0]
    cellsy = field.shape[1]
    padded = extended(field, (("gx", 0), ("gy", 1)), 3)
    term_x = padded_term(padded[:, 3 : 3 + cellsy], faces_x, cellsx, 0)
    term_y = padded_term(padded[3 : 3 + cellsx], faces_y, cellsy, 1)
    term_z = rolled_term(field, faces_z)
    return kappa * field - (term_x + term_y + term_z)


def precondition(field):
    cellsx, cellsy, length_z = field.shape
    size_x = cellsx * lax.axis_size("gx")
    size_y = cellsy * lax.axis_size("gy")
    hart_x = hartley(size_x)
    hart_y = hartley(size_y)
    hart_z = hartley(length_z)
    scaling = float(size_x * size_y * length_z)
    forward = jnp.dot(field, hart_z, precision=HIGHEST)
    zpiece = length_z // lax.axis_size("gx")
    xpiece = size_x // lax.axis_size("gy")
    lines_x = lax.all_to_all(forward, "gx", split_axis=2, concat_axis=0, tiled=True)
    along_x = jnp.einsum("xyk,xa->yka", lines_x, hart_x, precision=HIGHEST)
    lines_y = lax.all_to_all(along_x, "gy", split_axis=2, concat_axis=0, tiled=True)
    along_y = jnp.einsum("ykb,yc->kbc", lines_y, hart_y, precision=HIGHEST)
    wave_z = lax.axis_index("gx") * zpiece + jnp.arange(zpiece, dtype=jnp.int32)
    wave_x = lax.axis_index("gy") * xpiece + jnp.arange(xpiece, dtype=jnp.int32)
    wave_y = jnp.arange(size_y, dtype=jnp.int32)
    symbol = (
        EPS_PRECOND
        * (
            spectrum(wave_z, length_z)[:, None, None]
            + spectrum(wave_x, size_x)[None, :, None]
            + spectrum(wave_y, size_y)[None, None, :]
        )
        + SHIFT_PRECOND
    )
    scaled = along_y / (symbol * scaling)
    back_y = jnp.einsum("kbc,cy->ykb", scaled, hart_y, precision=HIGHEST)
    lines_back = lax.all_to_all(back_y, "gy", split_axis=0, concat_axis=2, tiled=True)
    back_x = jnp.einsum("yka,ax->xyk", lines_back, hart_x, precision=HIGHEST)
    bricks = lax.all_to_all(back_x, "gx", split_axis=0, concat_axis=2, tiled=True)
    return jnp.dot(bricks, hart_z, precision=HIGHEST)


def residual_inner(residual, precond):
    return lax.psum(jnp.sum(residual * precond), ("gx", "gy"))


def local_lines(density, charge):
    eps = permittivity(density)
    kappa = KAPPA_SCALE * (eps - 1.0) / (EPS_SOLVENT - 1.0)
    cellsx = eps.shape[0]
    cellsy = eps.shape[1]
    eps_padded = extended(eps, (("gx", 0), ("gy", 1)), 2)
    strip_x = eps_padded[:, 2 : 2 + cellsy]
    faces_x = 0.5 * (strip_x[:-1] + strip_x[1:])
    strip_y = eps_padded[2 : 2 + cellsx]
    faces_y = 0.5 * (strip_y[:, :-1] + strip_y[:, 1:])
    faces_z = 0.5 * (eps + jnp.roll(eps, -1, 2))
    rhs = 4.0 * math.pi * charge
    residual = rhs
    precond = precondition(residual)
    inner_now = residual_inner(residual, precond)
    image = operate(precond, faces_x, faces_y, faces_z, kappa)
    alpha = inner_now / lax.psum(jnp.sum(precond * image), ("gx", "gy"))
    solution_field = alpha * precond
    residual = residual - alpha * image
    return (solution_field, residual)


def cas_table(rows, columns, length):
    angle = (np.outer(rows, columns) % length).astype(np.float64) * (2.0 * np.pi / length)
    return np.cos(angle) + np.sin(angle)


def symbol_table(length):
    halfang = np.arange(length, dtype=np.float64) * (np.pi / length)
    return ((27.0 * np.sin(halfang) - np.sin(3.0 * halfang)) / 12.0) ** 2


def halves(table):
    high = table.astype(ml_dtypes.bfloat16)
    low = (table - high.astype(np.float64)).astype(ml_dtypes.bfloat16)
    return high, low


def thirds(table):
    high, low = halves(table)
    return np.concatenate([high, low, high], axis=1)


def split(values):
    high = values.astype(jnp.bfloat16)
    low = (values - high.astype(jnp.float32)).astype(jnp.bfloat16)
    return high, low


def stacked(values, axis):
    high, low = split(values)
    return jnp.concatenate([high, high, low], axis=axis)


def mul(left, right):
    return jnp.dot(left, right, preferred_element_type=jnp.float32)


def mul_t(left, right):
    return lax.dot_general(
        left, right, (((1,), (1,)), ((), ())), preferred_element_type=jnp.float32
    )


def padded_rows(values, rows):
    if values.shape[0] == rows:
        return values
    gap = jnp.zeros((rows - values.shape[0],) + values.shape[1:], values.dtype)
    return jnp.concatenate([values, gap], axis=0)


def up(size, step):
    return -(-size // step) * step


STENCIL = tuple(EPS_PRECOND * c / 576.0 for c in (-783.0, 54.0, -1.0))


class Plan:
    def __init__(self, shape, count_x, count_y):
        size_x, size_y, self.nz = shape
        self.gx, self.gl = count_x, count_y // 2
        self.nx, self.ny = size_x, size_y // 2
        self.cx, self.cy = size_x // count_x, size_y // count_y
        self.ng = self.gx * self.gl
        self.even = count_y % 2 == 0 and self.cy % 2 == 0 and self.ng > 0
        self.kz = self.nz // max(self.ng, 1)
        self.yq = self.cy // 2
        self.xp = up(self.cx, 8)
        self.xe = self.cx + 2 * HALO
        self.xw = up(self.xe, 8)
        self.yp = up(self.ny, 16)
        self.step = self.yq * self.kz
        self.edge = HALO * self.kz
        self.group = LANES // max(self.kz, 1)
        self.chunks = -(-self.ng // self.group)
        self.deep = self.chunks * LANES
        self.extra = self.cx // self.yq if self.yq else 0
        self.rows = up(2 * self.xe + self.cx + self.extra, 8)
        self.mirror = self.nx // 2 + 1
        self.lines = self.cy * self.xw + (2 * HALO - 1) * self.xp + self.yq * 8

    def fits(self):
        return (
            self.even
            and self.gx % 2 == 0
            and self.gl % 2 == 0
            and self.nz % (self.ng * 8) == 0
            and self.nz % LANES == 0
            and self.yq == 2 * HALO - 1
            and self.cx == 4 * self.yq
            and self.step <= LANES
            and self.step % 8 == 0
            and self.nx <= LANES
            and 2 * (LANES - self.nx) >= self.nx
            and 3 * self.mirror <= LANES
            and self.ny % 8 == 0
            and self.nx % 16 == 0
            and self.ny >= 2 * HALO
            and self.gx * self.xw <= LANES
        )

    def z_forward(self):
        wave = np.arange(self.nz)
        owner = wave // self.kz
        place = owner // self.group * LANES + owner % self.group * self.kz + wave % self.kz
        table = np.zeros((self.nz, self.deep))
        table[:, place] = cas_table(wave, wave, self.nz)
        return halves(table)

    def x_waves(self):
        return np.concatenate([np.arange(self.mirror), np.arange(self.nx - 1, self.mirror - 1, -1)])

    def x_forward(self):
        table = np.zeros((LANES, self.nx))
        table[: self.nx] = cas_table(self.x_waves(), np.arange(self.nx), self.nx)
        return thirds(table)

    def y_both(self):
        table = np.zeros((self.ny, self.yp))
        table[:, : self.ny] = cas_table(np.arange(self.ny), np.arange(self.ny), self.ny)
        return thirds(table)

    def ends(self):
        low = np.arange(HALO)
        return np.concatenate([low, self.ny - 1 - low])

    def y_ends(self):
        table = np.zeros((8, self.yp))
        table[: 2 * HALO, : self.ny] = cas_table(self.ends(), np.arange(self.ny), self.ny)
        return thirds(table)

    def y_sources(self):
        columns = cas_table(np.arange(self.ny), self.ends(), self.ny).T
        wide = np.broadcast_to(columns[:, :, None], (2 * HALO, self.ny, LANES))
        return np.ascontiguousarray(wide).astype(np.float32)

    def x_backward(self):
        wide = np.zeros((self.gx * self.xw, LANES))
        own = np.zeros((self.gx * self.xp, LANES))
        waves = self.x_waves()
        for g in range(self.gx):
            x = (g * self.cx - HALO + np.arange(self.xe)) % self.nx
            wide[g * self.xw : g * self.xw + self.xe, : self.nx] = cas_table(x, waves, self.nx)
            x = g * self.cx + np.arange(self.cx)
            own[g * self.xp : g * self.xp + self.cx, : self.nx] = cas_table(x, waves, self.nx)
        scale = 4.0 * np.pi / (self.nx * self.nz)
        return thirds(np.concatenate([wide, own], axis=0) * scale)

    def plane(self):
        plane = np.full((self.ny, LANES), 1e30)
        lam_x = symbol_table(self.nx)[self.x_waves()]
        plane[:, : self.nx] = lam_x[None, :] + symbol_table(self.ny)[:, None]
        return plane.astype(np.float32)

    def coarse_pack(self):
        parts = [self.x_forward(), self.y_both(), self.y_ends(), self.x_backward()]
        width = max(part.shape[1] for part in parts)
        self.places, rows = [], 0
        for part in parts:
            self.places.append((rows, part.shape))
            rows = up(rows + part.shape[0], 16)
        table = np.zeros((rows, width), ml_dtypes.bfloat16)
        for (row, shape), part in zip(self.places, parts):
            table[row : row + shape[0], : shape[1]] = part
        return table

    def fine_pack(self):
        parts = [self.plane(), self.y_sources(), self.joins()]
        return np.concatenate([part.reshape(-1, LANES) for part in parts], axis=0)

    def coarse(self, ref, which):
        row, shape = self.places[which]
        return ref[row : row + shape[0], : shape[1]]

    def join_rows(self, ref, row):
        me = lax.axis_index("gx") * self.gl + lax.axis_index("gl")
        size = (2 * HALO + 1) * self.kz
        start = (2 * HALO + 1) * self.ny + me * size + row * self.kz
        return ref[pl.ds(pl.multiple_of(start, 8), self.kz), :]

    def joins(self):
        lam_x = symbol_table(self.nx)[: self.mirror]
        lam_y, lam_z = symbol_table(self.ny), symbol_table(self.nz)
        total = EPS_PRECOND * (lam_z[:, None, None] + lam_x[None, :, None] + lam_y) + SHIFT_PRECOND
        green = np.real(np.fft.ifft(1.0 / total, axis=-1))
        i = np.arange(HALO)
        near = green[..., np.abs(i[:, None] - i[None, :])]
        far = green[..., i[:, None] + i[None, :] + 1]
        band = np.zeros((HALO, HALO))
        for row in range(HALO):
            for column in range(HALO - row):
                band[row, column] = STENCIL[row + column]
        eye = np.eye(HALO)
        even = np.linalg.inv(eye - 2.0 * (near + far) @ band)
        odd = np.linalg.inv(eye + 2.0 * (near - far) @ band)
        both = np.stack([even, odd], axis=2).reshape(self.ng, self.kz, self.mirror, 2 * HALO, HALO)
        both = both.transpose(0, 3, 1, 4, 2).reshape(self.ng, 2 * HALO, self.kz, HALO * self.mirror)
        table = np.zeros((self.ng, 2 * HALO + 1, self.kz, LANES), np.float32)
        table[:, : 2 * HALO, :, : HALO * self.mirror] = both
        table[:, 2 * HALO] = lam_z.reshape(self.ng, self.kz, 1)
        return table


VMEM_SPEC = pl.BlockSpec(memory_space=pltpu.VMEM)
ANY_SPEC = pl.BlockSpec(memory_space=pl.ANY)


def call(kernel, outs, args, scratch=(), specs=None, limit=VMEM_LIMIT, flops=0):
    nbytes = sum(int(np.prod(a.shape)) * a.dtype.itemsize for a in (*args, *outs))
    return pl.pallas_call(
        kernel,
        out_shape=tuple(outs),
        in_specs=specs or [VMEM_SPEC] * len(args),
        out_specs=tuple([VMEM_SPEC] * len(outs)),
        scratch_shapes=list(scratch),
        compiler_params=pltpu.CompilerParams(vmem_limit_bytes=limit),
        cost_estimate=pl.CostEstimate(flops=flops, bytes_accessed=nbytes, transcendentals=0),
    )(*args)


def lane_index(rows):
    return lax.broadcasted_iota(jnp.int32, (rows, LANES), 1)


def moved(values, shift):
    shift = shift % LANES
    return values if shift == 0 else pltpu.roll(values, shift, 1)


def between(lane, slot, width):
    return (lane >= slot * width) & (lane < (slot + 1) * width)


def fetched(pairs, sems):
    copies = [
        pltpu.make_async_copy(source, target, sems.at[i])
        for i, (source, target) in enumerate(pairs)
    ]
    for copy in copies:
        copy.start()
    return copies


def forward_kernel(p, charge_in, high_in, low_in, out, charge, high_z, low_z, sems):
    copies = fetched(((charge_in, charge), (high_in, high_z), (low_in, low_z)), sems)
    copies[0].wait()
    rows = [padded_rows(charge[y], p.xp) for y in range(p.cy)]
    high, low = split(jnp.concatenate(rows, axis=0))
    copies[1].wait()
    spec = mul(high, high_z[...]) + mul(low, high_z[...])
    copies[2].wait()
    spec = spec + mul(high, low_z[...])
    lane = lane_index(p.xp)
    for target in range(p.ng):
        chunk, slot = divmod(target, p.group)
        for part in range(2):
            block = jnp.zeros((p.xp, LANES), jnp.float32)
            for i in range(p.yq):
                y = part * p.yq + i
                piece = spec[y * p.xp : (y + 1) * p.xp, chunk * LANES : (chunk + 1) * LANES]
                block = jnp.where(between(lane, i, p.kz), moved(piece, (i - slot) * p.kz), block)
            out[target, part * p.cx : (part + 1) * p.cx] = block[: p.cx]


def table_kernel(p, fine, out):
    plane = fine[: p.ny, :]
    waves = p.join_rows(fine, 2 * HALO)
    for k in range(p.kz):
        symbol = EPS_PRECOND * (plane + waves[k : k + 1]) + SHIFT_PRECOND
        out[:, k * LANES : (k + 1) * LANES] = 1.0 / (float(p.ny) * symbol)


def lanes_of(values, k):
    return values[:, k * LANES : (k + 1) * LANES]


def solve_kernel(p, blocks, coarse, table, spectrum_out, own, sent, turned, ends):
    x_fwd, y_both, y_ends = (p.coarse(coarse, i) for i in range(3))
    columns = []
    for gl in range(p.gl):
        for part in range(2):
            pieces = [
                blocks[gx * p.gl + gl, part * p.cx : (part + 1) * p.cx] for gx in range(p.gx)
            ]
            columns.append(jnp.concatenate(pieces, axis=0))
    along_x = mul(x_fwd, stacked(jnp.concatenate(columns, axis=1), 0))
    for b in range(2 * p.gl):
        turned[pl.ds(b * p.step, LANES), :] = lanes_of(along_x, b).T
    field = jnp.concatenate(
        [turned[pl.ds(k, p.ny, stride=p.kz), :] for k in range(p.kz)], axis=1
    )
    along_y = mul(y_both, stacked(padded_rows(field, p.yp), 0))
    solved = along_y * table[...]
    spectrum_out[...] = solved
    at_ends = mul(y_ends, stacked(padded_rows(solved, p.yp), 0))
    for k in range(p.kz):
        ends[pl.ds(k, 8, stride=p.kz), :] = lanes_of(at_ends, k)
    own[...] = ends[pl.ds(0, 2 * HALO * p.kz), :]
    piece = [ends[pl.ds(j * p.kz, p.kz), :] for j in range(2 * HALO)]
    lane = lane_index(p.kz)
    free = LANES - p.nx
    for i in range(4):
        spare = moved(piece[4 + i // 2], p.nx if i % 2 == 0 else p.nx - free)
        sent[pl.ds(i * p.kz, p.kz), :] = jnp.where(lane < p.nx, piece[i], spare)


def return_kernel(
    p, spectrum_in, own, received, table, fine, coarse,
    out, sources, planes,
):
    y_both, x_bwd = p.coarse(coarse, 1), p.coarse(coarse, 3)
    y_sources = [fine[(j + 1) * p.ny : (j + 2) * p.ny, :] for j in range(2 * HALO)]
    lane = lane_index(p.kz)
    free = LANES - p.nx
    part = [received[pl.ds(i * p.kz, p.kz), :] for i in range(4)]
    other = [jnp.where(lane < p.nx, value, 0.0) for value in part]
    for i in range(2):
        first = moved(part[2 * i], -p.nx)
        second = moved(part[2 * i + 1], free - p.nx)
        other.append(jnp.where(lane < free, first, jnp.where(lane < p.nx, second, 0.0)))
    mine = [own[pl.ds(j * p.kz, p.kz), :] for j in range(2 * HALO)]
    jump = [mine[j] - other[j] for j in range(2 * HALO)]
    even = [jump[j] + jump[HALO + j] for j in range(HALO)]
    odd = [jump[j] - jump[HALO + j] for j in range(HALO)]

    def mixed(base, vector):
        results = []
        for i in range(HALO):
            packed = p.join_rows(fine, base + i)
            total = 0.0
            for j in range(HALO):
                first = moved(packed, -j * p.mirror)
                second = moved(packed, p.mirror - 1 - j * p.mirror)
                total = total + jnp.where(lane < p.mirror, first, second) * vector[j]
            results.append(total)
        return results

    even_full, odd_full = mixed(0, even), mixed(HALO, odd)
    low_full = [0.5 * (e + o) for e, o in zip(even_full, odd_full)]
    high_full = [0.5 * (e - o) for e, o in zip(even_full, odd_full)]
    far_low = [other[j] - 0.5 * (low_full[j] - jump[j]) for j in range(HALO)]
    far_high = [other[HALO + j] - 0.5 * (high_full[j] - jump[HALO + j]) for j in range(HALO)]
    for i in range(HALO):
        sources[pl.ds(i * p.kz, p.kz), :] = sum(
            STENCIL[i + j] * high_full[j] for j in range(HALO - i)
        )
        sources[pl.ds((HALO + i) * p.kz, p.kz), :] = sum(
            STENCIL[i + j] * low_full[j] for j in range(HALO - i)
        )
    whole = []
    for k in range(p.kz):
        added = sum(y_sources[j] * sources[pl.ds(j * p.kz + k, 1), :] for j in range(2 * HALO))
        whole.append(
            spectrum_in[:, k * LANES : (k + 1) * LANES]
            + added * table[:, k * LANES : (k + 1) * LANES]
        )
    back_y = mul(y_both, stacked(padded_rows(jnp.concatenate(whole, axis=1), p.yp), 0))
    base = p.edge
    for k in range(p.kz):
        planes[pl.ds(base + k, p.ny, stride=p.kz), :] = lanes_of(back_y, k)
    after = base + p.ny * p.kz
    for i in range(HALO):
        planes[pl.ds(base - (i + 1) * p.kz, p.kz), :] = far_high[i]
        planes[pl.ds(after + i * p.kz, p.kz), :] = far_low[i]
    cut = p.gx * p.xw
    wide_rows = x_bwd[:cut, :]
    own_rows = x_bwd[cut:, :]
    gap = jnp.zeros((LANES - p.step, LANES), jnp.float32)
    slots = lane_index(p.extra)
    rest = p.rows - 2 * p.xe - p.cx - p.extra
    for gl in range(p.gl):
        start = base + gl * 2 * p.step
        end = start + 2 * p.step
        last = planes[pl.ds(end + p.edge - p.kz, p.kz), :]
        both = jnp.concatenate(
            [planes[pl.ds(start, LANES), :], planes[pl.ds(start + p.step, LANES), :]], axis=0
        )
        wide = mul_t(wide_rows, stacked(both, 1))
        sides = jnp.concatenate(
            [
                planes[pl.ds(start - p.edge, p.edge), :],
                planes[pl.ds(end, p.edge - p.kz), :],
                gap,
                *[last] * p.yq,
                gap,
            ],
            axis=0,
        )
        side = mul_t(own_rows, stacked(sides, 1))
        for gx in range(p.gx):
            target = gx * p.gl + gl
            for half in range(2):
                out[target, half * p.xe : (half + 1) * p.xe] = wide[
                    gx * p.xw : gx * p.xw + p.xe, half * LANES : (half + 1) * LANES
                ]
            at, line = 2 * p.xe, gx * p.xp
            out[target, at : at + p.cx] = side[line : line + p.cx, :LANES]
            at += p.cx
            extra = jnp.zeros((p.extra, LANES), jnp.float32)
            for q in range(p.yq):
                value = side[line + q * p.extra : line + (q + 1) * p.extra, LANES:]
                extra = jnp.where(between(slots, q, p.kz), value, extra)
            out[target, at : at + p.extra] = extra
            if rest:
                out[target, at + p.extra :] = jnp.zeros((rest, LANES), jnp.float32)


def stencil_kernel(
    p, blocks, high_z, low_z, charge, eps, ex_low, ex_high, ey_low, ey_high,
    pre, image, sums, lines, field, eps_x, eps_y,
):
    lane = lane_index(p.xw)
    windows, at = [], 0
    for y in range(p.cy):
        half = y // p.yq
        windows.append((half * p.xe // 8 * 8, p.xw, y % p.yq, at))
        at += p.xw
    side = 2 * p.xe
    for h in range(2 * HALO - 1):
        windows.append((side // 8 * 8, p.xp, h, at))
        at += p.xp
    tail = side + p.cx
    for q in range(p.yq):
        windows.append((tail // 8 * 8, 8, q, at))
        at += 8
    for chunk in range(p.chunks):
        count = min(p.group, p.ng - chunk * p.group)
        for first, rows, piece, at in windows:
            here = lane[:rows]
            line = jnp.zeros((rows, LANES), jnp.float32)
            for slot in range(count):
                part = blocks[chunk * p.group + slot, first : first + rows, :]
                part = moved(part, (slot - piece) * p.kz)
                line = jnp.where(between(here, slot, p.kz), part, line)
            lines[at : at + rows, chunk * LANES : (chunk + 1) * LANES] = line
    high, low = split(lines[...])
    whole = mul_t(high, high_z[...]) + mul_t(low, high_z[...]) + mul_t(high, low_z[...])
    for y in range(p.cy):
        first, rows, piece, at = windows[y]
        off = (y // p.yq) * p.xe - first
        field[HALO + y, : p.xe] = whole[at + off : at + off + p.xe]
    for h in range(2 * HALO - 1):
        first, rows, piece, at = windows[p.cy + h]
        off = side - first
        y = h if h < HALO else h + p.cy
        field[y, HALO : HALO + p.cx] = whole[at + off : at + off + p.cx]
    for q in range(p.yq):
        first, rows, piece, at = windows[p.cy + 2 * HALO - 1 + q]
        off = tail - first
        field[p.cy + 2 * HALO - 1, HALO + q * p.extra : HALO + (q + 1) * p.extra] = whole[
            at + off : at + off + p.extra
        ]
    eps_x[:, 0:2, :] = ex_low[...]
    eps_x[:, 2 : 2 + p.cx, :] = eps[...]
    eps_x[:, 2 + p.cx : 4 + p.cx, :] = ex_high[...]
    eps_y[0:2] = ey_low[...]
    eps_y[2 : 2 + p.cy] = eps[...]
    eps_y[2 + p.cy : 4 + p.cy] = ey_high[...]

    def stretch(flux_at):
        return 27.0 * (flux_at(2) - flux_at(1)) - (flux_at(3) - flux_at(0))

    rz = jnp.zeros((p.cx, LANES), jnp.float32)
    dot = jnp.zeros((p.cx, LANES), jnp.float32)
    faces_y = {}

    def face_y(y):
        if y not in faces_y:
            val = [field[y + i, HALO : HALO + p.cx, :] for i in range(4)]
            grad = 27.0 * (val[2] - val[1]) - (val[3] - val[0])
            faces_y[y] = (eps_y[y] + eps_y[y + 1]) * grad
        return faces_y[y]

    for y in range(p.cy):
        line = field[HALO + y]
        val = [line[i : i + p.cx + 3] for i in range(4)]
        grad = 27.0 * (val[2] - val[1]) - (val[3] - val[0])
        eps_line = eps_x[y]
        flux = (eps_line[0 : p.cx + 3] + eps_line[1 : p.cx + 4]) * grad
        term = stretch(lambda i: flux[i : i + p.cx])
        term = term + stretch(lambda i: face_y(y + i))
        here = line[HALO : HALO + p.cx]
        eps_here = eps[y]
        n = p.nz
        grad = 27.0 * (pltpu.roll(here, n - 1, 1) - here) - (
            pltpu.roll(here, n - 2, 1) - pltpu.roll(here, 1, 1)
        )
        flux = (eps_here + pltpu.roll(eps_here, n - 1, 1)) * grad
        term = term + (
            27.0 * (flux - pltpu.roll(flux, 1, 1))
            - (pltpu.roll(flux, n - 1, 1) - pltpu.roll(flux, 2, 1))
        )
        result = (KAPPA_SCALE / (EPS_SOLVENT - 1.0)) * (eps_here - 1.0) * here - term * (0.5 / 576.0)
        pre[y] = here
        image[y] = result
        one = charge[y] * here
        two = result * here
        for c in range(n // LANES):
            rz = rz + one[:, c * LANES : (c + 1) * LANES]
            dot = dot + two[:, c * LANES : (c + 1) * LANES]
    rz = jnp.sum(rz, axis=0, keepdims=True)
    dot = jnp.sum(dot, axis=0, keepdims=True)
    half = LANES // 2
    rz = rz + pltpu.roll(rz, half, 1)
    dot = dot + pltpu.roll(dot, half, 1)
    both = jnp.where(lane_index(1) < half, rz, dot)
    sums[...] = jnp.broadcast_to(both[None], sums.shape)


def update_kernel(p, sums, charge, pre, image, solution_field, residual):
    half = LANES // 2
    total = jnp.sum(sums[...], axis=0)
    lane = lane_index(1)
    rz = jnp.sum(jnp.where(lane < half, total, 0.0), axis=1, keepdims=True)
    dot = jnp.sum(jnp.where(lane < half, 0.0, total), axis=1, keepdims=True)
    alpha = jnp.broadcast_to((4.0 * math.pi) * rz / dot, (p.cx, p.nz))
    for y in range(p.cy):
        solution_field[y] = alpha * pre[y]
        residual[y] = (4.0 * math.pi) * charge[y] - alpha * image[y]


def local_planes(p, density, charge):
    group = ("gx", "gl")
    along_y = ("gh", "gl")
    f32 = jnp.float32

    def shape(*dims):
        return jax.ShapeDtypeStruct(dims, f32)

    def pairs(count, first):
        low = range(first, count, 2)
        near = [(i, (i + 1) % count) for i in low]
        return near + [(target, source) for source, target in near]

    even_x = lax.axis_index("gx") % 2 == 0
    even_y = lax.axis_index("gl") % 2 == 0

    density = density.transpose(1, 0, 2)
    charge = charge.transpose(1, 0, 2)
    high_z, low_z = (jnp.asarray(part) for part in p.z_forward())
    coarse, fine = jnp.asarray(p.coarse_pack()), jnp.asarray(p.fine_pack())
    (blocks,) = call(
        lambda *refs: forward_kernel(p, *refs),
        [shape(p.ng, 2 * p.cx, LANES)],
        [charge, high_z, low_z],
        [
            pltpu.VMEM((p.cy, p.cx, p.nz), f32),
            pltpu.VMEM((p.nz, p.deep), jnp.bfloat16),
            pltpu.VMEM((p.nz, p.deep), jnp.bfloat16),
            pltpu.SemaphoreType.DMA((3,)),
        ],
        specs=[ANY_SPEC] * 3,
        limit=None,
    )
    blocks = lax.all_to_all(blocks, group, 0, 0)
    (table,) = call(
        lambda *refs: table_kernel(p, *refs), [shape(p.ny, p.kz * LANES)], [fine]
    )
    eps = permittivity(density)
    swap_by = lax.ppermute(
        jnp.where(even_y, eps[:2], eps[p.cy - 2 :]), along_y, pairs(2 * p.gl, 1)
    )
    swap_bx = lax.ppermute(
        jnp.where(even_x, eps[:, :2], eps[:, p.cx - 2 :]), "gx", pairs(p.gx, 1)
    )
    swap_ay = lax.ppermute(
        jnp.where(even_y, eps[p.cy - 2 :], eps[:2]), along_y, pairs(2 * p.gl, 0)
    )
    swap_ax = lax.ppermute(
        jnp.where(even_x, eps[:, p.cx - 2 :], eps[:, :2]), "gx", pairs(p.gx, 0)
    )
    blocks, eps, table = lax.optimization_barrier(
        (blocks, eps, table)
    )
    spectrum_half, own, sent = call(
        lambda *refs: solve_kernel(p, *refs),
        [shape(p.ny, p.kz * LANES), shape(2 * HALO * p.kz, LANES), shape(4 * p.kz, LANES)],
        [blocks, coarse, table],
        [pltpu.VMEM((p.ny * p.kz + LANES, LANES), f32), pltpu.VMEM((8 * p.kz, LANES), f32)],
    )
    sent, eps = lax.optimization_barrier((sent, eps))
    received = lax.ppermute(sent, "gh", [(0, 1), (1, 0)])
    ex_low, ex_high = jnp.where(even_x, swap_bx, swap_ax), jnp.where(even_x, swap_ax, swap_bx)
    ey_low, ey_high = jnp.where(even_y, swap_by, swap_ay), jnp.where(even_y, swap_ay, swap_by)
    received, eps, ex_low, ex_high, ey_low, ey_high = lax.optimization_barrier(
        (received, eps, ex_low, ex_high, ey_low, ey_high)
    )
    (blocks,) = call(
        lambda *refs: return_kernel(p, *refs),
        [shape(p.ng, p.rows, LANES)],
        [
            spectrum_half, own, received, table, fine, coarse,
        ],
        [
            pltpu.VMEM((2 * HALO * p.kz, LANES), f32),
            pltpu.VMEM((p.ny * p.kz + 2 * p.edge, LANES), f32),
        ],
    )
    blocks = lax.all_to_all(blocks, group, 0, 0)
    pre, image, sums = call(
        lambda *refs: stencil_kernel(p, *refs),
        [shape(p.cy, p.cx, p.nz), shape(p.cy, p.cx, p.nz), shape(2 * p.ng, 1, LANES)],
        [
            blocks, high_z, low_z, charge, eps, ex_low, ex_high, ey_low, ey_high,
        ],
        [
            pltpu.VMEM((p.lines, p.deep), f32),
            pltpu.VMEM((p.cy + 2 * HALO, p.xw, p.nz), f32),
            pltpu.VMEM((p.cy, p.cx + 4, p.nz), f32),
            pltpu.VMEM((p.cy + 4, p.cx, p.nz), f32),
        ],
    )
    sums = lax.all_to_all(sums, ("gx", "gh", "gl"), 0, 0)
    solution_field, residual = call(
        lambda *refs: update_kernel(p, *refs),
        [shape(p.cy, p.cx, p.nz), shape(p.cy, p.cx, p.nz)],
        [sums, charge, pre, image],
    )
    return solution_field.transpose(1, 0, 2), residual.transpose(1, 0, 2)


def solution(mesh):
    count_x, count_y = mesh.shape["gx"], mesh.shape["gy"]

    def run(density, charge):
        plan = Plan(charge.shape, count_x, count_y)
        if plan.fits():
            split_mesh = jax.sharding.Mesh(
                mesh.devices.reshape(count_x, 2, count_y // 2), ("gx", "gh", "gl")
            )
            spec = P("gx", ("gh", "gl"), None)
            body, over = (lambda *args: local_planes(plan, *args)), split_mesh
        else:
            spec = P("gx", "gy", None)
            body, over = local_lines, mesh
        return jax.shard_map(
            body, mesh=over, in_specs=(spec, spec), out_specs=(spec, spec), check_vma=False
        )(density, charge)

    return run
```

```python
import math

import jax
import jax.numpy as jnp
import ml_dtypes
import numpy as np
from jax import lax
from jax.experimental import pallas as pl
from jax.experimental.pallas import tpu as pltpu
from jax.sharding import PartitionSpec as P

EPS_SOLVENT = 78.3
RHO_UPPER = 0.005
RHO_LOWER = 0.0001
KAPPA_SCALE = 0.1
EPS_PRECOND = 20.0
SHIFT_PRECOND = 0.05
HIGHEST = lax.Precision.HIGHEST
LANES = 128
HALO = 3
VMEM_LIMIT = 48 << 20


def extended(block, sides, width):
    for axis, dim in sides:
        count = lax.axis_size(axis)
        forward = [(i, i + 1) for i in range(count - 1)]
        forward.append((count - 1, 0))
        backward = [(target, source) for source, target in forward]
        low = lax.ppermute(
            lax.slice_in_dim(block, block.shape[dim] - width, None, axis=dim), axis, forward
        )
        high = lax.ppermute(lax.slice_in_dim(block, 0, width, axis=dim), axis, backward)
        block = jnp.concatenate([low, block, high], axis=dim)
    return block


def permittivity(density):
    upper = math.log(RHO_UPPER)
    lower = math.log(RHO_LOWER)
    fraction = jnp.clip((upper - jnp.log(density)) / (upper - lower), 0.0, 1.0)
    exponent = fraction - jnp.sin(2.0 * math.pi * fraction) / (2.0 * math.pi)
    return jnp.exp(exponent * math.log(EPS_SOLVENT))


def hartley(length):
    indices = jnp.arange(length, dtype=jnp.int32)
    product = indices[:, None] * indices[None, :] % length
    angles = product.astype(jnp.float32) * (2.0 * math.pi / length)
    return jnp.cos(angles) + jnp.sin(angles)


def spectrum(wavenum, length):
    halfang = wavenum.astype(jnp.float32) * (math.pi / length)
    return ((27.0 * jnp.sin(halfang) - jnp.sin(3.0 * halfang)) / 12.0) ** 2


def cutout(values, offset, length, dimen):
    return lax.slice_in_dim(values, offset, offset + length, axis=dimen)


def padded_term(padded, faces, count, dimen):
    nfaces = count + 3
    grad = (
        27.0 * (cutout(padded, 2, nfaces, dimen) - cutout(padded, 1, nfaces, dimen))
        - (cutout(padded, 3, nfaces, dimen) - cutout(padded, 0, nfaces, dimen))
    ) / 24.0
    flux = faces * grad
    return (
        27.0 * (cutout(flux, 2, count, dimen) - cutout(flux, 1, count, dimen))
        - (cutout(flux, 3, count, dimen) - cutout(flux, 0, count, dimen))
    ) / 24.0


def rolled_term(field, faces):
    grad = (
        27.0 * (jnp.roll(field, -1, 2) - field) - (jnp.roll(field, -2, 2) - jnp.roll(field, 1, 2))
    ) / 24.0
    flux = faces * grad
    return (
        27.0 * (flux - jnp.roll(flux, 1, 2)) - (jnp.roll(flux, -1, 2) - jnp.roll(flux, 2, 2))
    ) / 24.0


def operate(field, faces_x, faces_y, faces_z, kappa):
    cellsx = field.shape[0]
    cellsy = field.shape[1]
    padded = extended(field, (("gx", 0), ("gy", 1)), 3)
    term_x = padded_term(padded[:, 3 : 3 + cellsy], faces_x, cellsx, 0)
    term_y = padded_term(padded[3 : 3 + cellsx], faces_y, cellsy, 1)
    term_z = rolled_term(field, faces_z)
    return kappa * field - (term_x + term_y + term_z)


def precondition(field):
    cellsx, cellsy, length_z = field.shape
    size_x = cellsx * lax.axis_size("gx")
    size_y = cellsy * lax.axis_size("gy")
    hart_x = hartley(size_x)
    hart_y = hartley(size_y)
    hart_z = hartley(length_z)
    scaling = float(size_x * size_y * length_z)
    forward = jnp.dot(field, hart_z, precision=HIGHEST)
    zpiece = length_z // lax.axis_size("gx")
    xpiece = size_x // lax.axis_size("gy")
    lines_x = lax.all_to_all(forward, "gx", split_axis=2, concat_axis=0, tiled=True)
    along_x = jnp.einsum("xyk,xa->yka", lines_x, hart_x, precision=HIGHEST)
    lines_y = lax.all_to_all(along_x, "gy", split_axis=2, concat_axis=0, tiled=True)
    along_y = jnp.einsum("ykb,yc->kbc", lines_y, hart_y, precision=HIGHEST)
    wave_z = lax.axis_index("gx") * zpiece + jnp.arange(zpiece, dtype=jnp.int32)
    wave_x = lax.axis_index("gy") * xpiece + jnp.arange(xpiece, dtype=jnp.int32)
    wave_y = jnp.arange(size_y, dtype=jnp.int32)
    symbol = (
        EPS_PRECOND
        * (
            spectrum(wave_z, length_z)[:, None, None]
            + spectrum(wave_x, size_x)[None, :, None]
            + spectrum(wave_y, size_y)[None, None, :]
        )
        + SHIFT_PRECOND
    )
    scaled = along_y / (symbol * scaling)
    back_y = jnp.einsum("kbc,cy->ykb", scaled, hart_y, precision=HIGHEST)
    lines_back = lax.all_to_all(back_y, "gy", split_axis=0, concat_axis=2, tiled=True)
    back_x = jnp.einsum("yka,ax->xyk", lines_back, hart_x, precision=HIGHEST)
    bricks = lax.all_to_all(back_x, "gx", split_axis=0, concat_axis=2, tiled=True)
    return jnp.dot(bricks, hart_z, precision=HIGHEST)


def residual_inner(residual, precond):
    return lax.psum(jnp.sum(residual * precond), ("gx", "gy"))


def local_lines(density, charge):
    eps = permittivity(density)
    kappa = KAPPA_SCALE * (eps - 1.0) / (EPS_SOLVENT - 1.0)
    cellsx = eps.shape[0]
    cellsy = eps.shape[1]
    eps_padded = extended(eps, (("gx", 0), ("gy", 1)), 2)
    strip_x = eps_padded[:, 2 : 2 + cellsy]
    faces_x = 0.5 * (strip_x[:-1] + strip_x[1:])
    strip_y = eps_padded[2 : 2 + cellsx]
    faces_y = 0.5 * (strip_y[:, :-1] + strip_y[:, 1:])
    faces_z = 0.5 * (eps + jnp.roll(eps, -1, 2))
    rhs = 4.0 * math.pi * charge
    residual = rhs
    precond = precondition(residual)
    inner_now = residual_inner(residual, precond)
    image = operate(precond, faces_x, faces_y, faces_z, kappa)
    alpha = inner_now / lax.psum(jnp.sum(precond * image), ("gx", "gy"))
    solution_field = alpha * precond
    residual = residual - alpha * image
    return (solution_field, residual)


def cas_table(rows, columns, length):
    angle = (np.outer(rows, columns) % length).astype(np.float64) * (2.0 * np.pi / length)
    return np.cos(angle) + np.sin(angle)


def symbol_table(length):
    halfang = np.arange(length, dtype=np.float64) * (np.pi / length)
    return ((27.0 * np.sin(halfang) - np.sin(3.0 * halfang)) / 12.0) ** 2


def halves(table):
    high = table.astype(ml_dtypes.bfloat16)
    low = (table - high.astype(np.float64)).astype(ml_dtypes.bfloat16)
    return high, low


def thirds(table):
    high, low = halves(table)
    return np.concatenate([high, low, high], axis=1)


def split(values):
    high = values.astype(jnp.bfloat16)
    low = (values - high.astype(jnp.float32)).astype(jnp.bfloat16)
    return high, low


def stacked(values, axis):
    high, low = split(values)
    return jnp.concatenate([high, high, low], axis=axis)


def mul(left, right):
    return jnp.dot(left, right, preferred_element_type=jnp.float32)


def mul_t(left, right):
    return lax.dot_general(
        left, right, (((1,), (1,)), ((), ())), preferred_element_type=jnp.float32
    )


def padded_rows(values, rows):
    if values.shape[0] == rows:
        return values
    gap = jnp.zeros((rows - values.shape[0],) + values.shape[1:], values.dtype)
    return jnp.concatenate([values, gap], axis=0)


def up(size, step):
    return -(-size // step) * step


STENCIL = tuple(EPS_PRECOND * c / 576.0 for c in (-783.0, 54.0, -1.0))


class Plan:
    def __init__(self, shape, count_x, count_y):
        size_x, size_y, self.nz = shape
        self.gx, self.gl = count_x, count_y // 2
        self.nx, self.ny = size_x, size_y // 2
        self.cx, self.cy = size_x // count_x, size_y // count_y
        self.ng = self.gx * self.gl
        self.even = count_y % 2 == 0 and self.cy % 2 == 0 and self.ng > 0
        self.kz = self.nz // max(self.ng, 1)
        self.yq = self.cy // 2
        self.xp = up(self.cx, 8)
        self.xe = self.cx + 2 * HALO
        self.xw = up(self.xe, 8)
        self.yp = up(self.ny, 16)
        self.step = self.yq * self.kz
        self.edge = HALO * self.kz
        self.group = LANES // max(self.kz, 1)
        self.chunks = -(-self.ng // self.group)
        self.deep = self.chunks * LANES
        self.extra = self.cx // self.yq if self.yq else 0
        self.rows = up(2 * self.xe + self.cx + self.extra, 8)
        self.mirror = self.nx // 2 + 1
        self.lines = self.cy * self.xw + (2 * HALO - 1) * self.xp + self.yq * 8

    def fits(self):
        return (
            self.even
            and self.gx % 2 == 0
            and self.gl % 2 == 0
            and self.nz % (self.ng * 8) == 0
            and self.nz % LANES == 0
            and self.yq == 2 * HALO - 1
            and self.cx == 4 * self.yq
            and self.step <= LANES
            and self.step % 8 == 0
            and self.nx <= LANES
            and 2 * (LANES - self.nx) >= self.nx
            and 3 * self.mirror <= LANES
            and self.ny % 8 == 0
            and self.nx % 16 == 0
            and self.ny >= 2 * HALO
            and self.gx * self.xw <= LANES
        )

    def z_forward(self):
        wave = np.arange(self.nz)
        owner = wave // self.kz
        place = owner // self.group * LANES + owner % self.group * self.kz + wave % self.kz
        table = np.zeros((self.nz, self.deep))
        table[:, place] = cas_table(wave, wave, self.nz)
        return halves(table)

    def x_waves(self):
        return np.concatenate([np.arange(self.mirror), np.arange(self.nx - 1, self.mirror - 1, -1)])

    def x_forward(self):
        table = np.zeros((LANES, self.nx))
        table[: self.nx] = cas_table(self.x_waves(), np.arange(self.nx), self.nx)
        return thirds(table)

    def y_both(self):
        table = np.zeros((self.ny, self.yp))
        table[:, : self.ny] = cas_table(np.arange(self.ny), np.arange(self.ny), self.ny)
        return thirds(table)

    def ends(self):
        low = np.arange(HALO)
        return np.concatenate([low, self.ny - 1 - low])

    def y_ends(self):
        table = np.zeros((8, self.yp))
        table[: 2 * HALO, : self.ny] = cas_table(self.ends(), np.arange(self.ny), self.ny)
        return thirds(table)

    def y_sources(self):
        columns = cas_table(np.arange(self.ny), self.ends(), self.ny).T
        wide = np.broadcast_to(columns[:, :, None], (2 * HALO, self.ny, LANES))
        return np.ascontiguousarray(wide).astype(np.float32)

    def x_backward(self):
        wide = np.zeros((self.gx * self.xw, LANES))
        own = np.zeros((self.gx * self.xp, LANES))
        waves = self.x_waves()
        for g in range(self.gx):
            x = (g * self.cx - HALO + np.arange(self.xe)) % self.nx
            wide[g * self.xw : g * self.xw + self.xe, : self.nx] = cas_table(x, waves, self.nx)
            x = g * self.cx + np.arange(self.cx)
            own[g * self.xp : g * self.xp + self.cx, : self.nx] = cas_table(x, waves, self.nx)
        scale = 4.0 * np.pi / (self.nx * self.nz)
        return thirds(np.concatenate([wide, own], axis=0) * scale)

    def plane(self):
        plane = np.full((self.ny, LANES), 1e30)
        lam_x = symbol_table(self.nx)[self.x_waves()]
        plane[:, : self.nx] = lam_x[None, :] + symbol_table(self.ny)[:, None]
        return plane.astype(np.float32)

    def coarse_pack(self):
        parts = [self.x_forward(), self.y_both(), self.y_ends(), self.x_backward()]
        width = max(part.shape[1] for part in parts)
        self.places, rows = [], 0
        for part in parts:
            self.places.append((rows, part.shape))
            rows = up(rows + part.shape[0], 16)
        table = np.zeros((rows, width), ml_dtypes.bfloat16)
        for (row, shape), part in zip(self.places, parts):
            table[row : row + shape[0], : shape[1]] = part
        return table

    def fine_pack(self):
        parts = [self.plane(), self.y_sources(), self.joins()]
        return np.concatenate([part.reshape(-1, LANES) for part in parts], axis=0)

    def coarse(self, ref, which):
        row, shape = self.places[which]
        return ref[row : row + shape[0], : shape[1]]

    def join_rows(self, ref, row):
        me = lax.axis_index("gx") * self.gl + lax.axis_index("gl")
        size = (2 * HALO + 1) * self.kz
        start = (2 * HALO + 1) * self.ny + me * size + row * self.kz
        return ref[pl.ds(pl.multiple_of(start, 8), self.kz), :]

    def joins(self):
        lam_x = symbol_table(self.nx)[: self.mirror]
        lam_y, lam_z = symbol_table(self.ny), symbol_table(self.nz)
        total = EPS_PRECOND * (lam_z[:, None, None] + lam_x[None, :, None] + lam_y) + SHIFT_PRECOND
        green = np.real(np.fft.ifft(1.0 / total, axis=-1))
        i = np.arange(HALO)
        near = green[..., np.abs(i[:, None] - i[None, :])]
        far = green[..., i[:, None] + i[None, :] + 1]
        band = np.zeros((HALO, HALO))
        for row in range(HALO):
            for column in range(HALO - row):
                band[row, column] = STENCIL[row + column]
        eye = np.eye(HALO)
        even = np.linalg.inv(eye - 2.0 * (near + far) @ band)
        odd = np.linalg.inv(eye + 2.0 * (near - far) @ band)
        both = np.stack([even, odd], axis=2).reshape(self.ng, self.kz, self.mirror, 2 * HALO, HALO)
        both = both.transpose(0, 3, 1, 4, 2).reshape(self.ng, 2 * HALO, self.kz, HALO * self.mirror)
        table = np.zeros((self.ng, 2 * HALO + 1, self.kz, LANES), np.float32)
        table[:, : 2 * HALO, :, : HALO * self.mirror] = both
        table[:, 2 * HALO] = lam_z.reshape(self.ng, self.kz, 1)
        return table


VMEM_SPEC = pl.BlockSpec(memory_space=pltpu.VMEM)
ANY_SPEC = pl.BlockSpec(memory_space=pl.ANY)


def call(kernel, outs, args, scratch=(), specs=None, limit=VMEM_LIMIT):
    nbytes = sum(int(np.prod(a.shape)) * a.dtype.itemsize for a in (*args, *outs))
    return pl.pallas_call(
        kernel,
        out_shape=tuple(outs),
        in_specs=specs or [VMEM_SPEC] * len(args),
        out_specs=tuple([VMEM_SPEC] * len(outs)),
        scratch_shapes=list(scratch),
        compiler_params=pltpu.CompilerParams(vmem_limit_bytes=limit),
        cost_estimate=pl.CostEstimate(flops=0, bytes_accessed=nbytes, transcendentals=0),
    )(*args)


def lane_index(rows):
    return lax.broadcasted_iota(jnp.int32, (rows, LANES), 1)


def moved(values, shift):
    shift = shift % LANES
    return values if shift == 0 else pltpu.roll(values, shift, 1)


def between(lane, slot, width):
    return (lane >= slot * width) & (lane < (slot + 1) * width)


def fetched(pairs, sems):
    copies = [
        pltpu.make_async_copy(source, target, sems.at[i])
        for i, (source, target) in enumerate(pairs)
    ]
    for copy in copies:
        copy.start()
    return copies


def forward_kernel(p, charge_in, high_in, low_in, out, charge, high_z, low_z, sems):
    copies = fetched(((charge_in, charge), (high_in, high_z), (low_in, low_z)), sems)
    copies[0].wait()
    rows = [padded_rows(charge[y], p.xp) for y in range(p.cy)]
    high, low = split(jnp.concatenate(rows, axis=0))
    copies[1].wait()
    spec = mul(high, high_z[...]) + mul(low, high_z[...])
    copies[2].wait()
    spec = spec + mul(high, low_z[...])
    lane = lane_index(p.xp)
    for target in range(p.ng):
        chunk, slot = divmod(target, p.group)
        for part in range(2):
            block = jnp.zeros((p.xp, LANES), jnp.float32)
            for i in range(p.yq):
                y = part * p.yq + i
                piece = spec[y * p.xp : (y + 1) * p.xp, chunk * LANES : (chunk + 1) * LANES]
                block = jnp.where(between(lane, i, p.kz), moved(piece, (i - slot) * p.kz), block)
            out[target, part * p.cx : (part + 1) * p.cx] = block[: p.cx]


def table_kernel(p, fine, out):
    plane = fine[: p.ny, :]
    waves = p.join_rows(fine, 2 * HALO)
    for k in range(p.kz):
        symbol = EPS_PRECOND * (plane + waves[k : k + 1]) + SHIFT_PRECOND
        out[:, k * LANES : (k + 1) * LANES] = 1.0 / (float(p.ny) * symbol)


def lanes_of(values, k):
    return values[:, k * LANES : (k + 1) * LANES]


def solve_kernel(p, blocks, coarse, table, spectrum_out, own, sent, turned, ends):
    x_fwd, y_both, y_ends = (p.coarse(coarse, i) for i in range(3))
    columns = []
    for gl in range(p.gl):
        for part in range(2):
            pieces = [
                blocks[gx * p.gl + gl, part * p.cx : (part + 1) * p.cx] for gx in range(p.gx)
            ]
            columns.append(jnp.concatenate(pieces, axis=0))
    along_x = mul(x_fwd, stacked(jnp.concatenate(columns, axis=1), 0))
    for b in range(2 * p.gl):
        turned[pl.ds(b * p.step, LANES), :] = lanes_of(along_x, b).T
    field = jnp.concatenate(
        [turned[pl.ds(k, p.ny, stride=p.kz), :] for k in range(p.kz)], axis=1
    )
    along_y = mul(y_both, stacked(padded_rows(field, p.yp), 0))
    solved = along_y * table[...]
    spectrum_out[...] = solved
    at_ends = mul(y_ends, stacked(padded_rows(solved, p.yp), 0))
    for k in range(p.kz):
        ends[pl.ds(k, 8, stride=p.kz), :] = lanes_of(at_ends, k)
    own[...] = ends[pl.ds(0, 2 * HALO * p.kz), :]
    piece = [ends[pl.ds(j * p.kz, p.kz), :] for j in range(2 * HALO)]
    lane = lane_index(p.kz)
    free = LANES - p.nx
    for i in range(4):
        spare = moved(piece[4 + i // 2], p.nx if i % 2 == 0 else p.nx - free)
        sent[pl.ds(i * p.kz, p.kz), :] = jnp.where(lane < p.nx, piece[i], spare)


def return_kernel(
    p, spectrum_in, own, received, table, fine, coarse,
    out, sources, planes,
):
    y_both, x_bwd = p.coarse(coarse, 1), p.coarse(coarse, 3)
    y_sources = [fine[(j + 1) * p.ny : (j + 2) * p.ny, :] for j in range(2 * HALO)]
    lane = lane_index(p.kz)
    free = LANES - p.nx
    part = [received[pl.ds(i * p.kz, p.kz), :] for i in range(4)]
    other = [jnp.where(lane < p.nx, value, 0.0) for value in part]
    for i in range(2):
        first = moved(part[2 * i], -p.nx)
        second = moved(part[2 * i + 1], free - p.nx)
        other.append(jnp.where(lane < free, first, jnp.where(lane < p.nx, second, 0.0)))
    mine = [own[pl.ds(j * p.kz, p.kz), :] for j in range(2 * HALO)]
    jump = [mine[j] - other[j] for j in range(2 * HALO)]
    even = [jump[j] + jump[HALO + j] for j in range(HALO)]
    odd = [jump[j] - jump[HALO + j] for j in range(HALO)]

    def mixed(base, vector):
        results = []
        for i in range(HALO):
            packed = p.join_rows(fine, base + i)
            total = 0.0
            for j in range(HALO):
                first = moved(packed, -j * p.mirror)
                second = moved(packed, p.mirror - 1 - j * p.mirror)
                total = total + jnp.where(lane < p.mirror, first, second) * vector[j]
            results.append(total)
        return results

    even_full, odd_full = mixed(0, even), mixed(HALO, odd)
    low_full = [0.5 * (e + o) for e, o in zip(even_full, odd_full)]
    high_full = [0.5 * (e - o) for e, o in zip(even_full, odd_full)]
    far_low = [other[j] - 0.5 * (low_full[j] - jump[j]) for j in range(HALO)]
    far_high = [other[HALO + j] - 0.5 * (high_full[j] - jump[HALO + j]) for j in range(HALO)]
    for i in range(HALO):
        sources[pl.ds(i * p.kz, p.kz), :] = sum(
            STENCIL[i + j] * high_full[j] for j in range(HALO - i)
        )
        sources[pl.ds((HALO + i) * p.kz, p.kz), :] = sum(
            STENCIL[i + j] * low_full[j] for j in range(HALO - i)
        )
    whole = []
    for k in range(p.kz):
        added = sum(y_sources[j] * sources[pl.ds(j * p.kz + k, 1), :] for j in range(2 * HALO))
        whole.append(
            spectrum_in[:, k * LANES : (k + 1) * LANES]
            + added * table[:, k * LANES : (k + 1) * LANES]
        )
    back_y = mul(y_both, stacked(padded_rows(jnp.concatenate(whole, axis=1), p.yp), 0))
    base = p.edge
    for k in range(p.kz):
        planes[pl.ds(base + k, p.ny, stride=p.kz), :] = lanes_of(back_y, k)
    after = base + p.ny * p.kz
    for i in range(HALO):
        planes[pl.ds(base - (i + 1) * p.kz, p.kz), :] = far_high[i]
        planes[pl.ds(after + i * p.kz, p.kz), :] = far_low[i]
    cut = p.gx * p.xw
    wide_rows = x_bwd[:cut, :]
    own_rows = x_bwd[cut:, :]
    gap = jnp.zeros((LANES - p.step, LANES), jnp.float32)
    slots = lane_index(p.extra)
    rest = p.rows - 2 * p.xe - p.cx - p.extra
    for gl in range(p.gl):
        start = base + gl * 2 * p.step
        end = start + 2 * p.step
        last = planes[pl.ds(end + p.edge - p.kz, p.kz), :]
        both = jnp.concatenate(
            [planes[pl.ds(start, LANES), :], planes[pl.ds(start + p.step, LANES), :]], axis=0
        )
        wide = mul_t(wide_rows, stacked(both, 1))
        sides = jnp.concatenate(
            [
                planes[pl.ds(start - p.edge, p.edge), :],
                planes[pl.ds(end, p.edge - p.kz), :],
                gap,
                *[last] * p.yq,
                gap,
            ],
            axis=0,
        )
        side = mul_t(own_rows, stacked(sides, 1))
        for gx in range(p.gx):
            target = gx * p.gl + gl
            for half in range(2):
                out[target, half * p.xe : (half + 1) * p.xe] = wide[
                    gx * p.xw : gx * p.xw + p.xe, half * LANES : (half + 1) * LANES
                ]
            at, line = 2 * p.xe, gx * p.xp
            out[target, at : at + p.cx] = side[line : line + p.cx, :LANES]
            at += p.cx
            extra = jnp.zeros((p.extra, LANES), jnp.float32)
            for q in range(p.yq):
                value = side[line + q * p.extra : line + (q + 1) * p.extra, LANES:]
                extra = jnp.where(between(slots, q, p.kz), value, extra)
            out[target, at : at + p.extra] = extra
            if rest:
                out[target, at + p.extra :] = jnp.zeros((rest, LANES), jnp.float32)


def faces_kernel(p, eps, ex_low, ex_high, ey_low, ey_high, faces_x, faces_y, faces_z, mass):
    for y in range(p.cy):
        here = eps[y]
        line = jnp.concatenate([ex_low[y], here, ex_high[y]], axis=0)
        faces_x[y, : p.cx + 3] = line[: p.cx + 3] + line[1 : p.cx + 4]
        faces_z[y] = here + pltpu.roll(here, p.nz - 1, 1)
        mass[y] = (KAPPA_SCALE / (EPS_SOLVENT - 1.0)) * (here - 1.0)
    planes = [ey_low[0], ey_low[1], *[eps[y] for y in range(p.cy)], ey_high[0], ey_high[1]]
    for y in range(p.cy + 3):
        faces_y[y] = planes[y] + planes[y + 1]


def stencil_kernel(
    p, blocks, high_z, low_z, charge, faces_x, faces_y, faces_z, mass,
    pre, image, sums, lines, field,
):
    lane = lane_index(p.xw)
    windows, at = [], 0
    for y in range(p.cy):
        half = y // p.yq
        windows.append((half * p.xe // 8 * 8, p.xw, y % p.yq, at))
        at += p.xw
    side = 2 * p.xe
    for h in range(2 * HALO - 1):
        windows.append((side // 8 * 8, p.xp, h, at))
        at += p.xp
    tail = side + p.cx
    for q in range(p.yq):
        windows.append((tail // 8 * 8, 8, q, at))
        at += 8
    for chunk in range(p.chunks):
        count = min(p.group, p.ng - chunk * p.group)
        for first, rows, piece, at in windows:
            here = lane[:rows]
            line = jnp.zeros((rows, LANES), jnp.float32)
            for slot in range(count):
                part = blocks[chunk * p.group + slot, first : first + rows, :]
                part = moved(part, (slot - piece) * p.kz)
                line = jnp.where(between(here, slot, p.kz), part, line)
            lines[at : at + rows, chunk * LANES : (chunk + 1) * LANES] = line
    high, low = split(lines[...])
    whole = mul_t(high, high_z[...]) + mul_t(low, high_z[...]) + mul_t(high, low_z[...])
    for y in range(p.cy):
        first, rows, piece, at = windows[y]
        off = (y // p.yq) * p.xe - first
        field[HALO + y, : p.xe] = whole[at + off : at + off + p.xe]
    for h in range(2 * HALO - 1):
        first, rows, piece, at = windows[p.cy + h]
        off = side - first
        y = h if h < HALO else h + p.cy
        field[y, HALO : HALO + p.cx] = whole[at + off : at + off + p.cx]
    for q in range(p.yq):
        first, rows, piece, at = windows[p.cy + 2 * HALO - 1 + q]
        off = tail - first
        field[p.cy + 2 * HALO - 1, HALO + q * p.extra : HALO + (q + 1) * p.extra] = whole[
            at + off : at + off + p.extra
        ]
    def stretch(flux_at):
        return 27.0 * (flux_at(2) - flux_at(1)) - (flux_at(3) - flux_at(0))

    rz = jnp.zeros((p.cx, LANES), jnp.float32)
    dot = jnp.zeros((p.cx, LANES), jnp.float32)
    fluxes_y = {}

    def flux_y(y):
        if y not in fluxes_y:
            val = [field[y + i, HALO : HALO + p.cx, :] for i in range(4)]
            fluxes_y[y] = faces_y[y] * stretch(lambda i: val[i])
        return fluxes_y[y]

    n = p.nz
    for y in range(p.cy):
        line = field[HALO + y]
        flux = faces_x[y, : p.cx + 3] * stretch(lambda i: line[i : i + p.cx + 3])
        term = stretch(lambda i: flux[i : i + p.cx])
        term = term + stretch(lambda i: flux_y(y + i))
        here = line[HALO : HALO + p.cx]
        grad = 27.0 * (pltpu.roll(here, n - 1, 1) - here) - (
            pltpu.roll(here, n - 2, 1) - pltpu.roll(here, 1, 1)
        )
        flux = faces_z[y] * grad
        term = term + (
            27.0 * (flux - pltpu.roll(flux, 1, 1))
            - (pltpu.roll(flux, n - 1, 1) - pltpu.roll(flux, 2, 1))
        )
        result = mass[y] * here - term * (0.5 / 576.0)
        pre[y] = here
        image[y] = result
        one = charge[y] * here
        two = result * here
        for c in range(n // LANES):
            rz = rz + one[:, c * LANES : (c + 1) * LANES]
            dot = dot + two[:, c * LANES : (c + 1) * LANES]
    rz = jnp.sum(rz, axis=0, keepdims=True)
    dot = jnp.sum(dot, axis=0, keepdims=True)
    half = LANES // 2
    rz = rz + pltpu.roll(rz, half, 1)
    dot = dot + pltpu.roll(dot, half, 1)
    both = jnp.where(lane_index(1) < half, rz, dot)
    sums[...] = jnp.broadcast_to(both[None], sums.shape)


def update_kernel(p, sums, charge, pre, image, solution_field, residual):
    half = LANES // 2
    total = jnp.sum(sums[...], axis=0)
    lane = lane_index(1)
    rz = jnp.sum(jnp.where(lane < half, total, 0.0), axis=1, keepdims=True)
    dot = jnp.sum(jnp.where(lane < half, 0.0, total), axis=1, keepdims=True)
    alpha = jnp.broadcast_to((4.0 * math.pi) * rz / dot, (p.cx, p.nz))
    for y in range(p.cy):
        solution_field[y] = alpha * pre[y]
        residual[y] = (4.0 * math.pi) * charge[y] - alpha * image[y]


def local_planes(p, density, charge):
    group = ("gx", "gl")
    along_y = ("gh", "gl")
    f32 = jnp.float32

    def shape(*dims):
        return jax.ShapeDtypeStruct(dims, f32)

    def pairs(count, first):
        low = range(first, count, 2)
        near = [(i, (i + 1) % count) for i in low]
        return near + [(target, source) for source, target in near]

    even_x = lax.axis_index("gx") % 2 == 0
    even_y = lax.axis_index("gl") % 2 == 0

    density = density.transpose(1, 0, 2)
    charge = charge.transpose(1, 0, 2)
    high_z, low_z = (jnp.asarray(part) for part in p.z_forward())
    coarse, fine = jnp.asarray(p.coarse_pack()), jnp.asarray(p.fine_pack())
    (blocks,) = call(
        lambda *refs: forward_kernel(p, *refs),
        [shape(p.ng, 2 * p.cx, LANES)],
        [charge, high_z, low_z],
        [
            pltpu.VMEM((p.cy, p.cx, p.nz), f32),
            pltpu.VMEM((p.nz, p.deep), jnp.bfloat16),
            pltpu.VMEM((p.nz, p.deep), jnp.bfloat16),
            pltpu.SemaphoreType.DMA((3,)),
        ],
        specs=[ANY_SPEC] * 3,
        limit=None,
    )
    blocks = lax.all_to_all(blocks, group, 0, 0)
    (table,) = call(
        lambda *refs: table_kernel(p, *refs), [shape(p.ny, p.kz * LANES)], [fine]
    )
    eps = permittivity(density)
    swap_by = lax.ppermute(
        jnp.where(even_y, eps[:2], eps[p.cy - 2 :]), along_y, pairs(2 * p.gl, 1)
    )
    swap_bx = lax.ppermute(
        jnp.where(even_x, eps[:, :2], eps[:, p.cx - 2 :]), "gx", pairs(p.gx, 1)
    )
    swap_ay = lax.ppermute(
        jnp.where(even_y, eps[p.cy - 2 :], eps[:2]), along_y, pairs(2 * p.gl, 0)
    )
    swap_ax = lax.ppermute(
        jnp.where(even_x, eps[:, p.cx - 2 :], eps[:, :2]), "gx", pairs(p.gx, 0)
    )
    blocks, eps, table = lax.optimization_barrier(
        (blocks, eps, table)
    )
    spectrum_half, own, sent = call(
        lambda *refs: solve_kernel(p, *refs),
        [shape(p.ny, p.kz * LANES), shape(2 * HALO * p.kz, LANES), shape(4 * p.kz, LANES)],
        [blocks, coarse, table],
        [pltpu.VMEM((p.ny * p.kz + LANES, LANES), f32), pltpu.VMEM((8 * p.kz, LANES), f32)],
    )
    sent, eps = lax.optimization_barrier((sent, eps))
    received = lax.ppermute(sent, "gh", [(0, 1), (1, 0)])
    ex_low, ex_high = jnp.where(even_x, swap_bx, swap_ax), jnp.where(even_x, swap_ax, swap_bx)
    ey_low, ey_high = jnp.where(even_y, swap_by, swap_ay), jnp.where(even_y, swap_ay, swap_by)
    brick = (p.cy, p.cx, p.nz)
    faces = call(
        lambda *refs: faces_kernel(p, *refs),
        [
            shape(p.cy, p.xp, p.nz), shape(p.cy + 3, p.cx, p.nz), shape(*brick), shape(*brick),
        ],
        [eps, ex_low, ex_high, ey_low, ey_high],
    )
    received, *faces = lax.optimization_barrier((received, *faces))
    (blocks,) = call(
        lambda *refs: return_kernel(p, *refs),
        [shape(p.ng, p.rows, LANES)],
        [
            spectrum_half, own, received, table, fine, coarse,
        ],
        [
            pltpu.VMEM((2 * HALO * p.kz, LANES), f32),
            pltpu.VMEM((p.ny * p.kz + 2 * p.edge, LANES), f32),
        ],
    )
    blocks = lax.all_to_all(blocks, group, 0, 0)
    pre, image, sums = call(
        lambda *refs: stencil_kernel(p, *refs),
        [shape(*brick), shape(*brick), shape(2 * p.ng, 1, LANES)],
        [blocks, high_z, low_z, charge, *faces],
        [
            pltpu.VMEM((p.lines, p.deep), f32),
            pltpu.VMEM((p.cy + 2 * HALO, p.xw, p.nz), f32),
        ],
    )
    sums = lax.all_to_all(sums, ("gx", "gh", "gl"), 0, 0)
    solution_field, residual = call(
        lambda *refs: update_kernel(p, *refs),
        [shape(*brick), shape(*brick)],
        [sums, charge, pre, image],
    )
    return solution_field.transpose(1, 0, 2), residual.transpose(1, 0, 2)


def solution(mesh):
    count_x, count_y = mesh.shape["gx"], mesh.shape["gy"]

    def run(density, charge):
        plan = Plan(charge.shape, count_x, count_y)
        if plan.fits():
            split_mesh = jax.sharding.Mesh(
                mesh.devices.reshape(count_x, 2, count_y // 2), ("gx", "gh", "gl")
            )
            spec = P("gx", ("gh", "gl"), None)
            body, over = (lambda *args: local_planes(plan, *args)), split_mesh
        else:
            spec = P("gx", "gy", None)
            body, over = local_lines, mesh
        return jax.shard_map(
            body, mesh=over, in_specs=(spec, spec), out_specs=(spec, spec), check_vma=False
        )(density, charge)

    return run
```

```python
import math

import jax
import jax.numpy as jnp
import ml_dtypes
import numpy as np
from jax import lax
from jax.experimental import pallas as pl
from jax.experimental.pallas import tpu as pltpu
from jax.sharding import PartitionSpec as P

EPS_SOLVENT = 78.3
RHO_UPPER = 0.005
RHO_LOWER = 0.0001
KAPPA_SCALE = 0.1
EPS_PRECOND = 20.0
SHIFT_PRECOND = 0.05
HIGHEST = lax.Precision.HIGHEST
LANES = 128
HALO = 3
VMEM_LIMIT = 48 << 20


def extended(block, sides, width):
    for axis, dim in sides:
        count = lax.axis_size(axis)
        forward = [(i, i + 1) for i in range(count - 1)]
        forward.append((count - 1, 0))
        backward = [(target, source) for source, target in forward]
        low = lax.ppermute(
            lax.slice_in_dim(block, block.shape[dim] - width, None, axis=dim), axis, forward
        )
        high = lax.ppermute(lax.slice_in_dim(block, 0, width, axis=dim), axis, backward)
        block = jnp.concatenate([low, block, high], axis=dim)
    return block


def permittivity(density):
    upper = math.log(RHO_UPPER)
    lower = math.log(RHO_LOWER)
    fraction = jnp.clip((upper - jnp.log(density)) / (upper - lower), 0.0, 1.0)
    exponent = fraction - jnp.sin(2.0 * math.pi * fraction) / (2.0 * math.pi)
    return jnp.exp(exponent * math.log(EPS_SOLVENT))


def hartley(length):
    indices = jnp.arange(length, dtype=jnp.int32)
    product = indices[:, None] * indices[None, :] % length
    angles = product.astype(jnp.float32) * (2.0 * math.pi / length)
    return jnp.cos(angles) + jnp.sin(angles)


def spectrum(wavenum, length):
    halfang = wavenum.astype(jnp.float32) * (math.pi / length)
    return ((27.0 * jnp.sin(halfang) - jnp.sin(3.0 * halfang)) / 12.0) ** 2


def cutout(values, offset, length, dimen):
    return lax.slice_in_dim(values, offset, offset + length, axis=dimen)


def padded_term(padded, faces, count, dimen):
    nfaces = count + 3
    grad = (
        27.0 * (cutout(padded, 2, nfaces, dimen) - cutout(padded, 1, nfaces, dimen))
        - (cutout(padded, 3, nfaces, dimen) - cutout(padded, 0, nfaces, dimen))
    ) / 24.0
    flux = faces * grad
    return (
        27.0 * (cutout(flux, 2, count, dimen) - cutout(flux, 1, count, dimen))
        - (cutout(flux, 3, count, dimen) - cutout(flux, 0, count, dimen))
    ) / 24.0


def rolled_term(field, faces):
    grad = (
        27.0 * (jnp.roll(field, -1, 2) - field) - (jnp.roll(field, -2, 2) - jnp.roll(field, 1, 2))
    ) / 24.0
    flux = faces * grad
    return (
        27.0 * (flux - jnp.roll(flux, 1, 2)) - (jnp.roll(flux, -1, 2) - jnp.roll(flux, 2, 2))
    ) / 24.0


def operate(field, faces_x, faces_y, faces_z, kappa):
    cellsx = field.shape[0]
    cellsy = field.shape[1]
    padded = extended(field, (("gx", 0), ("gy", 1)), 3)
    term_x = padded_term(padded[:, 3 : 3 + cellsy], faces_x, cellsx, 0)
    term_y = padded_term(padded[3 : 3 + cellsx], faces_y, cellsy, 1)
    term_z = rolled_term(field, faces_z)
    return kappa * field - (term_x + term_y + term_z)


def precondition(field):
    cellsx, cellsy, length_z = field.shape
    size_x = cellsx * lax.axis_size("gx")
    size_y = cellsy * lax.axis_size("gy")
    hart_x = hartley(size_x)
    hart_y = hartley(size_y)
    hart_z = hartley(length_z)
    scaling = float(size_x * size_y * length_z)
    forward = jnp.dot(field, hart_z, precision=HIGHEST)
    zpiece = length_z // lax.axis_size("gx")
    xpiece = size_x // lax.axis_size("gy")
    lines_x = lax.all_to_all(forward, "gx", split_axis=2, concat_axis=0, tiled=True)
    along_x = jnp.einsum("xyk,xa->yka", lines_x, hart_x, precision=HIGHEST)
    lines_y = lax.all_to_all(along_x, "gy", split_axis=2, concat_axis=0, tiled=True)
    along_y = jnp.einsum("ykb,yc->kbc", lines_y, hart_y, precision=HIGHEST)
    wave_z = lax.axis_index("gx") * zpiece + jnp.arange(zpiece, dtype=jnp.int32)
    wave_x = lax.axis_index("gy") * xpiece + jnp.arange(xpiece, dtype=jnp.int32)
    wave_y = jnp.arange(size_y, dtype=jnp.int32)
    symbol = (
        EPS_PRECOND
        * (
            spectrum(wave_z, length_z)[:, None, None]
            + spectrum(wave_x, size_x)[None, :, None]
            + spectrum(wave_y, size_y)[None, None, :]
        )
        + SHIFT_PRECOND
    )
    scaled = along_y / (symbol * scaling)
    back_y = jnp.einsum("kbc,cy->ykb", scaled, hart_y, precision=HIGHEST)
    lines_back = lax.all_to_all(back_y, "gy", split_axis=0, concat_axis=2, tiled=True)
    back_x = jnp.einsum("yka,ax->xyk", lines_back, hart_x, precision=HIGHEST)
    bricks = lax.all_to_all(back_x, "gx", split_axis=0, concat_axis=2, tiled=True)
    return jnp.dot(bricks, hart_z, precision=HIGHEST)


def residual_inner(residual, precond):
    return lax.psum(jnp.sum(residual * precond), ("gx", "gy"))


def local_lines(density, charge):
    eps = permittivity(density)
    kappa = KAPPA_SCALE * (eps - 1.0) / (EPS_SOLVENT - 1.0)
    cellsx = eps.shape[0]
    cellsy = eps.shape[1]
    eps_padded = extended(eps, (("gx", 0), ("gy", 1)), 2)
    strip_x = eps_padded[:, 2 : 2 + cellsy]
    faces_x = 0.5 * (strip_x[:-1] + strip_x[1:])
    strip_y = eps_padded[2 : 2 + cellsx]
    faces_y = 0.5 * (strip_y[:, :-1] + strip_y[:, 1:])
    faces_z = 0.5 * (eps + jnp.roll(eps, -1, 2))
    rhs = 4.0 * math.pi * charge
    residual = rhs
    precond = precondition(residual)
    inner_now = residual_inner(residual, precond)
    image = operate(precond, faces_x, faces_y, faces_z, kappa)
    alpha = inner_now / lax.psum(jnp.sum(precond * image), ("gx", "gy"))
    solution_field = alpha * precond
    residual = residual - alpha * image
    return (solution_field, residual)


def cas_table(rows, columns, length):
    angle = (np.outer(rows, columns) % length).astype(np.float64) * (2.0 * np.pi / length)
    return np.cos(angle) + np.sin(angle)


def symbol_table(length):
    halfang = np.arange(length, dtype=np.float64) * (np.pi / length)
    return ((27.0 * np.sin(halfang) - np.sin(3.0 * halfang)) / 12.0) ** 2


def halves(table):
    high = table.astype(ml_dtypes.bfloat16)
    low = (table - high.astype(np.float64)).astype(ml_dtypes.bfloat16)
    return high, low


def thirds(table):
    high, low = halves(table)
    return np.concatenate([high, low, high], axis=1)


def split(values):
    high = values.astype(jnp.bfloat16)
    low = (values - high.astype(jnp.float32)).astype(jnp.bfloat16)
    return high, low


def stacked(values, axis):
    high, low = split(values)
    return jnp.concatenate([high, high, low], axis=axis)


def mul(left, right):
    return jnp.dot(left, right, preferred_element_type=jnp.float32)


def mul_t(left, right):
    return lax.dot_general(
        left, right, (((1,), (1,)), ((), ())), preferred_element_type=jnp.float32
    )


def padded_rows(values, rows):
    if values.shape[0] == rows:
        return values
    gap = jnp.zeros((rows - values.shape[0],) + values.shape[1:], values.dtype)
    return jnp.concatenate([values, gap], axis=0)


def up(size, step):
    return -(-size // step) * step


STENCIL = tuple(EPS_PRECOND * c / 576.0 for c in (-783.0, 54.0, -1.0))


class Plan:
    def __init__(self, shape, count_x, count_y):
        size_x, size_y, self.nz = shape
        self.gx, self.gl = count_x, count_y // 2
        self.nx, self.ny = size_x, size_y // 2
        self.cx, self.cy = size_x // count_x, size_y // count_y
        self.ng = self.gx * self.gl
        self.even = count_y % 2 == 0 and self.cy % 2 == 0 and self.ng > 0
        self.kz = self.nz // max(self.ng, 1)
        self.yq = self.cy // 2
        self.xp = up(self.cx, 8)
        self.xe = self.cx + 2 * HALO
        self.xw = up(self.xe, 8)
        self.yp = up(self.ny, 16)
        self.step = self.yq * self.kz
        self.edge = HALO * self.kz
        self.group = LANES // max(self.kz, 1)
        self.chunks = -(-self.ng // self.group)
        self.deep = self.chunks * LANES
        self.extra = self.cx // self.yq if self.yq else 0
        self.rows = up(2 * self.xe + self.cx + self.extra, 8)
        self.mirror = self.nx // 2 + 1
        self.lines = self.cy * self.xw + (2 * HALO - 1) * self.xp + self.yq * 8

    def fits(self):
        return (
            self.even
            and self.gx % 2 == 0
            and self.gl % 2 == 0
            and self.nz % (self.ng * 8) == 0
            and self.nz % LANES == 0
            and self.yq == 2 * HALO - 1
            and self.cx == 4 * self.yq
            and self.step <= LANES
            and self.step % 8 == 0
            and self.nx <= LANES
            and 2 * (LANES - self.nx) >= self.nx
            and 3 * self.mirror <= LANES
            and self.ny % 8 == 0
            and self.nx % 16 == 0
            and self.ny >= 2 * HALO
            and self.gx * self.xw <= LANES
        )

    def z_forward(self):
        wave = np.arange(self.nz)
        owner = wave // self.kz
        place = owner // self.group * LANES + owner % self.group * self.kz + wave % self.kz
        table = np.zeros((self.nz, self.deep))
        table[:, place] = cas_table(wave, wave, self.nz)
        return halves(table)

    def x_waves(self):
        return np.concatenate([np.arange(self.mirror), np.arange(self.nx - 1, self.mirror - 1, -1)])

    def x_forward(self):
        table = np.zeros((LANES, self.nx))
        table[: self.nx] = cas_table(self.x_waves(), np.arange(self.nx), self.nx)
        return thirds(table)

    def y_both(self):
        table = np.zeros((self.ny, self.yp))
        table[:, : self.ny] = cas_table(np.arange(self.ny), np.arange(self.ny), self.ny)
        return thirds(table)

    def ends(self):
        low = np.arange(HALO)
        return np.concatenate([low, self.ny - 1 - low])

    def y_ends(self):
        table = np.zeros((8, self.yp))
        table[: 2 * HALO, : self.ny] = cas_table(self.ends(), np.arange(self.ny), self.ny)
        return thirds(table)

    def y_sources(self):
        columns = cas_table(np.arange(self.ny), self.ends(), self.ny).T
        wide = np.broadcast_to(columns[:, :, None], (2 * HALO, self.ny, LANES))
        return np.ascontiguousarray(wide).astype(np.float32)

    def x_backward(self):
        wide = np.zeros((self.gx * self.xw, LANES))
        own = np.zeros((self.gx * self.xp, LANES))
        waves = self.x_waves()
        for g in range(self.gx):
            x = (g * self.cx - HALO + np.arange(self.xe)) % self.nx
            wide[g * self.xw : g * self.xw + self.xe, : self.nx] = cas_table(x, waves, self.nx)
            x = g * self.cx + np.arange(self.cx)
            own[g * self.xp : g * self.xp + self.cx, : self.nx] = cas_table(x, waves, self.nx)
        scale = 4.0 * np.pi / (self.nx * self.nz)
        return thirds(np.concatenate([wide, own], axis=0) * scale)

    def plane(self):
        plane = np.full((self.ny, LANES), 1e30)
        lam_x = symbol_table(self.nx)[self.x_waves()]
        plane[:, : self.nx] = lam_x[None, :] + symbol_table(self.ny)[:, None]
        return plane.astype(np.float32)

    def coarse_pack(self):
        parts = [self.x_forward(), self.y_both(), self.y_ends(), self.x_backward()]
        width = max(part.shape[1] for part in parts)
        self.places, rows = [], 0
        for part in parts:
            self.places.append((rows, part.shape))
            rows = up(rows + part.shape[0], 16)
        table = np.zeros((rows, width), ml_dtypes.bfloat16)
        for (row, shape), part in zip(self.places, parts):
            table[row : row + shape[0], : shape[1]] = part
        return table

    def fine_pack(self):
        parts = [self.plane(), self.y_sources(), self.joins()]
        return np.concatenate([part.reshape(-1, LANES) for part in parts], axis=0)

    def coarse(self, ref, which):
        row, shape = self.places[which]
        return ref[row : row + shape[0], : shape[1]]

    def join_rows(self, ref, row):
        me = lax.axis_index("gx") * self.gl + lax.axis_index("gl")
        size = (2 * HALO + 1) * self.kz
        start = (2 * HALO + 1) * self.ny + me * size + row * self.kz
        return ref[pl.ds(pl.multiple_of(start, 8), self.kz), :]

    def joins(self):
        lam_x = symbol_table(self.nx)[: self.mirror]
        lam_y, lam_z = symbol_table(self.ny), symbol_table(self.nz)
        total = EPS_PRECOND * (lam_z[:, None, None] + lam_x[None, :, None] + lam_y) + SHIFT_PRECOND
        green = np.real(np.fft.ifft(1.0 / total, axis=-1))
        i = np.arange(HALO)
        near = green[..., np.abs(i[:, None] - i[None, :])]
        far = green[..., i[:, None] + i[None, :] + 1]
        band = np.zeros((HALO, HALO))
        for row in range(HALO):
            for column in range(HALO - row):
                band[row, column] = STENCIL[row + column]
        eye = np.eye(HALO)
        even = np.linalg.inv(eye - 2.0 * (near + far) @ band)
        odd = np.linalg.inv(eye + 2.0 * (near - far) @ band)
        both = np.stack([even, odd], axis=2).reshape(self.ng, self.kz, self.mirror, 2 * HALO, HALO)
        both = both.transpose(0, 3, 1, 4, 2).reshape(self.ng, 2 * HALO, self.kz, HALO * self.mirror)
        table = np.zeros((self.ng, 2 * HALO + 1, self.kz, LANES), np.float32)
        table[:, : 2 * HALO, :, : HALO * self.mirror] = both
        table[:, 2 * HALO] = lam_z.reshape(self.ng, self.kz, 1)
        return table


VMEM_SPEC = pl.BlockSpec(memory_space=pltpu.VMEM)
ANY_SPEC = pl.BlockSpec(memory_space=pl.ANY)


def call(kernel, outs, args, scratch=(), specs=None, limit=VMEM_LIMIT):
    nbytes = sum(int(np.prod(a.shape)) * a.dtype.itemsize for a in (*args, *outs))
    return pl.pallas_call(
        kernel,
        out_shape=tuple(outs),
        in_specs=specs or [VMEM_SPEC] * len(args),
        out_specs=tuple([VMEM_SPEC] * len(outs)),
        scratch_shapes=list(scratch),
        compiler_params=pltpu.CompilerParams(vmem_limit_bytes=limit),
        cost_estimate=pl.CostEstimate(flops=0, bytes_accessed=nbytes, transcendentals=0),
    )(*args)


def lane_index(rows):
    return lax.broadcasted_iota(jnp.int32, (rows, LANES), 1)


def moved(values, shift):
    shift = shift % LANES
    return values if shift == 0 else pltpu.roll(values, shift, 1)


def between(lane, slot, width):
    return (lane >= slot * width) & (lane < (slot + 1) * width)


def fetched(pairs, sems):
    copies = [
        pltpu.make_async_copy(source, target, sems.at[i])
        for i, (source, target) in enumerate(pairs)
    ]
    for copy in copies:
        copy.start()
    return copies


def forward_kernel(p, charge_in, high_in, low_in, out, charge, high_z, low_z, sems):
    copies = fetched(((charge_in, charge), (high_in, high_z), (low_in, low_z)), sems)
    copies[0].wait()
    lane = lane_index(p.xp)
    ready = False
    for part in range(2):
        ys = range(part * p.yq, (part + 1) * p.yq)
        high, low = split(jnp.concatenate([padded_rows(charge[y], p.xp) for y in ys], axis=0))
        if not ready:
            copies[1].wait()
        spec = mul(high, high_z[...]) + mul(low, high_z[...])
        if not ready:
            copies[2].wait()
            ready = True
        spec = spec + mul(high, low_z[...])
        for target in range(p.ng):
            chunk, slot = divmod(target, p.group)
            block = jnp.zeros((p.xp, LANES), jnp.float32)
            for i in range(p.yq):
                piece = spec[i * p.xp : (i + 1) * p.xp, chunk * LANES : (chunk + 1) * LANES]
                block = jnp.where(between(lane, i, p.kz), moved(piece, (i - slot) * p.kz), block)
            out[target, part * p.cx : (part + 1) * p.cx] = block[: p.cx]


def table_kernel(p, fine, out):
    plane = fine[: p.ny, :]
    waves = p.join_rows(fine, 2 * HALO)
    for k in range(p.kz):
        symbol = EPS_PRECOND * (plane + waves[k : k + 1]) + SHIFT_PRECOND
        out[:, k * LANES : (k + 1) * LANES] = 1.0 / (float(p.ny) * symbol)


def lanes_of(values, k):
    return values[:, k * LANES : (k + 1) * LANES]


def solve_kernel(p, blocks, coarse, table, spectrum_out, own, sent, turned, ends):
    x_fwd, y_both, y_ends = (p.coarse(coarse, i) for i in range(3))
    columns = []
    for gl in range(p.gl):
        for part in range(2):
            pieces = [
                blocks[gx * p.gl + gl, part * p.cx : (part + 1) * p.cx] for gx in range(p.gx)
            ]
            columns.append(jnp.concatenate(pieces, axis=0))
    along_x = mul(x_fwd, stacked(jnp.concatenate(columns, axis=1), 0))
    for b in range(2 * p.gl):
        turned[pl.ds(b * p.step, LANES), :] = lanes_of(along_x, b).T
    field = jnp.concatenate(
        [turned[pl.ds(k, p.ny, stride=p.kz), :] for k in range(p.kz)], axis=1
    )
    along_y = mul(y_both, stacked(padded_rows(field, p.yp), 0))
    solved = along_y * table[...]
    spectrum_out[...] = solved
    at_ends = mul(y_ends, stacked(padded_rows(solved, p.yp), 0))
    for k in range(p.kz):
        ends[pl.ds(k, 8, stride=p.kz), :] = lanes_of(at_ends, k)
    own[...] = ends[pl.ds(0, 2 * HALO * p.kz), :]
    piece = [ends[pl.ds(j * p.kz, p.kz), :] for j in range(2 * HALO)]
    lane = lane_index(p.kz)
    free = LANES - p.nx
    for i in range(4):
        spare = moved(piece[4 + i // 2], p.nx if i % 2 == 0 else p.nx - free)
        sent[pl.ds(i * p.kz, p.kz), :] = jnp.where(lane < p.nx, piece[i], spare)


def return_kernel(
    p, spectrum_in, own, received, table, fine, coarse,
    out, sources, planes,
):
    y_both, x_bwd = p.coarse(coarse, 1), p.coarse(coarse, 3)
    y_sources = [fine[(j + 1) * p.ny : (j + 2) * p.ny, :] for j in range(2 * HALO)]
    lane = lane_index(p.kz)
    free = LANES - p.nx
    part = [received[pl.ds(i * p.kz, p.kz), :] for i in range(4)]
    other = [jnp.where(lane < p.nx, value, 0.0) for value in part]
    for i in range(2):
        first = moved(part[2 * i], -p.nx)
        second = moved(part[2 * i + 1], free - p.nx)
        other.append(jnp.where(lane < free, first, jnp.where(lane < p.nx, second, 0.0)))
    mine = [own[pl.ds(j * p.kz, p.kz), :] for j in range(2 * HALO)]
    jump = [mine[j] - other[j] for j in range(2 * HALO)]
    even = [jump[j] + jump[HALO + j] for j in range(HALO)]
    odd = [jump[j] - jump[HALO + j] for j in range(HALO)]

    def mixed(base, vector):
        results = []
        for i in range(HALO):
            packed = p.join_rows(fine, base + i)
            total = 0.0
            for j in range(HALO):
                first = moved(packed, -j * p.mirror)
                second = moved(packed, p.mirror - 1 - j * p.mirror)
                total = total + jnp.where(lane < p.mirror, first, second) * vector[j]
            results.append(total)
        return results

    even_full, odd_full = mixed(0, even), mixed(HALO, odd)
    low_full = [0.5 * (e + o) for e, o in zip(even_full, odd_full)]
    high_full = [0.5 * (e - o) for e, o in zip(even_full, odd_full)]
    far_low = [other[j] - 0.5 * (low_full[j] - jump[j]) for j in range(HALO)]
    far_high = [other[HALO + j] - 0.5 * (high_full[j] - jump[HALO + j]) for j in range(HALO)]
    for i in range(HALO):
        sources[pl.ds(i * p.kz, p.kz), :] = sum(
            STENCIL[i + j] * high_full[j] for j in range(HALO - i)
        )
        sources[pl.ds((HALO + i) * p.kz, p.kz), :] = sum(
            STENCIL[i + j] * low_full[j] for j in range(HALO - i)
        )
    whole = []
    for k in range(p.kz):
        added = sum(y_sources[j] * sources[pl.ds(j * p.kz + k, 1), :] for j in range(2 * HALO))
        whole.append(
            spectrum_in[:, k * LANES : (k + 1) * LANES]
            + added * table[:, k * LANES : (k + 1) * LANES]
        )
    back_y = mul(y_both, stacked(padded_rows(jnp.concatenate(whole, axis=1), p.yp), 0))
    base = p.edge
    for k in range(p.kz):
        planes[pl.ds(base + k, p.ny, stride=p.kz), :] = lanes_of(back_y, k)
    after = base + p.ny * p.kz
    for i in range(HALO):
        planes[pl.ds(base - (i + 1) * p.kz, p.kz), :] = far_high[i]
        planes[pl.ds(after + i * p.kz, p.kz), :] = far_low[i]
    cut = p.gx * p.xw
    wide_rows = x_bwd[:cut, :]
    own_rows = x_bwd[cut:, :]
    gap = jnp.zeros((LANES - p.step, LANES), jnp.float32)
    slots = lane_index(p.extra)
    rest = p.rows - 2 * p.xe - p.cx - p.extra
    for gl in range(p.gl):
        start = base + gl * 2 * p.step
        end = start + 2 * p.step
        last = planes[pl.ds(end + p.edge - p.kz, p.kz), :]
        both = jnp.concatenate(
            [planes[pl.ds(start, LANES), :], planes[pl.ds(start + p.step, LANES), :]], axis=0
        )
        wide = mul_t(wide_rows, stacked(both, 1))
        sides = jnp.concatenate(
            [
                planes[pl.ds(start - p.edge, p.edge), :],
                planes[pl.ds(end, p.edge - p.kz), :],
                gap,
                *[last] * p.yq,
                gap,
            ],
            axis=0,
        )
        side = mul_t(own_rows, stacked(sides, 1))
        for gx in range(p.gx):
            target = gx * p.gl + gl
            for half in range(2):
                out[target, half * p.xe : (half + 1) * p.xe] = wide[
                    gx * p.xw : gx * p.xw + p.xe, half * LANES : (half + 1) * LANES
                ]
            at, line = 2 * p.xe, gx * p.xp
            out[target, at : at + p.cx] = side[line : line + p.cx, :LANES]
            at += p.cx
            extra = jnp.zeros((p.extra, LANES), jnp.float32)
            for q in range(p.yq):
                value = side[line + q * p.extra : line + (q + 1) * p.extra, LANES:]
                extra = jnp.where(between(slots, q, p.kz), value, extra)
            out[target, at : at + p.extra] = extra
            if rest:
                out[target, at + p.extra :] = jnp.zeros((rest, LANES), jnp.float32)


def faces_kernel(p, eps, ex_low, ex_high, ey_low, ey_high, faces_x, faces_y, faces_z, mass):
    for y in range(p.cy):
        here = eps[y]
        line = jnp.concatenate([ex_low[y], here, ex_high[y]], axis=0)
        faces_x[y, : p.cx + 3] = line[: p.cx + 3] + line[1 : p.cx + 4]
        faces_z[y] = here + pltpu.roll(here, p.nz - 1, 1)
        mass[y] = (KAPPA_SCALE / (EPS_SOLVENT - 1.0)) * (here - 1.0)
    planes = [ey_low[0], ey_low[1], *[eps[y] for y in range(p.cy)], ey_high[0], ey_high[1]]
    for y in range(p.cy + 3):
        faces_y[y] = planes[y] + planes[y + 1]


def stencil_kernel(
    p, blocks, high_z, low_z, charge, faces_x, faces_y, faces_z, mass,
    pre, image, sums, lines, field,
):
    lane = lane_index(p.xw)
    windows, at = [], 0
    for y in range(p.cy):
        half = y // p.yq
        windows.append((half * p.xe // 8 * 8, p.xw, y % p.yq, at))
        at += p.xw
    side = 2 * p.xe
    for h in range(2 * HALO - 1):
        windows.append((side // 8 * 8, p.xp, h, at))
        at += p.xp
    tail = side + p.cx
    for q in range(p.yq):
        windows.append((tail // 8 * 8, 8, q, at))
        at += 8
    three_z = jnp.concatenate([high_z[...], high_z[...], low_z[...]], axis=1)
    def assembled(group):
        parts = []
        for chunk in range(p.chunks):
            count = min(p.group, p.ng - chunk * p.group)
            pieces = []
            for first, rows, piece, at in group:
                here = lane[:rows]
                line = jnp.zeros((rows, LANES), jnp.float32)
                for slot in range(count):
                    part = blocks[chunk * p.group + slot, first : first + rows, :]
                    part = moved(part, (slot - piece) * p.kz)
                    line = jnp.where(between(here, slot, p.kz), part, line)
                pieces.append(line)
            parts.append(jnp.concatenate(pieces, axis=0))
        return jnp.concatenate(parts, axis=1)

    groups = [windows[p.cy :], windows[: p.yq], windows[p.yq : p.cy]]
    results = []
    for group in groups:
        high, low = split(assembled(group))
        results.append(mul_t(jnp.concatenate([high, low, high], axis=1), three_z))
    whole = jnp.concatenate([results[1], results[2], results[0]], axis=0)
    for y in range(p.cy):
        first, rows, piece, at = windows[y]
        off = (y // p.yq) * p.xe - first
        field[HALO + y, : p.xe] = whole[at + off : at + off + p.xe]
    for h in range(2 * HALO - 1):
        first, rows, piece, at = windows[p.cy + h]
        off = side - first
        y = h if h < HALO else h + p.cy
        field[y, HALO : HALO + p.cx] = whole[at + off : at + off + p.cx]
    for q in range(p.yq):
        first, rows, piece, at = windows[p.cy + 2 * HALO - 1 + q]
        off = tail - first
        field[p.cy + 2 * HALO - 1, HALO + q * p.extra : HALO + (q + 1) * p.extra] = whole[
            at + off : at + off + p.extra
        ]
    def stretch(flux_at):
        return 27.0 * (flux_at(2) - flux_at(1)) - (flux_at(3) - flux_at(0))

    rz = jnp.zeros((p.cx, LANES), jnp.float32)
    dot = jnp.zeros((p.cx, LANES), jnp.float32)
    fluxes_y = {}

    def flux_y(y):
        if y not in fluxes_y:
            val = [field[y + i, HALO : HALO + p.cx, :] for i in range(4)]
            fluxes_y[y] = faces_y[y] * stretch(lambda i: val[i])
        return fluxes_y[y]

    n = p.nz
    for y in range(p.cy):
        line = field[HALO + y]
        flux = faces_x[y, : p.cx + 3] * stretch(lambda i: line[i : i + p.cx + 3])
        term = stretch(lambda i: flux[i : i + p.cx])
        term = term + stretch(lambda i: flux_y(y + i))
        here = line[HALO : HALO + p.cx]
        grad = 27.0 * (pltpu.roll(here, n - 1, 1) - here) - (
            pltpu.roll(here, n - 2, 1) - pltpu.roll(here, 1, 1)
        )
        flux = faces_z[y] * grad
        term = term + (
            27.0 * (flux - pltpu.roll(flux, 1, 1))
            - (pltpu.roll(flux, n - 1, 1) - pltpu.roll(flux, 2, 1))
        )
        result = mass[y] * here - term * (0.5 / 576.0)
        pre[y] = here
        image[y] = result
        one = charge[y] * here
        two = result * here
        for c in range(n // LANES):
            rz = rz + one[:, c * LANES : (c + 1) * LANES]
            dot = dot + two[:, c * LANES : (c + 1) * LANES]
    rz = jnp.sum(rz, axis=0, keepdims=True)
    dot = jnp.sum(dot, axis=0, keepdims=True)
    half = LANES // 2
    rz = rz + pltpu.roll(rz, half, 1)
    dot = dot + pltpu.roll(dot, half, 1)
    both = jnp.where(lane_index(1) < half, rz, dot)
    sums[...] = jnp.broadcast_to(both[None], sums.shape)


def update_kernel(p, sums, charge, pre, image, solution_field, residual):
    half = LANES // 2
    total = jnp.sum(sums[...], axis=0)
    lane = lane_index(1)
    rz = jnp.sum(jnp.where(lane < half, total, 0.0), axis=1, keepdims=True)
    dot = jnp.sum(jnp.where(lane < half, 0.0, total), axis=1, keepdims=True)
    alpha = jnp.broadcast_to((4.0 * math.pi) * rz / dot, (p.cx, p.nz))
    for y in range(p.cy):
        solution_field[y] = alpha * pre[y]
        residual[y] = (4.0 * math.pi) * charge[y] - alpha * image[y]


def local_planes(p, density, charge):
    group = ("gx", "gl")
    along_y = ("gh", "gl")
    f32 = jnp.float32

    def shape(*dims):
        return jax.ShapeDtypeStruct(dims, f32)

    def pairs(count, first):
        low = range(first, count, 2)
        near = [(i, (i + 1) % count) for i in low]
        return near + [(target, source) for source, target in near]

    even_x = lax.axis_index("gx") % 2 == 0
    even_y = lax.axis_index("gl") % 2 == 0

    density = density.transpose(1, 0, 2)
    charge = charge.transpose(1, 0, 2)
    high_z, low_z = (jnp.asarray(part) for part in p.z_forward())
    coarse, fine = jnp.asarray(p.coarse_pack()), jnp.asarray(p.fine_pack())
    (blocks,) = call(
        lambda *refs: forward_kernel(p, *refs),
        [shape(p.ng, 2 * p.cx, LANES)],
        [charge, high_z, low_z],
        [
            pltpu.VMEM((p.cy, p.cx, p.nz), f32),
            pltpu.VMEM((p.nz, p.deep), jnp.bfloat16),
            pltpu.VMEM((p.nz, p.deep), jnp.bfloat16),
            pltpu.SemaphoreType.DMA((3,)),
        ],
        specs=[ANY_SPEC] * 3,
        limit=None,
    )
    blocks = lax.all_to_all(blocks, group, 0, 0)
    (table,) = call(
        lambda *refs: table_kernel(p, *refs), [shape(p.ny, p.kz * LANES)], [fine]
    )
    eps = permittivity(density)
    swap_by = lax.ppermute(
        jnp.where(even_y, eps[:2], eps[p.cy - 2 :]), along_y, pairs(2 * p.gl, 1)
    )
    swap_bx = lax.ppermute(
        jnp.where(even_x, eps[:, :2], eps[:, p.cx - 2 :]), "gx", pairs(p.gx, 1)
    )
    swap_ay = lax.ppermute(
        jnp.where(even_y, eps[p.cy - 2 :], eps[:2]), along_y, pairs(2 * p.gl, 0)
    )
    swap_ax = lax.ppermute(
        jnp.where(even_x, eps[:, p.cx - 2 :], eps[:, :2]), "gx", pairs(p.gx, 0)
    )
    blocks, eps, table = lax.optimization_barrier(
        (blocks, eps, table)
    )
    spectrum_half, own, sent = call(
        lambda *refs: solve_kernel(p, *refs),
        [shape(p.ny, p.kz * LANES), shape(2 * HALO * p.kz, LANES), shape(4 * p.kz, LANES)],
        [blocks, coarse, table],
        [pltpu.VMEM((p.ny * p.kz + LANES, LANES), f32), pltpu.VMEM((8 * p.kz, LANES), f32)],
    )
    sent, eps = lax.optimization_barrier((sent, eps))
    received = lax.ppermute(sent, "gh", [(0, 1), (1, 0)])
    ex_low, ex_high = jnp.where(even_x, swap_bx, swap_ax), jnp.where(even_x, swap_ax, swap_bx)
    ey_low, ey_high = jnp.where(even_y, swap_by, swap_ay), jnp.where(even_y, swap_ay, swap_by)
    brick = (p.cy, p.cx, p.nz)
    faces = call(
        lambda *refs: faces_kernel(p, *refs),
        [
            shape(p.cy, p.xp, p.nz), shape(p.cy + 3, p.cx, p.nz), shape(*brick), shape(*brick),
        ],
        [eps, ex_low, ex_high, ey_low, ey_high],
    )
    received, *faces = lax.optimization_barrier((received, *faces))
    (blocks,) = call(
        lambda *refs: return_kernel(p, *refs),
        [shape(p.ng, p.rows, LANES)],
        [
            spectrum_half, own, received, table, fine, coarse,
        ],
        [
            pltpu.VMEM((2 * HALO * p.kz, LANES), f32),
            pltpu.VMEM((p.ny * p.kz + 2 * p.edge, LANES), f32),
        ],
    )
    blocks = lax.all_to_all(blocks, group, 0, 0)
    pre, image, sums = call(
        lambda *refs: stencil_kernel(p, *refs),
        [shape(*brick), shape(*brick), shape(2 * p.ng, 1, LANES)],
        [blocks, high_z, low_z, charge, *faces],
        [
            pltpu.VMEM((p.lines, p.deep), f32),
            pltpu.VMEM((p.cy + 2 * HALO, p.xw, p.nz), f32),
        ],
    )
    sums = lax.all_to_all(sums, ("gx", "gh", "gl"), 0, 0)
    solution_field, residual = call(
        lambda *refs: update_kernel(p, *refs),
        [shape(*brick), shape(*brick)],
        [sums, charge, pre, image],
    )
    return solution_field.transpose(1, 0, 2), residual.transpose(1, 0, 2)


def solution(mesh):
    count_x, count_y = mesh.shape["gx"], mesh.shape["gy"]

    def run(density, charge):
        plan = Plan(charge.shape, count_x, count_y)
        if plan.fits():
            split_mesh = jax.sharding.Mesh(
                mesh.devices.reshape(count_x, 2, count_y // 2), ("gx", "gh", "gl")
            )
            spec = P("gx", ("gh", "gl"), None)
            body, over = (lambda *args: local_planes(plan, *args)), split_mesh
        else:
            spec = P("gx", "gy", None)
            body, over = local_lines, mesh
        return jax.shard_map(
            body, mesh=over, in_specs=(spec, spec), out_specs=(spec, spec), check_vma=False
        )(density, charge)

    return run
```

```python
import math

import jax
import jax.numpy as jnp
import ml_dtypes
import numpy as np
from jax import lax
from jax.experimental import pallas as pl
from jax.experimental.pallas import tpu as pltpu
from jax.sharding import PartitionSpec as P

EPS_SOLVENT = 78.3
RHO_UPPER = 0.005
RHO_LOWER = 0.0001
KAPPA_SCALE = 0.1
EPS_PRECOND = 20.0
SHIFT_PRECOND = 0.05
HIGHEST = lax.Precision.HIGHEST
LANES = 128
HALO = 3
VMEM_LIMIT = 48 << 20


def extended(block, sides, width):
    for axis, dim in sides:
        count = lax.axis_size(axis)
        forward = [(i, i + 1) for i in range(count - 1)]
        forward.append((count - 1, 0))
        backward = [(target, source) for source, target in forward]
        low = lax.ppermute(
            lax.slice_in_dim(block, block.shape[dim] - width, None, axis=dim), axis, forward
        )
        high = lax.ppermute(lax.slice_in_dim(block, 0, width, axis=dim), axis, backward)
        block = jnp.concatenate([low, block, high], axis=dim)
    return block


def permittivity(density):
    upper = math.log(RHO_UPPER)
    lower = math.log(RHO_LOWER)
    fraction = jnp.clip((upper - jnp.log(density)) / (upper - lower), 0.0, 1.0)
    exponent = fraction - jnp.sin(2.0 * math.pi * fraction) / (2.0 * math.pi)
    return jnp.exp(exponent * math.log(EPS_SOLVENT))


def hartley(length):
    indices = jnp.arange(length, dtype=jnp.int32)
    product = indices[:, None] * indices[None, :] % length
    angles = product.astype(jnp.float32) * (2.0 * math.pi / length)
    return jnp.cos(angles) + jnp.sin(angles)


def spectrum(wavenum, length):
    halfang = wavenum.astype(jnp.float32) * (math.pi / length)
    return ((27.0 * jnp.sin(halfang) - jnp.sin(3.0 * halfang)) / 12.0) ** 2


def cutout(values, offset, length, dimen):
    return lax.slice_in_dim(values, offset, offset + length, axis=dimen)


def padded_term(padded, faces, count, dimen):
    nfaces = count + 3
    grad = (
        27.0 * (cutout(padded, 2, nfaces, dimen) - cutout(padded, 1, nfaces, dimen))
        - (cutout(padded, 3, nfaces, dimen) - cutout(padded, 0, nfaces, dimen))
    ) / 24.0
    flux = faces * grad
    return (
        27.0 * (cutout(flux, 2, count, dimen) - cutout(flux, 1, count, dimen))
        - (cutout(flux, 3, count, dimen) - cutout(flux, 0, count, dimen))
    ) / 24.0


def rolled_term(field, faces):
    grad = (
        27.0 * (jnp.roll(field, -1, 2) - field) - (jnp.roll(field, -2, 2) - jnp.roll(field, 1, 2))
    ) / 24.0
    flux = faces * grad
    return (
        27.0 * (flux - jnp.roll(flux, 1, 2)) - (jnp.roll(flux, -1, 2) - jnp.roll(flux, 2, 2))
    ) / 24.0


def operate(field, faces_x, faces_y, faces_z, kappa):
    cellsx = field.shape[0]
    cellsy = field.shape[1]
    padded = extended(field, (("gx", 0), ("gy", 1)), 3)
    term_x = padded_term(padded[:, 3 : 3 + cellsy], faces_x, cellsx, 0)
    term_y = padded_term(padded[3 : 3 + cellsx], faces_y, cellsy, 1)
    term_z = rolled_term(field, faces_z)
    return kappa * field - (term_x + term_y + term_z)


def precondition(field):
    cellsx, cellsy, length_z = field.shape
    size_x = cellsx * lax.axis_size("gx")
    size_y = cellsy * lax.axis_size("gy")
    hart_x = hartley(size_x)
    hart_y = hartley(size_y)
    hart_z = hartley(length_z)
    scaling = float(size_x * size_y * length_z)
    forward = jnp.dot(field, hart_z, precision=HIGHEST)
    zpiece = length_z // lax.axis_size("gx")
    xpiece = size_x // lax.axis_size("gy")
    lines_x = lax.all_to_all(forward, "gx", split_axis=2, concat_axis=0, tiled=True)
    along_x = jnp.einsum("xyk,xa->yka", lines_x, hart_x, precision=HIGHEST)
    lines_y = lax.all_to_all(along_x, "gy", split_axis=2, concat_axis=0, tiled=True)
    along_y = jnp.einsum("ykb,yc->kbc", lines_y, hart_y, precision=HIGHEST)
    wave_z = lax.axis_index("gx") * zpiece + jnp.arange(zpiece, dtype=jnp.int32)
    wave_x = lax.axis_index("gy") * xpiece + jnp.arange(xpiece, dtype=jnp.int32)
    wave_y = jnp.arange(size_y, dtype=jnp.int32)
    symbol = (
        EPS_PRECOND
        * (
            spectrum(wave_z, length_z)[:, None, None]
            + spectrum(wave_x, size_x)[None, :, None]
            + spectrum(wave_y, size_y)[None, None, :]
        )
        + SHIFT_PRECOND
    )
    scaled = along_y / (symbol * scaling)
    back_y = jnp.einsum("kbc,cy->ykb", scaled, hart_y, precision=HIGHEST)
    lines_back = lax.all_to_all(back_y, "gy", split_axis=0, concat_axis=2, tiled=True)
    back_x = jnp.einsum("yka,ax->xyk", lines_back, hart_x, precision=HIGHEST)
    bricks = lax.all_to_all(back_x, "gx", split_axis=0, concat_axis=2, tiled=True)
    return jnp.dot(bricks, hart_z, precision=HIGHEST)


def residual_inner(residual, precond):
    return lax.psum(jnp.sum(residual * precond), ("gx", "gy"))


def local_lines(density, charge):
    eps = permittivity(density)
    kappa = KAPPA_SCALE * (eps - 1.0) / (EPS_SOLVENT - 1.0)
    cellsx = eps.shape[0]
    cellsy = eps.shape[1]
    eps_padded = extended(eps, (("gx", 0), ("gy", 1)), 2)
    strip_x = eps_padded[:, 2 : 2 + cellsy]
    faces_x = 0.5 * (strip_x[:-1] + strip_x[1:])
    strip_y = eps_padded[2 : 2 + cellsx]
    faces_y = 0.5 * (strip_y[:, :-1] + strip_y[:, 1:])
    faces_z = 0.5 * (eps + jnp.roll(eps, -1, 2))
    rhs = 4.0 * math.pi * charge
    residual = rhs
    precond = precondition(residual)
    inner_now = residual_inner(residual, precond)
    image = operate(precond, faces_x, faces_y, faces_z, kappa)
    alpha = inner_now / lax.psum(jnp.sum(precond * image), ("gx", "gy"))
    solution_field = alpha * precond
    residual = residual - alpha * image
    return (solution_field, residual)


def cas_table(rows, columns, length):
    angle = (np.outer(rows, columns) % length).astype(np.float64) * (2.0 * np.pi / length)
    return np.cos(angle) + np.sin(angle)


def symbol_table(length):
    halfang = np.arange(length, dtype=np.float64) * (np.pi / length)
    return ((27.0 * np.sin(halfang) - np.sin(3.0 * halfang)) / 12.0) ** 2


def halves(table):
    high = table.astype(ml_dtypes.bfloat16)
    low = (table - high.astype(np.float64)).astype(ml_dtypes.bfloat16)
    return high, low


def thirds(table):
    high, low = halves(table)
    return np.concatenate([high, low, high], axis=1)


def split(values):
    high = values.astype(jnp.bfloat16)
    low = (values - high.astype(jnp.float32)).astype(jnp.bfloat16)
    return high, low


def stacked(values, axis):
    high, low = split(values)
    return jnp.concatenate([high, high, low], axis=axis)


def mul(left, right):
    return jnp.dot(left, right, preferred_element_type=jnp.float32)


def mul_t(left, right):
    return lax.dot_general(
        left, right, (((1,), (1,)), ((), ())), preferred_element_type=jnp.float32
    )


def padded_rows(values, rows):
    if values.shape[0] == rows:
        return values
    gap = jnp.zeros((rows - values.shape[0],) + values.shape[1:], values.dtype)
    return jnp.concatenate([values, gap], axis=0)


def up(size, step):
    return -(-size // step) * step


STENCIL = tuple(EPS_PRECOND * c / 576.0 for c in (-783.0, 54.0, -1.0))


class Plan:
    def __init__(self, shape, count_x, count_y):
        size_x, size_y, self.nz = shape
        self.gx, self.gl = count_x, count_y // 2
        self.nx, self.ny = size_x, size_y // 2
        self.cx, self.cy = size_x // count_x, size_y // count_y
        self.ng = self.gx * self.gl
        self.even = count_y % 2 == 0 and self.cy % 2 == 0 and self.ng > 0
        self.kz = self.nz // max(self.ng, 1)
        self.yq = self.cy // 2
        self.xp = up(self.cx, 8)
        self.xe = self.cx + 2 * HALO
        self.xw = up(self.xe, 8)
        self.yp = up(self.ny, 16)
        self.step = self.yq * self.kz
        self.edge = HALO * self.kz
        self.group = LANES // max(self.kz, 1)
        self.chunks = -(-self.ng // self.group)
        self.deep = self.chunks * LANES
        self.third = self.kz // HALO
        self.rows = up(2 * self.xe + self.cx, 8)
        self.mirror = self.nx // 2 + 1

    def fits(self):
        return (
            self.even
            and self.gx % 2 == 0
            and self.gl % 2 == 0
            and self.nz % (self.ng * 8) == 0
            and self.nz % LANES == 0
            and self.yq == 2 * HALO - 1
            and self.kz % (8 * HALO) == 0
            and self.step + self.third <= LANES
            and self.step <= LANES
            and self.step % 8 == 0
            and self.nx <= LANES
            and 2 * (LANES - self.nx) >= self.nx
            and 3 * self.mirror <= LANES
            and self.ny % 8 == 0
            and self.nx % 16 == 0
            and self.ny >= 2 * HALO
            and self.gx * self.xw <= LANES
        )

    def z_forward(self):
        wave = np.arange(self.nz)
        owner = wave // self.kz
        place = owner // self.group * LANES + owner % self.group * self.kz + wave % self.kz
        table = np.zeros((self.nz, self.deep))
        table[:, place] = cas_table(wave, wave, self.nz)
        return halves(table)

    def x_waves(self):
        return np.concatenate([np.arange(self.mirror), np.arange(self.nx - 1, self.mirror - 1, -1)])

    def x_forward(self):
        table = np.zeros((LANES, self.nx))
        table[: self.nx] = cas_table(self.x_waves(), np.arange(self.nx), self.nx)
        return thirds(table)

    def y_both(self):
        table = np.zeros((self.ny, self.yp))
        table[:, : self.ny] = cas_table(np.arange(self.ny), np.arange(self.ny), self.ny)
        return thirds(table)

    def ends(self):
        low = np.arange(HALO)
        return np.concatenate([low, self.ny - 1 - low])

    def y_ends(self):
        table = np.zeros((8, self.yp))
        table[: 2 * HALO, : self.ny] = cas_table(self.ends(), np.arange(self.ny), self.ny)
        return thirds(table)

    def y_sources(self):
        columns = cas_table(np.arange(self.ny), self.ends(), self.ny).T
        wide = np.broadcast_to(columns[:, :, None], (2 * HALO, self.ny, LANES))
        return np.ascontiguousarray(wide).astype(np.float32)

    def x_backward(self):
        wide = np.zeros((self.gx * self.xw, LANES))
        own = np.zeros((self.gx * self.xp, LANES))
        waves = self.x_waves()
        for g in range(self.gx):
            x = (g * self.cx - HALO + np.arange(self.xe)) % self.nx
            wide[g * self.xw : g * self.xw + self.xe, : self.nx] = cas_table(x, waves, self.nx)
            x = g * self.cx + np.arange(self.cx)
            own[g * self.xp : g * self.xp + self.cx, : self.nx] = cas_table(x, waves, self.nx)
        scale = 4.0 * np.pi / (self.nx * self.nz)
        return thirds(np.concatenate([wide, own], axis=0) * scale)

    def plane(self):
        plane = np.full((self.ny, LANES), 1e30)
        lam_x = symbol_table(self.nx)[self.x_waves()]
        plane[:, : self.nx] = lam_x[None, :] + symbol_table(self.ny)[:, None]
        return plane.astype(np.float32)

    def coarse_pack(self):
        parts = [self.x_forward(), self.y_both(), self.y_ends(), self.x_backward()]
        width = max(part.shape[1] for part in parts)
        self.places, rows = [], 0
        for part in parts:
            self.places.append((rows, part.shape))
            rows = up(rows + part.shape[0], 16)
        table = np.zeros((rows, width), ml_dtypes.bfloat16)
        for (row, shape), part in zip(self.places, parts):
            table[row : row + shape[0], : shape[1]] = part
        return table

    def fine_pack(self):
        parts = [self.plane(), self.y_sources(), self.joins()]
        return np.concatenate([part.reshape(-1, LANES) for part in parts], axis=0)

    def coarse(self, ref, which):
        row, shape = self.places[which]
        return ref[row : row + shape[0], : shape[1]]

    def join_rows(self, ref, row):
        me = lax.axis_index("gx") * self.gl + lax.axis_index("gl")
        size = (2 * HALO + 1) * self.kz
        start = (2 * HALO + 1) * self.ny + me * size + row * self.kz
        return ref[pl.ds(pl.multiple_of(start, 8), self.kz), :]

    def joins(self):
        lam_x = symbol_table(self.nx)[: self.mirror]
        lam_y, lam_z = symbol_table(self.ny), symbol_table(self.nz)
        total = EPS_PRECOND * (lam_z[:, None, None] + lam_x[None, :, None] + lam_y) + SHIFT_PRECOND
        green = np.real(np.fft.ifft(1.0 / total, axis=-1))
        i = np.arange(HALO)
        near = green[..., np.abs(i[:, None] - i[None, :])]
        far = green[..., i[:, None] + i[None, :] + 1]
        band = np.zeros((HALO, HALO))
        for row in range(HALO):
            for column in range(HALO - row):
                band[row, column] = STENCIL[row + column]
        eye = np.eye(HALO)
        even = np.linalg.inv(eye - 2.0 * (near + far) @ band)
        odd = np.linalg.inv(eye + 2.0 * (near - far) @ band)
        both = np.stack([even, odd], axis=2).reshape(self.ng, self.kz, self.mirror, 2 * HALO, HALO)
        both = both.transpose(0, 3, 1, 4, 2).reshape(self.ng, 2 * HALO, self.kz, HALO * self.mirror)
        table = np.zeros((self.ng, 2 * HALO + 1, self.kz, LANES), np.float32)
        table[:, : 2 * HALO, :, : HALO * self.mirror] = both
        table[:, 2 * HALO] = lam_z.reshape(self.ng, self.kz, 1)
        return table


VMEM_SPEC = pl.BlockSpec(memory_space=pltpu.VMEM)
ANY_SPEC = pl.BlockSpec(memory_space=pl.ANY)


def call(kernel, outs, args, scratch=(), specs=None, limit=VMEM_LIMIT):
    nbytes = sum(int(np.prod(a.shape)) * a.dtype.itemsize for a in (*args, *outs))
    return pl.pallas_call(
        kernel,
        out_shape=tuple(outs),
        in_specs=specs or [VMEM_SPEC] * len(args),
        out_specs=tuple([VMEM_SPEC] * len(outs)),
        scratch_shapes=list(scratch),
        compiler_params=pltpu.CompilerParams(vmem_limit_bytes=limit),
        cost_estimate=pl.CostEstimate(flops=0, bytes_accessed=nbytes, transcendentals=0),
    )(*args)


def lane_index(rows):
    return lax.broadcasted_iota(jnp.int32, (rows, LANES), 1)


def moved(values, shift):
    shift = shift % LANES
    return values if shift == 0 else pltpu.roll(values, shift, 1)


def within(lane, first, count):
    return (lane >= first) & (lane < first + count)


def between(lane, slot, width):
    return within(lane, slot * width, width)


def fetched(pairs, sems):
    copies = [
        pltpu.make_async_copy(source, target, sems.at[i])
        for i, (source, target) in enumerate(pairs)
    ]
    for copy in copies:
        copy.start()
    return copies


def forward_kernel(p, charge_in, high_in, low_in, out, charge, high_z, low_z, sems):
    copies = fetched(((charge_in, charge), (high_in, high_z), (low_in, low_z)), sems)
    copies[0].wait()
    lane = lane_index(p.xp)
    ready = False
    for part in range(2):
        ys = range(part * p.yq, (part + 1) * p.yq)
        high, low = split(jnp.concatenate([padded_rows(charge[y], p.xp) for y in ys], axis=0))
        if not ready:
            copies[1].wait()
        spec = mul(high, high_z[...]) + mul(low, high_z[...])
        if not ready:
            copies[2].wait()
            ready = True
        spec = spec + mul(high, low_z[...])
        for target in range(p.ng):
            chunk, slot = divmod(target, p.group)
            block = jnp.zeros((p.xp, LANES), jnp.float32)
            for i in range(p.yq):
                piece = spec[i * p.xp : (i + 1) * p.xp, chunk * LANES : (chunk + 1) * LANES]
                block = jnp.where(between(lane, i, p.kz), moved(piece, (i - slot) * p.kz), block)
            out[target, part * p.cx : (part + 1) * p.cx] = block[: p.cx]


def table_kernel(p, fine, out):
    plane = fine[: p.ny, :]
    waves = p.join_rows(fine, 2 * HALO)
    for k in range(p.kz):
        symbol = EPS_PRECOND * (plane + waves[k : k + 1]) + SHIFT_PRECOND
        out[:, k * LANES : (k + 1) * LANES] = 1.0 / (float(p.ny) * symbol)


def lanes_of(values, k):
    return values[:, k * LANES : (k + 1) * LANES]


def solve_kernel(p, blocks, coarse, table, spectrum_out, own, sent, turned, ends):
    x_fwd, y_both, y_ends = (p.coarse(coarse, i) for i in range(3))
    columns = []
    for gl in range(p.gl):
        for part in range(2):
            pieces = [
                blocks[gx * p.gl + gl, part * p.cx : (part + 1) * p.cx] for gx in range(p.gx)
            ]
            columns.append(jnp.concatenate(pieces, axis=0))
    along_x = mul(x_fwd, stacked(jnp.concatenate(columns, axis=1), 0))
    for b in range(2 * p.gl):
        turned[pl.ds(b * p.step, LANES), :] = lanes_of(along_x, b).T
    field = jnp.concatenate(
        [turned[pl.ds(k, p.ny, stride=p.kz), :] for k in range(p.kz)], axis=1
    )
    along_y = mul(y_both, stacked(padded_rows(field, p.yp), 0))
    solved = along_y * table[...]
    spectrum_out[...] = solved
    at_ends = mul(y_ends, stacked(padded_rows(solved, p.yp), 0))
    for k in range(p.kz):
        ends[pl.ds(k, 8, stride=p.kz), :] = lanes_of(at_ends, k)
    own[...] = ends[pl.ds(0, 2 * HALO * p.kz), :]
    piece = [ends[pl.ds(j * p.kz, p.kz), :] for j in range(2 * HALO)]
    lane = lane_index(p.kz)
    free = LANES - p.nx
    for i in range(4):
        spare = moved(piece[4 + i // 2], p.nx if i % 2 == 0 else p.nx - free)
        sent[pl.ds(i * p.kz, p.kz), :] = jnp.where(lane < p.nx, piece[i], spare)


def return_kernel(
    p, spectrum_in, own, received, table, fine, coarse,
    out, sources, planes,
):
    y_both, x_bwd = p.coarse(coarse, 1), p.coarse(coarse, 3)
    y_sources = [fine[(j + 1) * p.ny : (j + 2) * p.ny, :] for j in range(2 * HALO)]
    lane = lane_index(p.kz)
    free = LANES - p.nx
    part = [received[pl.ds(i * p.kz, p.kz), :] for i in range(4)]
    other = [jnp.where(lane < p.nx, value, 0.0) for value in part]
    for i in range(2):
        first = moved(part[2 * i], -p.nx)
        second = moved(part[2 * i + 1], free - p.nx)
        other.append(jnp.where(lane < free, first, jnp.where(lane < p.nx, second, 0.0)))
    mine = [own[pl.ds(j * p.kz, p.kz), :] for j in range(2 * HALO)]
    jump = [mine[j] - other[j] for j in range(2 * HALO)]
    even = [jump[j] + jump[HALO + j] for j in range(HALO)]
    odd = [jump[j] - jump[HALO + j] for j in range(HALO)]

    def mixed(base, vector):
        results = []
        for i in range(HALO):
            packed = p.join_rows(fine, base + i)
            total = 0.0
            for j in range(HALO):
                first = moved(packed, -j * p.mirror)
                second = moved(packed, p.mirror - 1 - j * p.mirror)
                total = total + jnp.where(lane < p.mirror, first, second) * vector[j]
            results.append(total)
        return results

    even_full, odd_full = mixed(0, even), mixed(HALO, odd)
    low_full = [0.5 * (e + o) for e, o in zip(even_full, odd_full)]
    high_full = [0.5 * (e - o) for e, o in zip(even_full, odd_full)]
    far_low = [other[j] - 0.5 * (low_full[j] - jump[j]) for j in range(HALO)]
    far_high = [other[HALO + j] - 0.5 * (high_full[j] - jump[HALO + j]) for j in range(HALO)]
    for i in range(HALO):
        sources[pl.ds(i * p.kz, p.kz), :] = sum(
            STENCIL[i + j] * high_full[j] for j in range(HALO - i)
        )
        sources[pl.ds((HALO + i) * p.kz, p.kz), :] = sum(
            STENCIL[i + j] * low_full[j] for j in range(HALO - i)
        )
    whole = []
    for k in range(p.kz):
        added = sum(y_sources[j] * sources[pl.ds(j * p.kz + k, 1), :] for j in range(2 * HALO))
        whole.append(
            spectrum_in[:, k * LANES : (k + 1) * LANES]
            + added * table[:, k * LANES : (k + 1) * LANES]
        )
    back_y = mul(y_both, stacked(padded_rows(jnp.concatenate(whole, axis=1), p.yp), 0))
    base = p.edge
    for k in range(p.kz):
        planes[pl.ds(base + k, p.ny, stride=p.kz), :] = lanes_of(back_y, k)
    after = base + p.ny * p.kz
    for i in range(HALO):
        planes[pl.ds(base - (i + 1) * p.kz, p.kz), :] = far_high[i]
        planes[pl.ds(after + i * p.kz, p.kz), :] = far_low[i]
    cut = p.gx * p.xw
    wide_rows = x_bwd[:cut, :]
    own_rows = x_bwd[cut:, :]
    rest = p.rows - 2 * p.xe - p.cx

    def filled(pieces, part):
        first = base + (gl + 1) * 2 * p.step + p.edge - p.kz + part * p.third
        pieces = [planes[pl.ds(at, count), :] for at, count in (*pieces, (first, p.third))]
        return padded_rows(jnp.concatenate(pieces, axis=0), LANES)

    for gl in range(p.gl):
        start = base + gl * 2 * p.step
        end = start + 2 * p.step
        both = [filled([(start + i * p.step, p.step)], i) for i in range(2)]
        wide = mul_t(wide_rows, stacked(jnp.concatenate(both, axis=0), 1))
        sides = filled([(start - p.edge, p.edge), (end, p.edge - p.kz)], 2)
        side = mul_t(own_rows, stacked(sides, 1))
        for gx in range(p.gx):
            target = gx * p.gl + gl
            for half in range(2):
                out[target, half * p.xe : (half + 1) * p.xe] = wide[
                    gx * p.xw : gx * p.xw + p.xe, half * LANES : (half + 1) * LANES
                ]
            at, line = 2 * p.xe, gx * p.xp
            out[target, at : at + p.cx] = side[line : line + p.cx]
            if rest:
                out[target, at + p.cx :] = jnp.zeros((rest, LANES), jnp.float32)


def faces_kernel(p, eps, ex_low, ex_high, ey_low, ey_high, faces_x, faces_y, faces_z, mass):
    for y in range(p.cy):
        here = eps[y]
        line = jnp.concatenate([ex_low[y], here, ex_high[y]], axis=0)
        faces_x[y, : p.cx + 3] = line[: p.cx + 3] + line[1 : p.cx + 4]
        faces_z[y] = here + pltpu.roll(here, p.nz - 1, 1)
        mass[y] = (KAPPA_SCALE / (EPS_SOLVENT - 1.0)) * (here - 1.0)
    planes = [ey_low[0], ey_low[1], *[eps[y] for y in range(p.cy)], ey_high[0], ey_high[1]]
    for y in range(p.cy + 3):
        faces_y[y] = planes[y] + planes[y + 1]


def stencil_kernel(
    p, blocks, high_z, low_z, charge, faces_x, faces_y, faces_z, mass,
    pre, image, sums, field,
):
    lane = lane_index(p.xw)
    side = 2 * p.xe

    def line_of(chunk, first, rows, source_lane, skip, count):
        here = lane[:rows]
        line = jnp.zeros((rows, LANES), jnp.float32)
        for slot in range(min(p.group, p.ng - chunk * p.group)):
            part = blocks[chunk * p.group + slot, first : first + rows, :]
            at = slot * p.kz + skip
            line = jnp.where(within(here, at, count), moved(part, at - source_lane), line)
        return line

    def plain(first, rows, piece):
        return rows, lambda chunk: line_of(chunk, first, rows, piece * p.kz, 0, p.kz)

    def last_layer(chunk):
        total = 0.0
        for part, row in enumerate((HALO, p.xe + HALO, side)):
            first = max(0, row - HALO) // 8 * 8 if part < 2 else row // 8 * 8
            rows = p.xw if part < 2 else p.xp
            line = line_of(chunk, first, rows, p.step, part * p.third, p.third)
            total = total + line[row - first : row - first + p.cx]
        return padded_rows(total, p.xp)

    windows = [plain(y // p.yq * p.xe // 8 * 8, p.xw, y % p.yq) for y in range(p.cy)]
    windows += [plain(side // 8 * 8, p.xp, h) for h in range(2 * HALO - 1)]
    windows.append((p.xp, last_layer))
    three_z = jnp.concatenate([high_z[...], high_z[...], low_z[...]], axis=1)

    def assembled(group):
        parts = []
        for chunk in range(p.chunks):
            parts.append(jnp.concatenate([make(chunk) for rows, make in group], axis=0))
        return jnp.concatenate(parts, axis=1)

    groups = [windows[p.cy :], windows[: p.yq], windows[p.yq : p.cy]]
    results = []
    for group in groups:
        high, low = split(assembled(group))
        results.append(mul_t(jnp.concatenate([high, low, high], axis=1), three_z))
    whole = jnp.concatenate([results[1], results[2], results[0]], axis=0)
    starts = np.cumsum([0] + [rows for rows, make in windows])
    for y in range(p.cy):
        at = int(starts[y]) + y // p.yq * p.xe % 8
        field[HALO + y, : p.xe] = whole[at : at + p.xe]
    for h in range(2 * HALO):
        at = int(starts[p.cy + h]) + (side % 8 if h < 2 * HALO - 1 else 0)
        y = h if h < HALO else h + p.cy
        field[y, HALO : HALO + p.cx] = whole[at : at + p.cx]

    def stretch(flux_at):
        return 27.0 * (flux_at(2) - flux_at(1)) - (flux_at(3) - flux_at(0))

    rz = jnp.zeros((p.cx, LANES), jnp.float32)
    dot = jnp.zeros((p.cx, LANES), jnp.float32)
    fluxes_y = {}

    def flux_y(y):
        if y not in fluxes_y:
            val = [field[y + i, HALO : HALO + p.cx, :] for i in range(4)]
            fluxes_y[y] = faces_y[y] * stretch(lambda i: val[i])
        return fluxes_y[y]

    n = p.nz
    for y in range(p.cy):
        line = field[HALO + y]
        flux = faces_x[y, : p.cx + 3] * stretch(lambda i: line[i : i + p.cx + 3])
        term = stretch(lambda i: flux[i : i + p.cx])
        term = term + stretch(lambda i: flux_y(y + i))
        here = line[HALO : HALO + p.cx]
        grad = 27.0 * (pltpu.roll(here, n - 1, 1) - here) - (
            pltpu.roll(here, n - 2, 1) - pltpu.roll(here, 1, 1)
        )
        flux = faces_z[y] * grad
        term = term + (
            27.0 * (flux - pltpu.roll(flux, 1, 1))
            - (pltpu.roll(flux, n - 1, 1) - pltpu.roll(flux, 2, 1))
        )
        result = mass[y] * here - term * (0.5 / 576.0)
        pre[y] = here
        image[y] = result
        one = charge[y] * here
        two = result * here
        for c in range(n // LANES):
            rz = rz + one[:, c * LANES : (c + 1) * LANES]
            dot = dot + two[:, c * LANES : (c + 1) * LANES]
    rz = jnp.sum(rz, axis=0, keepdims=True)
    dot = jnp.sum(dot, axis=0, keepdims=True)
    half = LANES // 2
    rz = rz + pltpu.roll(rz, half, 1)
    dot = dot + pltpu.roll(dot, half, 1)
    both = jnp.where(lane_index(1) < half, rz, dot)
    sums[...] = jnp.broadcast_to(both[None], sums.shape)


def update_kernel(p, sums, charge, pre, image, solution_field, residual):
    half = LANES // 2
    total = jnp.sum(sums[...], axis=0)
    lane = lane_index(1)
    rz = jnp.sum(jnp.where(lane < half, total, 0.0), axis=1, keepdims=True)
    dot = jnp.sum(jnp.where(lane < half, 0.0, total), axis=1, keepdims=True)
    alpha = jnp.broadcast_to((4.0 * math.pi) * rz / dot, (p.cx, p.nz))
    for y in range(p.cy):
        solution_field[y] = alpha * pre[y]
        residual[y] = (4.0 * math.pi) * charge[y] - alpha * image[y]


def local_planes(p, density, charge):
    group = ("gx", "gl")
    along_y = ("gh", "gl")
    f32 = jnp.float32

    def shape(*dims):
        return jax.ShapeDtypeStruct(dims, f32)

    def pairs(count, first):
        low = range(first, count, 2)
        near = [(i, (i + 1) % count) for i in low]
        return near + [(target, source) for source, target in near]

    even_x = lax.axis_index("gx") % 2 == 0
    even_y = lax.axis_index("gl") % 2 == 0

    density = density.transpose(1, 0, 2)
    charge = charge.transpose(1, 0, 2)
    high_z, low_z = (jnp.asarray(part) for part in p.z_forward())
    coarse, fine = jnp.asarray(p.coarse_pack()), jnp.asarray(p.fine_pack())
    (blocks,) = call(
        lambda *refs: forward_kernel(p, *refs),
        [shape(p.ng, 2 * p.cx, LANES)],
        [charge, high_z, low_z],
        [
            pltpu.VMEM((p.cy, p.cx, p.nz), f32),
            pltpu.VMEM((p.nz, p.deep), jnp.bfloat16),
            pltpu.VMEM((p.nz, p.deep), jnp.bfloat16),
            pltpu.SemaphoreType.DMA((3,)),
        ],
        specs=[ANY_SPEC] * 3,
        limit=None,
    )
    blocks = lax.all_to_all(blocks, group, 0, 0)
    (table,) = call(
        lambda *refs: table_kernel(p, *refs), [shape(p.ny, p.kz * LANES)], [fine]
    )
    eps = permittivity(density)
    swap_by = lax.ppermute(
        jnp.where(even_y, eps[:2], eps[p.cy - 2 :]), along_y, pairs(2 * p.gl, 1)
    )
    swap_bx = lax.ppermute(
        jnp.where(even_x, eps[:, :2], eps[:, p.cx - 2 :]), "gx", pairs(p.gx, 1)
    )
    swap_ay = lax.ppermute(
        jnp.where(even_y, eps[p.cy - 2 :], eps[:2]), along_y, pairs(2 * p.gl, 0)
    )
    swap_ax = lax.ppermute(
        jnp.where(even_x, eps[:, p.cx - 2 :], eps[:, :2]), "gx", pairs(p.gx, 0)
    )
    blocks, eps, table = lax.optimization_barrier(
        (blocks, eps, table)
    )
    spectrum_half, own, sent = call(
        lambda *refs: solve_kernel(p, *refs),
        [shape(p.ny, p.kz * LANES), shape(2 * HALO * p.kz, LANES), shape(4 * p.kz, LANES)],
        [blocks, coarse, table],
        [pltpu.VMEM((p.ny * p.kz + LANES, LANES), f32), pltpu.VMEM((8 * p.kz, LANES), f32)],
    )
    sent, eps = lax.optimization_barrier((sent, eps))
    received = lax.ppermute(sent, "gh", [(0, 1), (1, 0)])
    ex_low, ex_high = jnp.where(even_x, swap_bx, swap_ax), jnp.where(even_x, swap_ax, swap_bx)
    ey_low, ey_high = jnp.where(even_y, swap_by, swap_ay), jnp.where(even_y, swap_ay, swap_by)
    brick = (p.cy, p.cx, p.nz)
    faces = call(
        lambda *refs: faces_kernel(p, *refs),
        [
            shape(p.cy, p.xp, p.nz), shape(p.cy + 3, p.cx, p.nz), shape(*brick), shape(*brick),
        ],
        [eps, ex_low, ex_high, ey_low, ey_high],
    )
    received, *faces = lax.optimization_barrier((received, *faces))
    (blocks,) = call(
        lambda *refs: return_kernel(p, *refs),
        [shape(p.ng, p.rows, LANES)],
        [
            spectrum_half, own, received, table, fine, coarse,
        ],
        [
            pltpu.VMEM((2 * HALO * p.kz, LANES), f32),
            pltpu.VMEM((p.ny * p.kz + 2 * p.edge, LANES), f32),
        ],
    )
    blocks = lax.all_to_all(blocks, group, 0, 0)
    pre, image, sums = call(
        lambda *refs: stencil_kernel(p, *refs),
        [shape(*brick), shape(*brick), shape(2 * p.ng, 1, LANES)],
        [blocks, high_z, low_z, charge, *faces],
        [
            pltpu.VMEM((p.cy + 2 * HALO, p.xw, p.nz), f32),
        ],
    )
    sums = lax.all_to_all(sums, ("gx", "gh", "gl"), 0, 0)
    solution_field, residual = call(
        lambda *refs: update_kernel(p, *refs),
        [shape(*brick), shape(*brick)],
        [sums, charge, pre, image],
    )
    return solution_field.transpose(1, 0, 2), residual.transpose(1, 0, 2)


def solution(mesh):
    count_x, count_y = mesh.shape["gx"], mesh.shape["gy"]

    def run(density, charge):
        plan = Plan(charge.shape, count_x, count_y)
        if plan.fits():
            split_mesh = jax.sharding.Mesh(
                mesh.devices.reshape(count_x, 2, count_y // 2), ("gx", "gh", "gl")
            )
            spec = P("gx", ("gh", "gl"), None)
            body, over = (lambda *args: local_planes(plan, *args)), split_mesh
        else:
            spec = P("gx", "gy", None)
            body, over = local_lines, mesh
        return jax.shard_map(
            body, mesh=over, in_specs=(spec, spec), out_specs=(spec, spec), check_vma=False
        )(density, charge)

    return run
```

```python
import math

import jax
import jax.numpy as jnp
import ml_dtypes
import numpy as np
from jax import lax
from jax.experimental import pallas as pl
from jax.experimental.pallas import tpu as pltpu
from jax.sharding import PartitionSpec as P

EPS_SOLVENT = 78.3
RHO_UPPER = 0.005
RHO_LOWER = 0.0001
KAPPA_SCALE = 0.1
EPS_PRECOND = 20.0
SHIFT_PRECOND = 0.05
HIGHEST = lax.Precision.HIGHEST
LANES = 128
HALO = 3
VMEM_LIMIT = 48 << 20


def extended(block, sides, width):
    for axis, dim in sides:
        count = lax.axis_size(axis)
        forward = [(i, i + 1) for i in range(count - 1)]
        forward.append((count - 1, 0))
        backward = [(target, source) for source, target in forward]
        low = lax.ppermute(
            lax.slice_in_dim(block, block.shape[dim] - width, None, axis=dim), axis, forward
        )
        high = lax.ppermute(lax.slice_in_dim(block, 0, width, axis=dim), axis, backward)
        block = jnp.concatenate([low, block, high], axis=dim)
    return block


def permittivity(density):
    upper = math.log(RHO_UPPER)
    lower = math.log(RHO_LOWER)
    fraction = jnp.clip((upper - jnp.log(density)) / (upper - lower), 0.0, 1.0)
    exponent = fraction - jnp.sin(2.0 * math.pi * fraction) / (2.0 * math.pi)
    return jnp.exp(exponent * math.log(EPS_SOLVENT))


def hartley(length):
    indices = jnp.arange(length, dtype=jnp.int32)
    product = indices[:, None] * indices[None, :] % length
    angles = product.astype(jnp.float32) * (2.0 * math.pi / length)
    return jnp.cos(angles) + jnp.sin(angles)


def spectrum(wavenum, length):
    halfang = wavenum.astype(jnp.float32) * (math.pi / length)
    return ((27.0 * jnp.sin(halfang) - jnp.sin(3.0 * halfang)) / 12.0) ** 2


def cutout(values, offset, length, dimen):
    return lax.slice_in_dim(values, offset, offset + length, axis=dimen)


def padded_term(padded, faces, count, dimen):
    nfaces = count + 3
    grad = (
        27.0 * (cutout(padded, 2, nfaces, dimen) - cutout(padded, 1, nfaces, dimen))
        - (cutout(padded, 3, nfaces, dimen) - cutout(padded, 0, nfaces, dimen))
    ) / 24.0
    flux = faces * grad
    return (
        27.0 * (cutout(flux, 2, count, dimen) - cutout(flux, 1, count, dimen))
        - (cutout(flux, 3, count, dimen) - cutout(flux, 0, count, dimen))
    ) / 24.0


def rolled_term(field, faces):
    grad = (
        27.0 * (jnp.roll(field, -1, 2) - field) - (jnp.roll(field, -2, 2) - jnp.roll(field, 1, 2))
    ) / 24.0
    flux = faces * grad
    return (
        27.0 * (flux - jnp.roll(flux, 1, 2)) - (jnp.roll(flux, -1, 2) - jnp.roll(flux, 2, 2))
    ) / 24.0


def operate(field, faces_x, faces_y, faces_z, kappa):
    cellsx = field.shape[0]
    cellsy = field.shape[1]
    padded = extended(field, (("gx", 0), ("gy", 1)), 3)
    term_x = padded_term(padded[:, 3 : 3 + cellsy], faces_x, cellsx, 0)
    term_y = padded_term(padded[3 : 3 + cellsx], faces_y, cellsy, 1)
    term_z = rolled_term(field, faces_z)
    return kappa * field - (term_x + term_y + term_z)


def precondition(field):
    cellsx, cellsy, length_z = field.shape
    size_x = cellsx * lax.axis_size("gx")
    size_y = cellsy * lax.axis_size("gy")
    hart_x = hartley(size_x)
    hart_y = hartley(size_y)
    hart_z = hartley(length_z)
    scaling = float(size_x * size_y * length_z)
    forward = jnp.dot(field, hart_z, precision=HIGHEST)
    zpiece = length_z // lax.axis_size("gx")
    xpiece = size_x // lax.axis_size("gy")
    lines_x = lax.all_to_all(forward, "gx", split_axis=2, concat_axis=0, tiled=True)
    along_x = jnp.einsum("xyk,xa->yka", lines_x, hart_x, precision=HIGHEST)
    lines_y = lax.all_to_all(along_x, "gy", split_axis=2, concat_axis=0, tiled=True)
    along_y = jnp.einsum("ykb,yc->kbc", lines_y, hart_y, precision=HIGHEST)
    wave_z = lax.axis_index("gx") * zpiece + jnp.arange(zpiece, dtype=jnp.int32)
    wave_x = lax.axis_index("gy") * xpiece + jnp.arange(xpiece, dtype=jnp.int32)
    wave_y = jnp.arange(size_y, dtype=jnp.int32)
    symbol = (
        EPS_PRECOND
        * (
            spectrum(wave_z, length_z)[:, None, None]
            + spectrum(wave_x, size_x)[None, :, None]
            + spectrum(wave_y, size_y)[None, None, :]
        )
        + SHIFT_PRECOND
    )
    scaled = along_y / (symbol * scaling)
    back_y = jnp.einsum("kbc,cy->ykb", scaled, hart_y, precision=HIGHEST)
    lines_back = lax.all_to_all(back_y, "gy", split_axis=0, concat_axis=2, tiled=True)
    back_x = jnp.einsum("yka,ax->xyk", lines_back, hart_x, precision=HIGHEST)
    bricks = lax.all_to_all(back_x, "gx", split_axis=0, concat_axis=2, tiled=True)
    return jnp.dot(bricks, hart_z, precision=HIGHEST)


def residual_inner(residual, precond):
    return lax.psum(jnp.sum(residual * precond), ("gx", "gy"))


def local_lines(density, charge):
    eps = permittivity(density)
    kappa = KAPPA_SCALE * (eps - 1.0) / (EPS_SOLVENT - 1.0)
    cellsx = eps.shape[0]
    cellsy = eps.shape[1]
    eps_padded = extended(eps, (("gx", 0), ("gy", 1)), 2)
    strip_x = eps_padded[:, 2 : 2 + cellsy]
    faces_x = 0.5 * (strip_x[:-1] + strip_x[1:])
    strip_y = eps_padded[2 : 2 + cellsx]
    faces_y = 0.5 * (strip_y[:, :-1] + strip_y[:, 1:])
    faces_z = 0.5 * (eps + jnp.roll(eps, -1, 2))
    rhs = 4.0 * math.pi * charge
    residual = rhs
    precond = precondition(residual)
    inner_now = residual_inner(residual, precond)
    image = operate(precond, faces_x, faces_y, faces_z, kappa)
    alpha = inner_now / lax.psum(jnp.sum(precond * image), ("gx", "gy"))
    solution_field = alpha * precond
    residual = residual - alpha * image
    return (solution_field, residual)


def cas_table(rows, columns, length):
    angle = (np.outer(rows, columns) % length).astype(np.float64) * (2.0 * np.pi / length)
    return np.cos(angle) + np.sin(angle)


def symbol_table(length):
    halfang = np.arange(length, dtype=np.float64) * (np.pi / length)
    return ((27.0 * np.sin(halfang) - np.sin(3.0 * halfang)) / 12.0) ** 2


def halves(table):
    high = table.astype(ml_dtypes.bfloat16)
    low = (table - high.astype(np.float64)).astype(ml_dtypes.bfloat16)
    return high, low


def thirds(table):
    high, low = halves(table)
    return np.concatenate([high, low, high], axis=1)


def three(table):
    parts, rest = [], np.asarray(table, np.float64)
    for _ in range(3):
        parts.append(rest.astype(ml_dtypes.bfloat16))
        rest = rest - parts[-1].astype(np.float64)
    return parts


def sixths(table):
    one, two, last = three(table)
    return np.concatenate([one, one, one, two, two, last], axis=1)


def spread(values, axis):
    parts, rest = [], values
    for _ in range(3):
        parts.append(rest.astype(jnp.bfloat16))
        rest = rest - parts[-1].astype(jnp.float32)
    one, two, last = parts
    return jnp.concatenate([one, two, last, one, two, one], axis=axis)


def split(values):
    high = values.astype(jnp.bfloat16)
    low = (values - high.astype(jnp.float32)).astype(jnp.bfloat16)
    return high, low


def stacked(values, axis):
    high, low = split(values)
    return jnp.concatenate([high, high, low], axis=axis)


def mul(left, right):
    return jnp.dot(left, right, preferred_element_type=jnp.float32)


def mul_t(left, right):
    return lax.dot_general(
        left, right, (((1,), (1,)), ((), ())), preferred_element_type=jnp.float32
    )


def padded_rows(values, rows):
    if values.shape[0] == rows:
        return values
    gap = jnp.zeros((rows - values.shape[0],) + values.shape[1:], values.dtype)
    return jnp.concatenate([values, gap], axis=0)


def up(size, step):
    return -(-size // step) * step


STENCIL = tuple(EPS_PRECOND * c / 576.0 for c in (-783.0, 54.0, -1.0))


class Plan:
    def __init__(self, shape, count_x, count_y):
        size_x, size_y, self.nz = shape
        self.gx, self.gl = count_x, count_y // 2
        self.nx, self.ny = size_x, size_y // 2
        self.cx, self.cy = size_x // count_x, size_y // count_y
        self.ng = self.gx * self.gl
        self.even = count_y % 2 == 0 and self.cy % 2 == 0 and self.ng > 0
        self.kz = self.nz // max(self.ng, 1)
        self.yq = self.cy // 2
        self.xp = up(self.cx, 8)
        self.xe = self.cx + 2 * HALO
        self.xw = up(self.xe, 8)
        self.yp = up(self.ny, 16)
        self.step = self.yq * self.kz
        self.edge = HALO * self.kz
        self.group = LANES // max(self.kz, 1)
        self.chunks = -(-self.ng // self.group)
        self.deep = self.chunks * LANES
        self.third = self.kz // HALO
        self.rows = up(2 * self.xe + self.cx, 8)
        self.mirror = self.nx // 2 + 1

    def fits(self):
        return (
            self.even
            and self.gx % 2 == 0
            and self.gl % 2 == 0
            and self.nz % (self.ng * 8) == 0
            and self.nz % LANES == 0
            and self.yq == 2 * HALO - 1
            and self.kz % (8 * HALO) == 0
            and self.step + self.third <= LANES
            and self.step <= LANES
            and self.step % 8 == 0
            and self.nx <= LANES
            and 2 * (LANES - self.nx) >= self.nx
            and 3 * self.mirror <= LANES
            and self.ny % 8 == 0
            and self.nx % 16 == 0
            and self.ny >= 2 * HALO
            and self.gx * self.xw <= LANES
        )

    def z_forward(self):
        wave = np.arange(self.nz)
        owner = wave // self.kz
        place = owner // self.group * LANES + owner % self.group * self.kz + wave % self.kz
        table = np.zeros((self.nz, self.deep))
        table[:, place] = cas_table(wave, wave, self.nz)
        return three(table)

    def x_waves(self):
        return np.concatenate([np.arange(self.mirror), np.arange(self.nx - 1, self.mirror - 1, -1)])

    def x_forward(self):
        table = np.zeros((LANES, self.nx))
        table[: self.nx] = cas_table(self.x_waves(), np.arange(self.nx), self.nx)
        return thirds(table)

    def y_both(self):
        table = np.zeros((self.ny, self.yp))
        table[:, : self.ny] = cas_table(np.arange(self.ny), np.arange(self.ny), self.ny)
        return table

    def ends(self):
        low = np.arange(HALO)
        return np.concatenate([low, self.ny - 1 - low])

    def y_ends(self):
        table = np.zeros((8, self.yp))
        table[: 2 * HALO, : self.ny] = cas_table(self.ends(), np.arange(self.ny), self.ny)
        return sixths(table)

    def y_sources(self):
        table = np.zeros((self.ny, LANES), np.float32)
        table[:, : 2 * HALO] = cas_table(np.arange(self.ny), self.ends(), self.ny)
        return table

    def x_backward(self):
        wide = np.zeros((self.gx * self.xw, LANES))
        own = np.zeros((self.gx * self.xp, LANES))
        waves = self.x_waves()
        for g in range(self.gx):
            x = (g * self.cx - HALO + np.arange(self.xe)) % self.nx
            wide[g * self.xw : g * self.xw + self.xe, : self.nx] = cas_table(x, waves, self.nx)
            x = g * self.cx + np.arange(self.cx)
            own[g * self.xp : g * self.xp + self.cx, : self.nx] = cas_table(x, waves, self.nx)
        scale = 4.0 * np.pi / (self.nx * self.nz)
        return np.concatenate(three(np.concatenate([wide, own], axis=0) * scale), axis=1)

    def plane(self):
        plane = np.full((self.ny, LANES), 1e30)
        lam_x = symbol_table(self.nx)[self.x_waves()]
        plane[:, : self.nx] = lam_x[None, :] + symbol_table(self.ny)[:, None]
        return plane.astype(np.float32)

    def coarse_pack(self):
        parts = [self.x_forward(), thirds(self.y_both()), sixths(self.y_both())]
        parts += [self.y_ends(), self.x_backward()]
        width = max(part.shape[1] for part in parts)
        self.places, rows = [], 0
        for part in parts:
            self.places.append((rows, part.shape))
            rows = up(rows + part.shape[0], 16)
        table = np.zeros((rows, width), ml_dtypes.bfloat16)
        for (row, shape), part in zip(self.places, parts):
            table[row : row + shape[0], : shape[1]] = part
        return table

    def fine_pack(self):
        parts = [self.plane(), self.y_sources(), self.joins()]
        return np.concatenate([part.reshape(-1, LANES) for part in parts], axis=0)

    def coarse(self, ref, which):
        row, shape = self.places[which]
        return ref[row : row + shape[0], : shape[1]]

    def join_rows(self, ref, row):
        me = lax.axis_index("gx") * self.gl + lax.axis_index("gl")
        size = (2 * HALO + 1) * self.kz
        start = 2 * self.ny + me * size + row * self.kz
        return ref[pl.ds(pl.multiple_of(start, 8), self.kz), :]

    def joins(self):
        lam_x = symbol_table(self.nx)[: self.mirror]
        lam_y, lam_z = symbol_table(self.ny), symbol_table(self.nz)
        total = EPS_PRECOND * (lam_z[:, None, None] + lam_x[None, :, None] + lam_y) + SHIFT_PRECOND
        green = np.real(np.fft.ifft(1.0 / total, axis=-1))
        i = np.arange(HALO)
        near = green[..., np.abs(i[:, None] - i[None, :])]
        far = green[..., i[:, None] + i[None, :] + 1]
        band = np.zeros((HALO, HALO))
        for row in range(HALO):
            for column in range(HALO - row):
                band[row, column] = STENCIL[row + column]
        eye = np.eye(HALO)
        even = np.linalg.inv(eye - 2.0 * (near + far) @ band)
        odd = np.linalg.inv(eye + 2.0 * (near - far) @ band)
        both = np.stack([even, odd], axis=2).reshape(self.ng, self.kz, self.mirror, 2 * HALO, HALO)
        both = both.transpose(0, 3, 1, 4, 2).reshape(self.ng, 2 * HALO, self.kz, HALO * self.mirror)
        table = np.zeros((self.ng, 2 * HALO + 1, self.kz, LANES), np.float32)
        table[:, : 2 * HALO, :, : HALO * self.mirror] = both
        table[:, 2 * HALO] = lam_z.reshape(self.ng, self.kz, 1)
        return table


VMEM_SPEC = pl.BlockSpec(memory_space=pltpu.VMEM)
ANY_SPEC = pl.BlockSpec(memory_space=pl.ANY)


def call(kernel, outs, args, scratch=(), specs=None, limit=VMEM_LIMIT):
    nbytes = sum(int(np.prod(a.shape)) * a.dtype.itemsize for a in (*args, *outs))
    return pl.pallas_call(
        kernel,
        out_shape=tuple(outs),
        in_specs=specs or [VMEM_SPEC] * len(args),
        out_specs=tuple([VMEM_SPEC] * len(outs)),
        scratch_shapes=list(scratch),
        compiler_params=pltpu.CompilerParams(vmem_limit_bytes=limit),
        cost_estimate=pl.CostEstimate(flops=0, bytes_accessed=nbytes, transcendentals=0),
    )(*args)


def lane_index(rows):
    return lax.broadcasted_iota(jnp.int32, (rows, LANES), 1)


def moved(values, shift):
    shift = shift % LANES
    return values if shift == 0 else pltpu.roll(values, shift, 1)


def within(lane, first, count):
    return (lane >= first) & (lane < first + count)


def between(lane, slot, width):
    return within(lane, slot * width, width)


def fetched(pairs, sems):
    copies = [
        pltpu.make_async_copy(source, target, sems.at[i])
        for i, (source, target) in enumerate(pairs)
    ]
    for copy in copies:
        copy.start()
    return copies


def forward_kernel(p, charge_in, high_in, low_in, out, charge, high_z, low_z, sems):
    copies = fetched(((charge_in, charge), (high_in, high_z), (low_in, low_z)), sems)
    copies[0].wait()
    lane = lane_index(p.xp)
    ready = False
    for part in range(2):
        ys = range(part * p.yq, (part + 1) * p.yq)
        high, low = split(jnp.concatenate([padded_rows(charge[y], p.xp) for y in ys], axis=0))
        if not ready:
            copies[1].wait()
        spec = mul(high, high_z[...]) + mul(low, high_z[...])
        if not ready:
            copies[2].wait()
            ready = True
        spec = spec + mul(high, low_z[...])
        for target in range(p.ng):
            chunk, slot = divmod(target, p.group)
            block = jnp.zeros((p.xp, LANES), jnp.float32)
            for i in range(p.yq):
                piece = spec[i * p.xp : (i + 1) * p.xp, chunk * LANES : (chunk + 1) * LANES]
                block = jnp.where(between(lane, i, p.kz), moved(piece, (i - slot) * p.kz), block)
            out[target, part * p.cx : (part + 1) * p.cx] = block[: p.cx]


def table_kernel(p, fine, out):
    plane = fine[: p.ny, :]
    waves = p.join_rows(fine, 2 * HALO)
    for k in range(p.kz):
        symbol = EPS_PRECOND * (plane + waves[k : k + 1]) + SHIFT_PRECOND
        out[:, k * LANES : (k + 1) * LANES] = 1.0 / (float(p.ny) * symbol)


def lanes_of(values, k):
    return values[:, k * LANES : (k + 1) * LANES]


def solve_kernel(p, blocks, coarse, table, spectrum_out, own, sent, turned, ends):
    x_fwd, y_both, y_ends = (p.coarse(coarse, i) for i in (0, 1, 3))
    columns = []
    for gl in range(p.gl):
        for part in range(2):
            pieces = [
                blocks[gx * p.gl + gl, part * p.cx : (part + 1) * p.cx] for gx in range(p.gx)
            ]
            columns.append(jnp.concatenate(pieces, axis=0))
    along_x = mul(x_fwd, stacked(jnp.concatenate(columns, axis=1), 0))
    for b in range(2 * p.gl):
        turned[pl.ds(b * p.step, LANES), :] = lanes_of(along_x, b).T
    field = jnp.concatenate(
        [turned[pl.ds(k, p.ny, stride=p.kz), :] for k in range(p.kz)], axis=1
    )
    along_y = mul(y_both, stacked(padded_rows(field, p.yp), 0))
    solved = along_y * table[...]
    spectrum_out[...] = solved
    at_ends = mul(y_ends, spread(padded_rows(solved, p.yp), 0))
    for k in range(p.kz):
        ends[pl.ds(k, 8, stride=p.kz), :] = lanes_of(at_ends, k)
    own[...] = ends[pl.ds(0, 2 * HALO * p.kz), :]
    piece = [ends[pl.ds(j * p.kz, p.kz), :] for j in range(2 * HALO)]
    lane = lane_index(p.kz)
    free = LANES - p.nx
    for i in range(4):
        spare = moved(piece[4 + i // 2], p.nx if i % 2 == 0 else p.nx - free)
        sent[pl.ds(i * p.kz, p.kz), :] = jnp.where(lane < p.nx, piece[i], spare)


def return_kernel(
    p, spectrum_in, own, received, table, fine, coarse,
    out, sources, planes,
):
    y_back, x_bwd = p.coarse(coarse, 2), p.coarse(coarse, 4)
    one, two, last = (x_bwd[:, i * LANES : (i + 1) * LANES] for i in range(3))
    x_bwd = jnp.concatenate([one, one, one, two, two, last], axis=1)
    columns = fine[p.ny : 2 * p.ny, :]
    y_sources = [jnp.broadcast_to(columns[:, j : j + 1], columns.shape) for j in range(2 * HALO)]
    lane = lane_index(p.kz)
    free = LANES - p.nx
    part = [received[pl.ds(i * p.kz, p.kz), :] for i in range(4)]
    other = [jnp.where(lane < p.nx, value, 0.0) for value in part]
    for i in range(2):
        first = moved(part[2 * i], -p.nx)
        second = moved(part[2 * i + 1], free - p.nx)
        other.append(jnp.where(lane < free, first, jnp.where(lane < p.nx, second, 0.0)))
    mine = [own[pl.ds(j * p.kz, p.kz), :] for j in range(2 * HALO)]
    jump = [mine[j] - other[j] for j in range(2 * HALO)]
    even = [jump[j] + jump[HALO + j] for j in range(HALO)]
    odd = [jump[j] - jump[HALO + j] for j in range(HALO)]

    def mixed(base, vector):
        results = []
        for i in range(HALO):
            packed = p.join_rows(fine, base + i)
            total = 0.0
            for j in range(HALO):
                first = moved(packed, -j * p.mirror)
                second = moved(packed, p.mirror - 1 - j * p.mirror)
                total = total + jnp.where(lane < p.mirror, first, second) * vector[j]
            results.append(total)
        return results

    even_full, odd_full = mixed(0, even), mixed(HALO, odd)
    low_full = [0.5 * (e + o) for e, o in zip(even_full, odd_full)]
    high_full = [0.5 * (e - o) for e, o in zip(even_full, odd_full)]
    far_low = [other[j] - 0.5 * (low_full[j] - jump[j]) for j in range(HALO)]
    far_high = [other[HALO + j] - 0.5 * (high_full[j] - jump[HALO + j]) for j in range(HALO)]
    for i in range(HALO):
        sources[pl.ds(i * p.kz, p.kz), :] = sum(
            STENCIL[i + j] * high_full[j] for j in range(HALO - i)
        )
        sources[pl.ds((HALO + i) * p.kz, p.kz), :] = sum(
            STENCIL[i + j] * low_full[j] for j in range(HALO - i)
        )
    whole = []
    for k in range(p.kz):
        added = sum(y_sources[j] * sources[pl.ds(j * p.kz + k, 1), :] for j in range(2 * HALO))
        whole.append(
            spectrum_in[:, k * LANES : (k + 1) * LANES]
            + added * table[:, k * LANES : (k + 1) * LANES]
        )
    back_y = mul(y_back, spread(padded_rows(jnp.concatenate(whole, axis=1), p.yp), 0))
    base = p.edge
    for k in range(p.kz):
        planes[pl.ds(base + k, p.ny, stride=p.kz), :] = lanes_of(back_y, k)
    after = base + p.ny * p.kz
    for i in range(HALO):
        planes[pl.ds(base - (i + 1) * p.kz, p.kz), :] = far_high[i]
        planes[pl.ds(after + i * p.kz, p.kz), :] = far_low[i]
    cut = p.gx * p.xw
    wide_rows = x_bwd[:cut, :]
    own_rows = x_bwd[cut:, :]
    rest = p.rows - 2 * p.xe - p.cx

    def filled(pieces, part):
        first = base + (gl + 1) * 2 * p.step + p.edge - p.kz + part * p.third
        pieces = [planes[pl.ds(at, count), :] for at, count in (*pieces, (first, p.third))]
        return padded_rows(jnp.concatenate(pieces, axis=0), LANES)

    for gl in range(p.gl):
        start = base + gl * 2 * p.step
        end = start + 2 * p.step
        both = [filled([(start + i * p.step, p.step)], i) for i in range(2)]
        wide = mul_t(wide_rows, spread(jnp.concatenate(both, axis=0), 1))
        sides = filled([(start - p.edge, p.edge), (end, p.edge - p.kz)], 2)
        side = mul_t(own_rows, spread(sides, 1))
        for gx in range(p.gx):
            target = gx * p.gl + gl
            for half in range(2):
                out[target, half * p.xe : (half + 1) * p.xe] = wide[
                    gx * p.xw : gx * p.xw + p.xe, half * LANES : (half + 1) * LANES
                ]
            at, line = 2 * p.xe, gx * p.xp
            out[target, at : at + p.cx] = side[line : line + p.cx]
            if rest:
                out[target, at + p.cx :] = jnp.zeros((rest, LANES), jnp.float32)


def faces_kernel(p, eps, ex_low, ex_high, ey_low, ey_high, faces_x, faces_y, faces_z, mass):
    for y in range(p.cy):
        here = eps[y]
        line = jnp.concatenate([ex_low[y], here, ex_high[y]], axis=0)
        faces_x[y, : p.cx + 3] = line[: p.cx + 3] + line[1 : p.cx + 4]
        faces_z[y] = here + pltpu.roll(here, p.nz - 1, 1)
        mass[y] = (KAPPA_SCALE / (EPS_SOLVENT - 1.0)) * (here - 1.0)
    planes = [ey_low[0], ey_low[1], *[eps[y] for y in range(p.cy)], ey_high[0], ey_high[1]]
    for y in range(p.cy + 3):
        faces_y[y] = planes[y] + planes[y + 1]


def stencil_kernel(
    p, blocks, high_z, low_z, last_z, charge, faces_x, faces_y, faces_z, mass,
    pre, image, sums, field,
):
    lane = lane_index(p.xw)
    side = 2 * p.xe

    def line_of(chunk, first, rows, source_lane, skip, count):
        here = lane[:rows]
        line = jnp.zeros((rows, LANES), jnp.float32)
        for slot in range(min(p.group, p.ng - chunk * p.group)):
            part = blocks[chunk * p.group + slot, first : first + rows, :]
            at = slot * p.kz + skip
            line = jnp.where(within(here, at, count), moved(part, at - source_lane), line)
        return line

    def plain(first, rows, piece):
        return rows, lambda chunk: line_of(chunk, first, rows, piece * p.kz, 0, p.kz)

    def last_layer(chunk):
        total = 0.0
        for part, row in enumerate((HALO, p.xe + HALO, side)):
            first = max(0, row - HALO) // 8 * 8 if part < 2 else row // 8 * 8
            rows = p.xw if part < 2 else p.xp
            line = line_of(chunk, first, rows, p.step, part * p.third, p.third)
            total = total + line[row - first : row - first + p.cx]
        return padded_rows(total, p.xp)

    windows = [plain(y // p.yq * p.xe // 8 * 8, p.xw, y % p.yq) for y in range(p.cy)]
    windows += [plain(side // 8 * 8, p.xp, h) for h in range(2 * HALO - 1)]
    windows.append((p.xp, last_layer))
    one, two, last = high_z[...], low_z[...], last_z[...]
    six_z = jnp.concatenate([one, one, one, two, two, last], axis=1)

    def assembled(group):
        parts = []
        for chunk in range(p.chunks):
            parts.append(jnp.concatenate([make(chunk) for rows, make in group], axis=0))
        return jnp.concatenate(parts, axis=1)

    groups = [windows[: p.yq + 1], windows[p.yq + 1 :]]
    results = []
    for group in groups:
        value = assembled(group)
        rows = value.shape[0]
        parts, rest = [], value
        for _ in range(3):
            parts.append(rest.astype(jnp.bfloat16))
            rest = rest - parts[-1].astype(jnp.float32)
        tall = mul_t(jnp.concatenate(parts, axis=0), one)
        second = mul_t(jnp.concatenate(parts[:2], axis=0), two)
        small = tall[2 * rows :] + second[rows:] + mul_t(parts[0], last)
        results.append(tall[:rows] + ((tall[rows : 2 * rows] + second[:rows]) + small))
    whole = jnp.concatenate(results, axis=0)
    starts = np.cumsum([0] + [rows for rows, make in windows])
    for y in range(p.cy):
        at = int(starts[y]) + y // p.yq * p.xe % 8
        field[HALO + y, : p.xe] = whole[at : at + p.xe]
    for h in range(2 * HALO):
        at = int(starts[p.cy + h]) + (side % 8 if h < 2 * HALO - 1 else 0)
        y = h if h < HALO else h + p.cy
        field[y, HALO : HALO + p.cx] = whole[at : at + p.cx]

    def stretch(flux_at):
        return 27.0 * (flux_at(2) - flux_at(1)) - (flux_at(3) - flux_at(0))

    rz = jnp.zeros((p.cx, LANES), jnp.float32)
    dot = jnp.zeros((p.cx, LANES), jnp.float32)
    fluxes_y = {}

    def flux_y(y):
        if y not in fluxes_y:
            val = [field[y + i, HALO : HALO + p.cx, :] for i in range(4)]
            fluxes_y[y] = faces_y[y] * stretch(lambda i: val[i])
        return fluxes_y[y]

    n = p.nz
    for y in range(p.cy):
        line = field[HALO + y]
        flux = faces_x[y, : p.cx + 3] * stretch(lambda i: line[i : i + p.cx + 3])
        term = stretch(lambda i: flux[i : i + p.cx])
        term = term + stretch(lambda i: flux_y(y + i))
        here = line[HALO : HALO + p.cx]
        grad = 27.0 * (pltpu.roll(here, n - 1, 1) - here) - (
            pltpu.roll(here, n - 2, 1) - pltpu.roll(here, 1, 1)
        )
        flux = faces_z[y] * grad
        term = term + (
            27.0 * (flux - pltpu.roll(flux, 1, 1))
            - (pltpu.roll(flux, n - 1, 1) - pltpu.roll(flux, 2, 1))
        )
        result = mass[y] * here - term * (0.5 / 576.0)
        pre[y] = here
        image[y] = result
        one = charge[y] * here
        two = result * here
        for c in range(n // LANES):
            rz = rz + one[:, c * LANES : (c + 1) * LANES]
            dot = dot + two[:, c * LANES : (c + 1) * LANES]
    rz = jnp.sum(rz, axis=0, keepdims=True)
    dot = jnp.sum(dot, axis=0, keepdims=True)
    half = LANES // 2
    rz = rz + pltpu.roll(rz, half, 1)
    dot = dot + pltpu.roll(dot, half, 1)
    both = jnp.where(lane_index(1) < half, rz, dot)
    sums[...] = jnp.broadcast_to(both[None], sums.shape)


def update_kernel(p, sums, charge, pre, image, solution_field, residual):
    half = LANES // 2
    total = jnp.sum(sums[...], axis=0)
    lane = lane_index(1)
    rz = jnp.sum(jnp.where(lane < half, total, 0.0), axis=1, keepdims=True)
    dot = jnp.sum(jnp.where(lane < half, 0.0, total), axis=1, keepdims=True)
    alpha = jnp.broadcast_to((4.0 * math.pi) * rz / dot, (p.cx, p.nz))
    for y in range(p.cy):
        solution_field[y] = alpha * pre[y]
        residual[y] = (4.0 * math.pi) * charge[y] - alpha * image[y]


def local_planes(p, density, charge):
    group = ("gx", "gl")
    along_y = ("gh", "gl")
    f32 = jnp.float32

    def shape(*dims):
        return jax.ShapeDtypeStruct(dims, f32)

    def pairs(count, first):
        low = range(first, count, 2)
        near = [(i, (i + 1) % count) for i in low]
        return near + [(target, source) for source, target in near]

    even_x = lax.axis_index("gx") % 2 == 0
    even_y = lax.axis_index("gl") % 2 == 0

    density = density.transpose(1, 0, 2)
    charge = charge.transpose(1, 0, 2)
    high_z, low_z, last_z = (jnp.asarray(part) for part in p.z_forward())
    coarse, fine = jnp.asarray(p.coarse_pack()), jnp.asarray(p.fine_pack())
    (blocks,) = call(
        lambda *refs: forward_kernel(p, *refs),
        [shape(p.ng, 2 * p.cx, LANES)],
        [charge, high_z, low_z],
        [
            pltpu.VMEM((p.cy, p.cx, p.nz), f32),
            pltpu.VMEM((p.nz, p.deep), jnp.bfloat16),
            pltpu.VMEM((p.nz, p.deep), jnp.bfloat16),
            pltpu.SemaphoreType.DMA((3,)),
        ],
        specs=[ANY_SPEC] * 3,
        limit=None,
    )
    blocks = lax.all_to_all(blocks, group, 0, 0)
    (table,) = call(
        lambda *refs: table_kernel(p, *refs), [shape(p.ny, p.kz * LANES)], [fine]
    )
    eps = permittivity(density)
    swap_by = lax.ppermute(
        jnp.where(even_y, eps[:2], eps[p.cy - 2 :]), along_y, pairs(2 * p.gl, 1)
    )
    swap_bx = lax.ppermute(
        jnp.where(even_x, eps[:, :2], eps[:, p.cx - 2 :]), "gx", pairs(p.gx, 1)
    )
    swap_ay = lax.ppermute(
        jnp.where(even_y, eps[p.cy - 2 :], eps[:2]), along_y, pairs(2 * p.gl, 0)
    )
    swap_ax = lax.ppermute(
        jnp.where(even_x, eps[:, p.cx - 2 :], eps[:, :2]), "gx", pairs(p.gx, 0)
    )
    blocks, eps, table = lax.optimization_barrier(
        (blocks, eps, table)
    )
    spectrum_half, own, sent = call(
        lambda *refs: solve_kernel(p, *refs),
        [shape(p.ny, p.kz * LANES), shape(2 * HALO * p.kz, LANES), shape(4 * p.kz, LANES)],
        [blocks, coarse, table],
        [pltpu.VMEM((p.ny * p.kz + LANES, LANES), f32), pltpu.VMEM((8 * p.kz, LANES), f32)],
    )
    sent, eps = lax.optimization_barrier((sent, eps))
    received = lax.ppermute(sent, "gh", [(0, 1), (1, 0)])
    ex_low, ex_high = jnp.where(even_x, swap_bx, swap_ax), jnp.where(even_x, swap_ax, swap_bx)
    ey_low, ey_high = jnp.where(even_y, swap_by, swap_ay), jnp.where(even_y, swap_ay, swap_by)
    brick = (p.cy, p.cx, p.nz)
    faces = call(
        lambda *refs: faces_kernel(p, *refs),
        [
            shape(p.cy, p.xp, p.nz), shape(p.cy + 3, p.cx, p.nz), shape(*brick), shape(*brick),
        ],
        [eps, ex_low, ex_high, ey_low, ey_high],
    )
    received, *faces = lax.optimization_barrier((received, *faces))
    (blocks,) = call(
        lambda *refs: return_kernel(p, *refs),
        [shape(p.ng, p.rows, LANES)],
        [
            spectrum_half, own, received, table, fine, coarse,
        ],
        [
            pltpu.VMEM((2 * HALO * p.kz, LANES), f32),
            pltpu.VMEM((p.ny * p.kz + 2 * p.edge, LANES), f32),
        ],
    )
    blocks = lax.all_to_all(blocks, group, 0, 0)
    pre, image, sums = call(
        lambda *refs: stencil_kernel(p, *refs),
        [shape(*brick), shape(*brick), shape(2 * p.ng, 1, LANES)],
        [blocks, high_z, low_z, last_z, charge, *faces],
        [
            pltpu.VMEM((p.cy + 2 * HALO, p.xw, p.nz), f32),
        ],
    )
    sums = lax.all_to_all(sums, ("gx", "gh", "gl"), 0, 0)
    solution_field, residual = call(
        lambda *refs: update_kernel(p, *refs),
        [shape(*brick), shape(*brick)],
        [sums, charge, pre, image],
    )
    return solution_field.transpose(1, 0, 2), residual.transpose(1, 0, 2)


def solution(mesh):
    count_x, count_y = mesh.shape["gx"], mesh.shape["gy"]

    def run(density, charge):
        plan = Plan(charge.shape, count_x, count_y)
        if plan.fits():
            split_mesh = jax.sharding.Mesh(
                mesh.devices.reshape(count_x, 2, count_y // 2), ("gx", "gh", "gl")
            )
            spec = P("gx", ("gh", "gl"), None)
            body, over = (lambda *args: local_planes(plan, *args)), split_mesh
        else:
            spec = P("gx", "gy", None)
            body, over = local_lines, mesh
        return jax.shard_map(
            body, mesh=over, in_specs=(spec, spec), out_specs=(spec, spec), check_vma=False
        )(density, charge)

    return run
```

```python
import math

import jax
import jax.numpy as jnp
import ml_dtypes
import numpy as np
from jax import lax
from jax.experimental import pallas as pl
from jax.experimental.pallas import tpu as pltpu
from jax.sharding import PartitionSpec as P

EPS_SOLVENT = 78.3
RHO_UPPER = 0.005
RHO_LOWER = 0.0001
KAPPA_SCALE = 0.1
EPS_PRECOND = 20.0
SHIFT_PRECOND = 0.05
HIGHEST = lax.Precision.HIGHEST
LANES = 128
HALO = 3
VMEM_LIMIT = 48 << 20


def extended(block, sides, width):
    for axis, dim in sides:
        count = lax.axis_size(axis)
        forward = [(i, i + 1) for i in range(count - 1)]
        forward.append((count - 1, 0))
        backward = [(target, source) for source, target in forward]
        low = lax.ppermute(
            lax.slice_in_dim(block, block.shape[dim] - width, None, axis=dim), axis, forward
        )
        high = lax.ppermute(lax.slice_in_dim(block, 0, width, axis=dim), axis, backward)
        block = jnp.concatenate([low, block, high], axis=dim)
    return block


def permittivity(density):
    upper = math.log(RHO_UPPER)
    lower = math.log(RHO_LOWER)
    fraction = jnp.clip((upper - jnp.log(density)) / (upper - lower), 0.0, 1.0)
    exponent = fraction - jnp.sin(2.0 * math.pi * fraction) / (2.0 * math.pi)
    return jnp.exp(exponent * math.log(EPS_SOLVENT))


def hartley(length):
    indices = jnp.arange(length, dtype=jnp.int32)
    product = indices[:, None] * indices[None, :] % length
    angles = product.astype(jnp.float32) * (2.0 * math.pi / length)
    return jnp.cos(angles) + jnp.sin(angles)


def spectrum(wavenum, length):
    halfang = wavenum.astype(jnp.float32) * (math.pi / length)
    return ((27.0 * jnp.sin(halfang) - jnp.sin(3.0 * halfang)) / 12.0) ** 2


def cutout(values, offset, length, dimen):
    return lax.slice_in_dim(values, offset, offset + length, axis=dimen)


def padded_term(padded, faces, count, dimen):
    nfaces = count + 3
    grad = (
        27.0 * (cutout(padded, 2, nfaces, dimen) - cutout(padded, 1, nfaces, dimen))
        - (cutout(padded, 3, nfaces, dimen) - cutout(padded, 0, nfaces, dimen))
    ) / 24.0
    flux = faces * grad
    return (
        27.0 * (cutout(flux, 2, count, dimen) - cutout(flux, 1, count, dimen))
        - (cutout(flux, 3, count, dimen) - cutout(flux, 0, count, dimen))
    ) / 24.0


def rolled_term(field, faces):
    grad = (
        27.0 * (jnp.roll(field, -1, 2) - field) - (jnp.roll(field, -2, 2) - jnp.roll(field, 1, 2))
    ) / 24.0
    flux = faces * grad
    return (
        27.0 * (flux - jnp.roll(flux, 1, 2)) - (jnp.roll(flux, -1, 2) - jnp.roll(flux, 2, 2))
    ) / 24.0


def operate(field, faces_x, faces_y, faces_z, kappa):
    cellsx = field.shape[0]
    cellsy = field.shape[1]
    padded = extended(field, (("gx", 0), ("gy", 1)), 3)
    term_x = padded_term(padded[:, 3 : 3 + cellsy], faces_x, cellsx, 0)
    term_y = padded_term(padded[3 : 3 + cellsx], faces_y, cellsy, 1)
    term_z = rolled_term(field, faces_z)
    return kappa * field - (term_x + term_y + term_z)


def precondition(field):
    cellsx, cellsy, length_z = field.shape
    size_x = cellsx * lax.axis_size("gx")
    size_y = cellsy * lax.axis_size("gy")
    hart_x = hartley(size_x)
    hart_y = hartley(size_y)
    hart_z = hartley(length_z)
    scaling = float(size_x * size_y * length_z)
    forward = jnp.dot(field, hart_z, precision=HIGHEST)
    zpiece = length_z // lax.axis_size("gx")
    xpiece = size_x // lax.axis_size("gy")
    lines_x = lax.all_to_all(forward, "gx", split_axis=2, concat_axis=0, tiled=True)
    along_x = jnp.einsum("xyk,xa->yka", lines_x, hart_x, precision=HIGHEST)
    lines_y = lax.all_to_all(along_x, "gy", split_axis=2, concat_axis=0, tiled=True)
    along_y = jnp.einsum("ykb,yc->kbc", lines_y, hart_y, precision=HIGHEST)
    wave_z = lax.axis_index("gx") * zpiece + jnp.arange(zpiece, dtype=jnp.int32)
    wave_x = lax.axis_index("gy") * xpiece + jnp.arange(xpiece, dtype=jnp.int32)
    wave_y = jnp.arange(size_y, dtype=jnp.int32)
    symbol = (
        EPS_PRECOND
        * (
            spectrum(wave_z, length_z)[:, None, None]
            + spectrum(wave_x, size_x)[None, :, None]
            + spectrum(wave_y, size_y)[None, None, :]
        )
        + SHIFT_PRECOND
    )
    scaled = along_y / (symbol * scaling)
    back_y = jnp.einsum("kbc,cy->ykb", scaled, hart_y, precision=HIGHEST)
    lines_back = lax.all_to_all(back_y, "gy", split_axis=0, concat_axis=2, tiled=True)
    back_x = jnp.einsum("yka,ax->xyk", lines_back, hart_x, precision=HIGHEST)
    bricks = lax.all_to_all(back_x, "gx", split_axis=0, concat_axis=2, tiled=True)
    return jnp.dot(bricks, hart_z, precision=HIGHEST)


def residual_inner(residual, precond):
    return lax.psum(jnp.sum(residual * precond), ("gx", "gy"))


def local_lines(density, charge):
    eps = permittivity(density)
    kappa = KAPPA_SCALE * (eps - 1.0) / (EPS_SOLVENT - 1.0)
    cellsx = eps.shape[0]
    cellsy = eps.shape[1]
    eps_padded = extended(eps, (("gx", 0), ("gy", 1)), 2)
    strip_x = eps_padded[:, 2 : 2 + cellsy]
    faces_x = 0.5 * (strip_x[:-1] + strip_x[1:])
    strip_y = eps_padded[2 : 2 + cellsx]
    faces_y = 0.5 * (strip_y[:, :-1] + strip_y[:, 1:])
    faces_z = 0.5 * (eps + jnp.roll(eps, -1, 2))
    rhs = 4.0 * math.pi * charge
    residual = rhs
    precond = precondition(residual)
    inner_now = residual_inner(residual, precond)
    image = operate(precond, faces_x, faces_y, faces_z, kappa)
    alpha = inner_now / lax.psum(jnp.sum(precond * image), ("gx", "gy"))
    solution_field = alpha * precond
    residual = residual - alpha * image
    return (solution_field, residual)


def cas_table(rows, columns, length):
    angle = (np.outer(rows, columns) % length).astype(np.float64) * (2.0 * np.pi / length)
    return np.cos(angle) + np.sin(angle)


def symbol_table(length):
    halfang = np.arange(length, dtype=np.float64) * (np.pi / length)
    return ((27.0 * np.sin(halfang) - np.sin(3.0 * halfang)) / 12.0) ** 2


def halves(table):
    high = table.astype(ml_dtypes.bfloat16)
    low = (table - high.astype(np.float64)).astype(ml_dtypes.bfloat16)
    return high, low


def thirds(table):
    high, low = halves(table)
    return np.concatenate([high, low, high], axis=1)


def three(table):
    parts, rest = [], np.asarray(table, np.float64)
    for _ in range(3):
        parts.append(rest.astype(ml_dtypes.bfloat16))
        rest = rest - parts[-1].astype(np.float64)
    return parts


def sixths(table):
    one, two, last = three(table)
    return np.concatenate([one, one, one, two, two, last], axis=1)


def spread(values, axis):
    parts, rest = [], values
    for _ in range(3):
        parts.append(rest.astype(jnp.bfloat16))
        rest = rest - parts[-1].astype(jnp.float32)
    one, two, last = parts
    return jnp.concatenate([one, two, last, one, two, one], axis=axis)


def split(values):
    high = values.astype(jnp.bfloat16)
    low = (values - high.astype(jnp.float32)).astype(jnp.bfloat16)
    return high, low


def stacked(values, axis):
    high, low = split(values)
    return jnp.concatenate([high, high, low], axis=axis)


def mul(left, right):
    return jnp.dot(left, right, preferred_element_type=jnp.float32)


def mul_t(left, right):
    return lax.dot_general(
        left, right, (((1,), (1,)), ((), ())), preferred_element_type=jnp.float32
    )


def padded_rows(values, rows):
    if values.shape[0] == rows:
        return values
    gap = jnp.zeros((rows - values.shape[0],) + values.shape[1:], values.dtype)
    return jnp.concatenate([values, gap], axis=0)


def up(size, step):
    return -(-size // step) * step


STENCIL = tuple(EPS_PRECOND * c / 576.0 for c in (-783.0, 54.0, -1.0))


class Plan:
    def __init__(self, shape, count_x, count_y):
        size_x, size_y, self.nz = shape
        self.gx, self.gl = count_x, count_y // 2
        self.nx, self.ny = size_x, size_y // 2
        self.cx, self.cy = size_x // count_x, size_y // count_y
        self.ng = self.gx * self.gl
        self.even = count_y % 2 == 0 and self.cy % 2 == 0 and self.ng > 0
        self.kz = self.nz // max(self.ng, 1)
        self.yq = self.cy // 2
        self.xp = up(self.cx, 8)
        self.xe = self.cx + 2 * HALO
        self.xw = up(self.xe, 8)
        self.yp = up(self.ny, 16)
        self.step = self.yq * self.kz
        self.edge = HALO * self.kz
        self.group = LANES // max(self.kz, 1)
        self.chunks = -(-self.ng // self.group)
        self.deep = self.chunks * LANES
        self.third = self.kz // HALO
        self.rows = up(2 * self.xe + self.cx, 8)
        self.mirror = self.nx // 2 + 1

    def fits(self):
        return (
            self.even
            and self.gx % 2 == 0
            and self.gl % 2 == 0
            and self.nz % (self.ng * 8) == 0
            and self.nz % LANES == 0
            and self.yq == 2 * HALO - 1
            and self.kz % (8 * HALO) == 0
            and self.step + self.third <= LANES
            and self.step <= LANES
            and self.step % 8 == 0
            and self.nx <= LANES
            and 2 * (LANES - self.nx) >= self.nx
            and 3 * self.mirror <= LANES
            and self.ny % 8 == 0
            and self.nx % 16 == 0
            and self.ny >= 2 * HALO
            and self.gx * self.xw <= LANES
        )

    def z_forward(self):
        wave = np.arange(self.nz)
        owner = wave // self.kz
        place = owner // self.group * LANES + owner % self.group * self.kz + wave % self.kz
        table = np.zeros((self.nz, self.deep))
        table[:, place] = cas_table(wave, wave, self.nz)
        return three(table)

    def x_waves(self):
        return np.concatenate([np.arange(self.mirror), np.arange(self.nx - 1, self.mirror - 1, -1)])

    def x_forward(self):
        table = np.zeros((LANES, self.nx))
        table[: self.nx] = cas_table(self.x_waves(), np.arange(self.nx), self.nx)
        return thirds(table)

    def y_both(self):
        table = np.zeros((self.ny, self.yp))
        table[:, : self.ny] = cas_table(np.arange(self.ny), np.arange(self.ny), self.ny)
        return table

    def ends(self):
        low = np.arange(HALO)
        return np.concatenate([low, self.ny - 1 - low])

    def y_ends(self):
        table = np.zeros((8, self.yp))
        table[: 2 * HALO, : self.ny] = cas_table(self.ends(), np.arange(self.ny), self.ny)
        return sixths(table)

    def y_sources(self):
        table = np.zeros((self.ny, LANES), np.float32)
        table[:, : 2 * HALO] = cas_table(np.arange(self.ny), self.ends(), self.ny)
        return table

    def x_backward(self):
        wide = np.zeros((self.gx * self.xw, LANES))
        own = np.zeros((self.gx * self.xp, LANES))
        waves = self.x_waves()
        for g in range(self.gx):
            x = (g * self.cx - HALO + np.arange(self.xe)) % self.nx
            wide[g * self.xw : g * self.xw + self.xe, : self.nx] = cas_table(x, waves, self.nx)
            x = g * self.cx + np.arange(self.cx)
            own[g * self.xp : g * self.xp + self.cx, : self.nx] = cas_table(x, waves, self.nx)
        scale = 4.0 * np.pi / (self.nx * self.nz)
        return np.concatenate(three(np.concatenate([wide, own], axis=0) * scale), axis=1)

    def plane(self):
        plane = np.full((self.ny, LANES), 1e30)
        lam_x = symbol_table(self.nx)[self.x_waves()]
        plane[:, : self.nx] = lam_x[None, :] + symbol_table(self.ny)[:, None]
        return plane.astype(np.float32)

    def coarse_pack(self):
        parts = [self.x_forward(), thirds(self.y_both()), sixths(self.y_both())]
        parts += [self.y_ends(), self.x_backward()]
        width = max(part.shape[1] for part in parts)
        self.places, rows = [], 0
        for part in parts:
            self.places.append((rows, part.shape))
            rows = up(rows + part.shape[0], 16)
        table = np.zeros((rows, width), ml_dtypes.bfloat16)
        for (row, shape), part in zip(self.places, parts):
            table[row : row + shape[0], : shape[1]] = part
        return table

    def fine_pack(self):
        parts = [self.plane(), self.y_sources(), self.joins()]
        return np.concatenate([part.reshape(-1, LANES) for part in parts], axis=0)

    def coarse(self, ref, which):
        row, shape = self.places[which]
        return ref[row : row + shape[0], : shape[1]]

    def join_rows(self, ref, row):
        me = lax.axis_index("gx") * self.gl + lax.axis_index("gl")
        size = (2 * HALO + 1) * self.kz
        start = 2 * self.ny + me * size + row * self.kz
        return ref[pl.ds(pl.multiple_of(start, 8), self.kz), :]

    def joins(self):
        lam_x = symbol_table(self.nx)[: self.mirror]
        lam_y, lam_z = symbol_table(self.ny), symbol_table(self.nz)
        total = EPS_PRECOND * (lam_z[:, None, None] + lam_x[None, :, None] + lam_y) + SHIFT_PRECOND
        green = np.real(np.fft.ifft(1.0 / total, axis=-1))
        i = np.arange(HALO)
        near = green[..., np.abs(i[:, None] - i[None, :])]
        far = green[..., i[:, None] + i[None, :] + 1]
        band = np.zeros((HALO, HALO))
        for row in range(HALO):
            for column in range(HALO - row):
                band[row, column] = STENCIL[row + column]
        eye = np.eye(HALO)
        even = np.linalg.inv(eye - 2.0 * (near + far) @ band)
        odd = np.linalg.inv(eye + 2.0 * (near - far) @ band)
        both = np.stack([even, odd], axis=2).reshape(self.ng, self.kz, self.mirror, 2 * HALO, HALO)
        both = both.transpose(0, 3, 1, 4, 2).reshape(self.ng, 2 * HALO, self.kz, HALO * self.mirror)
        table = np.zeros((self.ng, 2 * HALO + 1, self.kz, LANES), np.float32)
        table[:, : 2 * HALO, :, : HALO * self.mirror] = both
        table[:, 2 * HALO] = lam_z.reshape(self.ng, self.kz, 1)
        return table


VMEM_SPEC = pl.BlockSpec(memory_space=pltpu.VMEM)
ANY_SPEC = pl.BlockSpec(memory_space=pl.ANY)


def call(kernel, outs, args, scratch=(), specs=None, limit=VMEM_LIMIT):
    nbytes = sum(int(np.prod(a.shape)) * a.dtype.itemsize for a in (*args, *outs))
    return pl.pallas_call(
        kernel,
        out_shape=tuple(outs),
        in_specs=specs or [VMEM_SPEC] * len(args),
        out_specs=tuple([VMEM_SPEC] * len(outs)),
        scratch_shapes=list(scratch),
        compiler_params=pltpu.CompilerParams(vmem_limit_bytes=limit),
        cost_estimate=pl.CostEstimate(flops=0, bytes_accessed=nbytes, transcendentals=0),
    )(*args)


def lane_index(rows):
    return lax.broadcasted_iota(jnp.int32, (rows, LANES), 1)


def moved(values, shift):
    shift = shift % LANES
    return values if shift == 0 else pltpu.roll(values, shift, 1)


def within(lane, first, count):
    return (lane >= first) & (lane < first + count)


def between(lane, slot, width):
    return within(lane, slot * width, width)


def fetched(pairs, sems):
    copies = [
        pltpu.make_async_copy(source, target, sems.at[i])
        for i, (source, target) in enumerate(pairs)
    ]
    for copy in copies:
        copy.start()
    return copies


def forward_kernel(p, charge_in, high_in, low_in, out, charge, high_z, low_z, sems):
    copies = fetched(((charge_in, charge), (high_in, high_z), (low_in, low_z)), sems)
    copies[0].wait()
    lane = lane_index(p.xp)
    ready = False
    for part in range(2):
        ys = range(part * p.yq, (part + 1) * p.yq)
        high, low = split(jnp.concatenate([padded_rows(charge[y], p.xp) for y in ys], axis=0))
        if not ready:
            copies[1].wait()
        spec = mul(high, high_z[...]) + mul(low, high_z[...])
        if not ready:
            copies[2].wait()
            ready = True
        spec = spec + mul(high, low_z[...])
        for target in range(p.ng):
            chunk, slot = divmod(target, p.group)
            block = jnp.zeros((p.xp, LANES), jnp.float32)
            for i in range(p.yq):
                piece = spec[i * p.xp : (i + 1) * p.xp, chunk * LANES : (chunk + 1) * LANES]
                block = jnp.where(between(lane, i, p.kz), moved(piece, (i - slot) * p.kz), block)
            out[target, part * p.cx : (part + 1) * p.cx] = block[: p.cx]


def table_kernel(p, fine, out):
    plane = fine[: p.ny, :]
    waves = p.join_rows(fine, 2 * HALO)
    for k in range(p.kz):
        symbol = EPS_PRECOND * (plane + waves[k : k + 1]) + SHIFT_PRECOND
        out[:, k * LANES : (k + 1) * LANES] = 1.0 / (float(p.ny) * symbol)


def lanes_of(values, k):
    return values[:, k * LANES : (k + 1) * LANES]


def solve_kernel(p, blocks, coarse, table, spectrum_out, own, sent, turned, ends):
    x_fwd, y_both, y_ends = (p.coarse(coarse, i) for i in (0, 1, 3))
    columns = []
    for gl in range(p.gl):
        for part in range(2):
            pieces = [
                blocks[gx * p.gl + gl, part * p.cx : (part + 1) * p.cx] for gx in range(p.gx)
            ]
            columns.append(jnp.concatenate(pieces, axis=0))
    along_x = mul(x_fwd, stacked(jnp.concatenate(columns, axis=1), 0))
    for b in range(2 * p.gl):
        turned[pl.ds(b * p.step, LANES), :] = lanes_of(along_x, b).T
    field = jnp.concatenate(
        [turned[pl.ds(k, p.ny, stride=p.kz), :] for k in range(p.kz)], axis=1
    )
    along_y = mul(y_both, stacked(padded_rows(field, p.yp), 0))
    solved = along_y * table[...]
    spectrum_out[...] = solved
    at_ends = mul(y_ends, spread(padded_rows(solved, p.yp), 0))
    for k in range(p.kz):
        ends[pl.ds(k, 8, stride=p.kz), :] = lanes_of(at_ends, k)
    own[...] = ends[pl.ds(0, 2 * HALO * p.kz), :]
    piece = [ends[pl.ds(j * p.kz, p.kz), :] for j in range(2 * HALO)]
    lane = lane_index(p.kz)
    free = LANES - p.nx
    for i in range(4):
        spare = moved(piece[4 + i // 2], p.nx if i % 2 == 0 else p.nx - free)
        sent[pl.ds(i * p.kz, p.kz), :] = jnp.where(lane < p.nx, piece[i], spare)


def return_kernel(
    p, spectrum_in, own, received, table, fine, coarse,
    out, sources, planes,
):
    y_back, x_bwd = p.coarse(coarse, 2), p.coarse(coarse, 4)
    one, two, last = (x_bwd[:, i * LANES : (i + 1) * LANES] for i in range(3))
    x_bwd = jnp.concatenate([one, one, one, two, two, last], axis=1)
    columns = fine[p.ny : 2 * p.ny, :]
    y_sources = [jnp.broadcast_to(columns[:, j : j + 1], columns.shape) for j in range(2 * HALO)]
    lane = lane_index(p.kz)
    free = LANES - p.nx
    part = [received[pl.ds(i * p.kz, p.kz), :] for i in range(4)]
    other = [jnp.where(lane < p.nx, value, 0.0) for value in part]
    for i in range(2):
        first = moved(part[2 * i], -p.nx)
        second = moved(part[2 * i + 1], free - p.nx)
        other.append(jnp.where(lane < free, first, jnp.where(lane < p.nx, second, 0.0)))
    mine = [own[pl.ds(j * p.kz, p.kz), :] for j in range(2 * HALO)]
    jump = [mine[j] - other[j] for j in range(2 * HALO)]
    even = [jump[j] + jump[HALO + j] for j in range(HALO)]
    odd = [jump[j] - jump[HALO + j] for j in range(HALO)]

    def mixed(base, vector):
        results = []
        for i in range(HALO):
            packed = p.join_rows(fine, base + i)
            total = 0.0
            for j in range(HALO):
                first = moved(packed, -j * p.mirror)
                second = moved(packed, p.mirror - 1 - j * p.mirror)
                total = total + jnp.where(lane < p.mirror, first, second) * vector[j]
            results.append(total)
        return results

    even_full, odd_full = mixed(0, even), mixed(HALO, odd)
    low_full = [0.5 * (e + o) for e, o in zip(even_full, odd_full)]
    high_full = [0.5 * (e - o) for e, o in zip(even_full, odd_full)]
    far_low = [other[j] - 0.5 * (low_full[j] - jump[j]) for j in range(HALO)]
    far_high = [other[HALO + j] - 0.5 * (high_full[j] - jump[HALO + j]) for j in range(HALO)]
    for i in range(HALO):
        sources[pl.ds(i * p.kz, p.kz), :] = sum(
            STENCIL[i + j] * high_full[j] for j in range(HALO - i)
        )
        sources[pl.ds((HALO + i) * p.kz, p.kz), :] = sum(
            STENCIL[i + j] * low_full[j] for j in range(HALO - i)
        )
    whole = []
    for k in range(p.kz):
        added = sum(y_sources[j] * sources[pl.ds(j * p.kz + k, 1), :] for j in range(2 * HALO))
        whole.append(
            spectrum_in[:, k * LANES : (k + 1) * LANES]
            + added * table[:, k * LANES : (k + 1) * LANES]
        )
    back_y = mul(y_back, spread(padded_rows(jnp.concatenate(whole, axis=1), p.yp), 0))
    base = p.edge
    for k in range(p.kz):
        planes[pl.ds(base + k, p.ny, stride=p.kz), :] = lanes_of(back_y, k)
    after = base + p.ny * p.kz
    for i in range(HALO):
        planes[pl.ds(base - (i + 1) * p.kz, p.kz), :] = far_high[i]
        planes[pl.ds(after + i * p.kz, p.kz), :] = far_low[i]
    cut = p.gx * p.xw
    wide_rows = x_bwd[:cut, :]
    own_rows = x_bwd[cut:, :]
    rest = p.rows - 2 * p.xe - p.cx

    def filled(pieces, part):
        first = base + (gl + 1) * 2 * p.step + p.edge - p.kz + part * p.third
        pieces = [planes[pl.ds(at, count), :] for at, count in (*pieces, (first, p.third))]
        return padded_rows(jnp.concatenate(pieces, axis=0), LANES)

    for gl in range(p.gl):
        start = base + gl * 2 * p.step
        end = start + 2 * p.step
        both = [filled([(start + i * p.step, p.step)], i) for i in range(2)]
        wide = mul_t(wide_rows, spread(jnp.concatenate(both, axis=0), 1))
        sides = filled([(start - p.edge, p.edge), (end, p.edge - p.kz)], 2)
        side = mul_t(own_rows, spread(sides, 1))
        for gx in range(p.gx):
            target = gx * p.gl + gl
            for half in range(2):
                out[target, half * p.xe : (half + 1) * p.xe] = wide[
                    gx * p.xw : gx * p.xw + p.xe, half * LANES : (half + 1) * LANES
                ]
            at, line = 2 * p.xe, gx * p.xp
            out[target, at : at + p.cx] = side[line : line + p.cx]
            if rest:
                out[target, at + p.cx :] = jnp.zeros((rest, LANES), jnp.float32)


def faces_kernel(p, eps, ex_low, ex_high, ey_low, ey_high, faces_x, faces_y, faces_z, mass):
    for y in range(p.cy):
        here = eps[y]
        line = jnp.concatenate([ex_low[y], here, ex_high[y]], axis=0)
        faces_x[y, : p.cx + 3] = line[: p.cx + 3] + line[1 : p.cx + 4]
        faces_z[y] = here + pltpu.roll(here, p.nz - 1, 1)
        mass[y] = (KAPPA_SCALE / (EPS_SOLVENT - 1.0)) * (here - 1.0)
    planes = [ey_low[0], ey_low[1], *[eps[y] for y in range(p.cy)], ey_high[0], ey_high[1]]
    for y in range(p.cy + 3):
        faces_y[y] = planes[y] + planes[y + 1]


def stencil_kernel(
    p, blocks, high_z, low_z, last_z, charge, faces_x, faces_y, faces_z, mass,
    pre, image, sums, field,
):
    lane = lane_index(p.xw)
    side = 2 * p.xe

    def line_of(chunk, first, rows, source_lane, skip, count):
        here = lane[:rows]
        line = jnp.zeros((rows, LANES), jnp.float32)
        for slot in range(min(p.group, p.ng - chunk * p.group)):
            part = blocks[chunk * p.group + slot, first : first + rows, :]
            at = slot * p.kz + skip
            line = jnp.where(within(here, at, count), moved(part, at - source_lane), line)
        return line

    def plain(first, rows, piece):
        return rows, lambda chunk: line_of(chunk, first, rows, piece * p.kz, 0, p.kz)

    def last_layer(chunk):
        total = 0.0
        for part, row in enumerate((HALO, p.xe + HALO, side)):
            first = max(0, row - HALO) // 8 * 8 if part < 2 else row // 8 * 8
            rows = p.xw if part < 2 else p.xp
            line = line_of(chunk, first, rows, p.step, part * p.third, p.third)
            total = total + line[row - first : row - first + p.cx]
        return padded_rows(total, p.xp)

    windows = [plain(y // p.yq * p.xe // 8 * 8, p.xw, y % p.yq) for y in range(p.cy)]
    windows += [plain(side // 8 * 8, p.xp, h) for h in range(2 * HALO - 1)]
    windows.append((p.xp, last_layer))
    one, two, last = high_z[...], low_z[...], last_z[...]
    six_z = jnp.concatenate([one, one, one, two, two, last], axis=1)

    def assembled(group):
        parts = []
        for chunk in range(p.chunks):
            parts.append(jnp.concatenate([make(chunk) for rows, make in group], axis=0))
        return jnp.concatenate(parts, axis=1)

    groups = [windows[: p.yq + 3], windows[p.yq + 3 :]]
    results = []
    for group in groups:
        value = assembled(group)
        rows = value.shape[0]
        parts, rest = [], value
        for _ in range(3):
            parts.append(rest.astype(jnp.bfloat16))
            rest = rest - parts[-1].astype(jnp.float32)
        tall = mul_t(jnp.concatenate(parts, axis=0), one)
        second = mul_t(jnp.concatenate(parts[:2], axis=0), two)
        small = tall[2 * rows :] + second[rows:] + mul_t(parts[0], last)
        results.append(tall[:rows] + ((tall[rows : 2 * rows] + second[:rows]) + small))
    whole = jnp.concatenate(results, axis=0)
    starts = np.cumsum([0] + [rows for rows, make in windows])
    for y in range(p.cy):
        at = int(starts[y]) + y // p.yq * p.xe % 8
        field[HALO + y, : p.xe] = whole[at : at + p.xe]
    for h in range(2 * HALO):
        at = int(starts[p.cy + h]) + (side % 8 if h < 2 * HALO - 1 else 0)
        y = h if h < HALO else h + p.cy
        field[y, HALO : HALO + p.cx] = whole[at : at + p.cx]

    def stretch(flux_at):
        return 27.0 * (flux_at(2) - flux_at(1)) - (flux_at(3) - flux_at(0))

    rz = jnp.zeros((p.cx, LANES), jnp.float32)
    dot = jnp.zeros((p.cx, LANES), jnp.float32)
    fluxes_y = {}

    def flux_y(y):
        if y not in fluxes_y:
            val = [field[y + i, HALO : HALO + p.cx, :] for i in range(4)]
            fluxes_y[y] = faces_y[y] * stretch(lambda i: val[i])
        return fluxes_y[y]

    n = p.nz
    for y in range(p.cy):
        line = field[HALO + y]
        flux = faces_x[y, : p.cx + 3] * stretch(lambda i: line[i : i + p.cx + 3])
        term = stretch(lambda i: flux[i : i + p.cx])
        term = term + stretch(lambda i: flux_y(y + i))
        here = line[HALO : HALO + p.cx]
        grad = 27.0 * (pltpu.roll(here, n - 1, 1) - here) - (
            pltpu.roll(here, n - 2, 1) - pltpu.roll(here, 1, 1)
        )
        flux = faces_z[y] * grad
        term = term + (
            27.0 * (flux - pltpu.roll(flux, 1, 1))
            - (pltpu.roll(flux, n - 1, 1) - pltpu.roll(flux, 2, 1))
        )
        result = mass[y] * here - term * (0.5 / 576.0)
        pre[y] = here
        image[y] = result
        one = charge[y] * here
        two = result * here
        for c in range(n // LANES):
            rz = rz + one[:, c * LANES : (c + 1) * LANES]
            dot = dot + two[:, c * LANES : (c + 1) * LANES]
    rz = jnp.sum(rz, axis=0, keepdims=True)
    dot = jnp.sum(dot, axis=0, keepdims=True)
    half = LANES // 2
    rz = rz + pltpu.roll(rz, half, 1)
    dot = dot + pltpu.roll(dot, half, 1)
    both = jnp.where(lane_index(1) < half, rz, dot)
    sums[...] = jnp.broadcast_to(both[None], sums.shape)


def update_kernel(p, sums, charge, pre, image, solution_field, residual):
    half = LANES // 2
    total = jnp.sum(sums[...], axis=0)
    lane = lane_index(1)
    rz = jnp.sum(jnp.where(lane < half, total, 0.0), axis=1, keepdims=True)
    dot = jnp.sum(jnp.where(lane < half, 0.0, total), axis=1, keepdims=True)
    alpha = jnp.broadcast_to((4.0 * math.pi) * rz / dot, (p.cx, p.nz))
    for y in range(p.cy):
        solution_field[y] = alpha * pre[y]
        residual[y] = (4.0 * math.pi) * charge[y] - alpha * image[y]


def local_planes(p, density, charge):
    group = ("gx", "gl")
    along_y = ("gh", "gl")
    f32 = jnp.float32

    def shape(*dims):
        return jax.ShapeDtypeStruct(dims, f32)

    def pairs(count, first):
        low = range(first, count, 2)
        near = [(i, (i + 1) % count) for i in low]
        return near + [(target, source) for source, target in near]

    even_x = lax.axis_index("gx") % 2 == 0
    even_y = lax.axis_index("gl") % 2 == 0

    density = density.transpose(1, 0, 2)
    charge = charge.transpose(1, 0, 2)
    high_z, low_z, last_z = (jnp.asarray(part) for part in p.z_forward())
    coarse, fine = jnp.asarray(p.coarse_pack()), jnp.asarray(p.fine_pack())
    (blocks,) = call(
        lambda *refs: forward_kernel(p, *refs),
        [shape(p.ng, 2 * p.cx, LANES)],
        [charge, high_z, low_z],
        [
            pltpu.VMEM((p.cy, p.cx, p.nz), f32),
            pltpu.VMEM((p.nz, p.deep), jnp.bfloat16),
            pltpu.VMEM((p.nz, p.deep), jnp.bfloat16),
            pltpu.SemaphoreType.DMA((3,)),
        ],
        specs=[ANY_SPEC] * 3,
        limit=None,
    )
    blocks = lax.all_to_all(blocks, group, 0, 0)
    (table,) = call(
        lambda *refs: table_kernel(p, *refs), [shape(p.ny, p.kz * LANES)], [fine]
    )
    eps = permittivity(density)
    swap_by = lax.ppermute(
        jnp.where(even_y, eps[:2], eps[p.cy - 2 :]), along_y, pairs(2 * p.gl, 1)
    )
    swap_bx = lax.ppermute(
        jnp.where(even_x, eps[:, :2], eps[:, p.cx - 2 :]), "gx", pairs(p.gx, 1)
    )
    swap_ay = lax.ppermute(
        jnp.where(even_y, eps[p.cy - 2 :], eps[:2]), along_y, pairs(2 * p.gl, 0)
    )
    swap_ax = lax.ppermute(
        jnp.where(even_x, eps[:, p.cx - 2 :], eps[:, :2]), "gx", pairs(p.gx, 0)
    )
    blocks, eps, table = lax.optimization_barrier(
        (blocks, eps, table)
    )
    spectrum_half, own, sent = call(
        lambda *refs: solve_kernel(p, *refs),
        [shape(p.ny, p.kz * LANES), shape(2 * HALO * p.kz, LANES), shape(4 * p.kz, LANES)],
        [blocks, coarse, table],
        [pltpu.VMEM((p.ny * p.kz + LANES, LANES), f32), pltpu.VMEM((8 * p.kz, LANES), f32)],
    )
    received = lax.ppermute(sent, "gh", [(0, 1), (1, 0)])
    ex_low, ex_high = jnp.where(even_x, swap_bx, swap_ax), jnp.where(even_x, swap_ax, swap_bx)
    ey_low, ey_high = jnp.where(even_y, swap_by, swap_ay), jnp.where(even_y, swap_ay, swap_by)
    brick = (p.cy, p.cx, p.nz)
    faces = call(
        lambda *refs: faces_kernel(p, *refs),
        [
            shape(p.cy, p.xp, p.nz), shape(p.cy + 3, p.cx, p.nz), shape(*brick), shape(*brick),
        ],
        [eps, ex_low, ex_high, ey_low, ey_high],
    )
    received, *faces = lax.optimization_barrier((received, *faces))
    (blocks,) = call(
        lambda *refs: return_kernel(p, *refs),
        [shape(p.ng, p.rows, LANES)],
        [
            spectrum_half, own, received, table, fine, coarse,
        ],
        [
            pltpu.VMEM((2 * HALO * p.kz, LANES), f32),
            pltpu.VMEM((p.ny * p.kz + 2 * p.edge, LANES), f32),
        ],
    )
    blocks = lax.all_to_all(blocks, group, 0, 0)
    pre, image, sums = call(
        lambda *refs: stencil_kernel(p, *refs),
        [shape(*brick), shape(*brick), shape(2 * p.ng, 1, LANES)],
        [blocks, high_z, low_z, last_z, charge, *faces],
        [
            pltpu.VMEM((p.cy + 2 * HALO, p.xw, p.nz), f32),
        ],
    )
    sums = lax.all_to_all(sums, ("gx", "gh", "gl"), 0, 0)
    solution_field, residual = call(
        lambda *refs: update_kernel(p, *refs),
        [shape(*brick), shape(*brick)],
        [sums, charge, pre, image],
    )
    return solution_field.transpose(1, 0, 2), residual.transpose(1, 0, 2)


def solution(mesh):
    count_x, count_y = mesh.shape["gx"], mesh.shape["gy"]

    def run(density, charge):
        plan = Plan(charge.shape, count_x, count_y)
        if plan.fits():
            split_mesh = jax.sharding.Mesh(
                mesh.devices.reshape(count_x, 2, count_y // 2), ("gx", "gh", "gl")
            )
            spec = P("gx", ("gh", "gl"), None)
            body, over = (lambda *args: local_planes(plan, *args)), split_mesh
        else:
            spec = P("gx", "gy", None)
            body, over = local_lines, mesh
        return jax.shard_map(
            body, mesh=over, in_specs=(spec, spec), out_specs=(spec, spec), check_vma=False
        )(density, charge)

    return run
```

```python
import math

import jax
import jax.numpy as jnp
import ml_dtypes
import numpy as np
from jax import lax
from jax.experimental import pallas as pl
from jax.experimental.pallas import tpu as pltpu
from jax.sharding import PartitionSpec as P

EPS_SOLVENT = 78.3
RHO_UPPER = 0.005
RHO_LOWER = 0.0001
KAPPA_SCALE = 0.1
EPS_PRECOND = 20.0
SHIFT_PRECOND = 0.05
HIGHEST = lax.Precision.HIGHEST
LANES = 128
HALO = 3
VMEM_LIMIT = 48 << 20


def extended(block, sides, width):
    for axis, dim in sides:
        count = lax.axis_size(axis)
        forward = [(i, i + 1) for i in range(count - 1)]
        forward.append((count - 1, 0))
        backward = [(target, source) for source, target in forward]
        low = lax.ppermute(
            lax.slice_in_dim(block, block.shape[dim] - width, None, axis=dim), axis, forward
        )
        high = lax.ppermute(lax.slice_in_dim(block, 0, width, axis=dim), axis, backward)
        block = jnp.concatenate([low, block, high], axis=dim)
    return block


def permittivity(density):
    upper = math.log(RHO_UPPER)
    lower = math.log(RHO_LOWER)
    fraction = jnp.clip((upper - jnp.log(density)) / (upper - lower), 0.0, 1.0)
    exponent = fraction - jnp.sin(2.0 * math.pi * fraction) / (2.0 * math.pi)
    return jnp.exp(exponent * math.log(EPS_SOLVENT))


def hartley(length):
    indices = jnp.arange(length, dtype=jnp.int32)
    product = indices[:, None] * indices[None, :] % length
    angles = product.astype(jnp.float32) * (2.0 * math.pi / length)
    return jnp.cos(angles) + jnp.sin(angles)


def spectrum(wavenum, length):
    halfang = wavenum.astype(jnp.float32) * (math.pi / length)
    return ((27.0 * jnp.sin(halfang) - jnp.sin(3.0 * halfang)) / 12.0) ** 2


def cutout(values, offset, length, dimen):
    return lax.slice_in_dim(values, offset, offset + length, axis=dimen)


def padded_term(padded, faces, count, dimen):
    nfaces = count + 3
    grad = (
        27.0 * (cutout(padded, 2, nfaces, dimen) - cutout(padded, 1, nfaces, dimen))
        - (cutout(padded, 3, nfaces, dimen) - cutout(padded, 0, nfaces, dimen))
    ) / 24.0
    flux = faces * grad
    return (
        27.0 * (cutout(flux, 2, count, dimen) - cutout(flux, 1, count, dimen))
        - (cutout(flux, 3, count, dimen) - cutout(flux, 0, count, dimen))
    ) / 24.0


def rolled_term(field, faces):
    grad = (
        27.0 * (jnp.roll(field, -1, 2) - field) - (jnp.roll(field, -2, 2) - jnp.roll(field, 1, 2))
    ) / 24.0
    flux = faces * grad
    return (
        27.0 * (flux - jnp.roll(flux, 1, 2)) - (jnp.roll(flux, -1, 2) - jnp.roll(flux, 2, 2))
    ) / 24.0


def operate(field, faces_x, faces_y, faces_z, kappa):
    cellsx = field.shape[0]
    cellsy = field.shape[1]
    padded = extended(field, (("gx", 0), ("gy", 1)), 3)
    term_x = padded_term(padded[:, 3 : 3 + cellsy], faces_x, cellsx, 0)
    term_y = padded_term(padded[3 : 3 + cellsx], faces_y, cellsy, 1)
    term_z = rolled_term(field, faces_z)
    return kappa * field - (term_x + term_y + term_z)


def precondition(field):
    cellsx, cellsy, length_z = field.shape
    size_x = cellsx * lax.axis_size("gx")
    size_y = cellsy * lax.axis_size("gy")
    hart_x = hartley(size_x)
    hart_y = hartley(size_y)
    hart_z = hartley(length_z)
    scaling = float(size_x * size_y * length_z)
    forward = jnp.dot(field, hart_z, precision=HIGHEST)
    zpiece = length_z // lax.axis_size("gx")
    xpiece = size_x // lax.axis_size("gy")
    lines_x = lax.all_to_all(forward, "gx", split_axis=2, concat_axis=0, tiled=True)
    along_x = jnp.einsum("xyk,xa->yka", lines_x, hart_x, precision=HIGHEST)
    lines_y = lax.all_to_all(along_x, "gy", split_axis=2, concat_axis=0, tiled=True)
    along_y = jnp.einsum("ykb,yc->kbc", lines_y, hart_y, precision=HIGHEST)
    wave_z = lax.axis_index("gx") * zpiece + jnp.arange(zpiece, dtype=jnp.int32)
    wave_x = lax.axis_index("gy") * xpiece + jnp.arange(xpiece, dtype=jnp.int32)
    wave_y = jnp.arange(size_y, dtype=jnp.int32)
    symbol = (
        EPS_PRECOND
        * (
            spectrum(wave_z, length_z)[:, None, None]
            + spectrum(wave_x, size_x)[None, :, None]
            + spectrum(wave_y, size_y)[None, None, :]
        )
        + SHIFT_PRECOND
    )
    scaled = along_y / (symbol * scaling)
    back_y = jnp.einsum("kbc,cy->ykb", scaled, hart_y, precision=HIGHEST)
    lines_back = lax.all_to_all(back_y, "gy", split_axis=0, concat_axis=2, tiled=True)
    back_x = jnp.einsum("yka,ax->xyk", lines_back, hart_x, precision=HIGHEST)
    bricks = lax.all_to_all(back_x, "gx", split_axis=0, concat_axis=2, tiled=True)
    return jnp.dot(bricks, hart_z, precision=HIGHEST)


def residual_inner(residual, precond):
    return lax.psum(jnp.sum(residual * precond), ("gx", "gy"))


def local_lines(density, charge):
    eps = permittivity(density)
    kappa = KAPPA_SCALE * (eps - 1.0) / (EPS_SOLVENT - 1.0)
    cellsx = eps.shape[0]
    cellsy = eps.shape[1]
    eps_padded = extended(eps, (("gx", 0), ("gy", 1)), 2)
    strip_x = eps_padded[:, 2 : 2 + cellsy]
    faces_x = 0.5 * (strip_x[:-1] + strip_x[1:])
    strip_y = eps_padded[2 : 2 + cellsx]
    faces_y = 0.5 * (strip_y[:, :-1] + strip_y[:, 1:])
    faces_z = 0.5 * (eps + jnp.roll(eps, -1, 2))
    rhs = 4.0 * math.pi * charge
    residual = rhs
    precond = precondition(residual)
    inner_now = residual_inner(residual, precond)
    image = operate(precond, faces_x, faces_y, faces_z, kappa)
    alpha = inner_now / lax.psum(jnp.sum(precond * image), ("gx", "gy"))
    solution_field = alpha * precond
    residual = residual - alpha * image
    return (solution_field, residual)


def cas_table(rows, columns, length):
    angle = (np.outer(rows, columns) % length).astype(np.float64) * (2.0 * np.pi / length)
    return np.cos(angle) + np.sin(angle)


def symbol_table(length):
    halfang = np.arange(length, dtype=np.float64) * (np.pi / length)
    return ((27.0 * np.sin(halfang) - np.sin(3.0 * halfang)) / 12.0) ** 2


def halves(table):
    high = table.astype(ml_dtypes.bfloat16)
    low = (table - high.astype(np.float64)).astype(ml_dtypes.bfloat16)
    return high, low


def thirds(table):
    high, low = halves(table)
    return np.concatenate([high, low, high], axis=1)


def three(table):
    parts, rest = [], np.asarray(table, np.float64)
    for _ in range(3):
        parts.append(rest.astype(ml_dtypes.bfloat16))
        rest = rest - parts[-1].astype(np.float64)
    return parts


def tower(parts, lib):
    one, two, last = parts
    none = lib.zeros_like(one)
    rows = [(one, one, one), (two, two, none), (last, none, none)]
    return lib.concatenate([lib.concatenate(row, axis=1) for row in rows], axis=0)


def spread(values, axis):
    parts, rest = [], values
    for _ in range(3):
        parts.append(rest.astype(jnp.bfloat16))
        rest = rest - parts[-1].astype(jnp.float32)
    return jnp.concatenate(parts, axis=axis)


def summed(tall):
    rows = tall.shape[0] // 3
    return tall[:rows] + (tall[rows : 2 * rows] + tall[2 * rows :])


def split(values):
    high = values.astype(jnp.bfloat16)
    low = (values - high.astype(jnp.float32)).astype(jnp.bfloat16)
    return high, low


def stacked(values, axis):
    high, low = split(values)
    return jnp.concatenate([high, high, low], axis=axis)


def mul(left, right):
    return jnp.dot(left, right, preferred_element_type=jnp.float32)


def mul_t(left, right):
    return lax.dot_general(
        left, right, (((1,), (1,)), ((), ())), preferred_element_type=jnp.float32
    )


def padded_rows(values, rows):
    if values.shape[0] == rows:
        return values
    gap = jnp.zeros((rows - values.shape[0],) + values.shape[1:], values.dtype)
    return jnp.concatenate([values, gap], axis=0)


def up(size, step):
    return -(-size // step) * step


STENCIL = tuple(EPS_PRECOND * c / 576.0 for c in (-783.0, 54.0, -1.0))


class Plan:
    def __init__(self, shape, count_x, count_y):
        size_x, size_y, self.nz = shape
        self.gx, self.gl = count_x, count_y // 2
        self.nx, self.ny = size_x, size_y // 2
        self.cx, self.cy = size_x // count_x, size_y // count_y
        self.ng = self.gx * self.gl
        self.even = count_y % 2 == 0 and self.cy % 2 == 0 and self.ng > 0
        self.kz = self.nz // max(self.ng, 1)
        self.yq = self.cy // 2
        self.xp = up(self.cx, 8)
        self.xe = self.cx + 2 * HALO
        self.xw = up(self.xe, 8)
        self.yp = up(self.ny, 16)
        self.step = self.yq * self.kz
        self.edge = HALO * self.kz
        self.group = LANES // max(self.kz, 1)
        self.chunks = -(-self.ng // self.group)
        self.deep = self.chunks * LANES
        self.third = self.kz // HALO
        self.rows = up(2 * self.xe + self.cx, 8)
        self.mirror = self.nx // 2 + 1

    def fits(self):
        return (
            self.even
            and self.gx % 2 == 0
            and self.gl % 2 == 0
            and self.nz % (self.ng * 8) == 0
            and self.nz % LANES == 0
            and self.yq == 2 * HALO - 1
            and self.kz % (8 * HALO) == 0
            and self.step + self.third <= LANES
            and self.step <= LANES
            and self.step % 8 == 0
            and self.nx <= LANES
            and 2 * (LANES - self.nx) >= self.nx
            and 3 * self.mirror <= LANES
            and self.ny % 8 == 0
            and self.nx % 16 == 0
            and self.ny >= 2 * HALO
            and self.gx * self.xw <= LANES
        )

    def z_forward(self):
        wave = np.arange(self.nz)
        owner = wave // self.kz
        place = owner // self.group * LANES + owner % self.group * self.kz + wave % self.kz
        table = np.zeros((self.nz, self.deep))
        table[:, place] = cas_table(wave, wave, self.nz)
        return three(table)

    def x_waves(self):
        return np.concatenate([np.arange(self.mirror), np.arange(self.nx - 1, self.mirror - 1, -1)])

    def x_forward(self):
        table = np.zeros((LANES, self.nx))
        table[: self.nx] = cas_table(self.x_waves(), np.arange(self.nx), self.nx)
        return thirds(table)

    def y_both(self):
        table = np.zeros((self.ny, self.yp))
        table[:, : self.ny] = cas_table(np.arange(self.ny), np.arange(self.ny), self.ny)
        return table

    def ends(self):
        low = np.arange(HALO)
        return np.concatenate([low, self.ny - 1 - low])

    def y_ends(self):
        table = np.zeros((8, self.yp))
        table[: 2 * HALO, : self.ny] = cas_table(self.ends(), np.arange(self.ny), self.ny)
        return tower(three(table), np)

    def y_sources(self):
        table = np.zeros((self.ny, LANES), np.float32)
        table[:, : 2 * HALO] = cas_table(np.arange(self.ny), self.ends(), self.ny)
        return table

    def x_backward(self):
        wide = np.zeros((self.gx * self.xw, LANES))
        own = np.zeros((self.gx * self.xp, LANES))
        waves = self.x_waves()
        for g in range(self.gx):
            x = (g * self.cx - HALO + np.arange(self.xe)) % self.nx
            wide[g * self.xw : g * self.xw + self.xe, : self.nx] = cas_table(x, waves, self.nx)
            x = g * self.cx + np.arange(self.cx)
            own[g * self.xp : g * self.xp + self.cx, : self.nx] = cas_table(x, waves, self.nx)
        scale = 4.0 * np.pi / (self.nx * self.nz)
        return np.concatenate(three(np.concatenate([wide, own], axis=0) * scale), axis=1)

    def plane(self):
        plane = np.full((self.ny, LANES), 1e30)
        lam_x = symbol_table(self.nx)[self.x_waves()]
        plane[:, : self.nx] = lam_x[None, :] + symbol_table(self.ny)[:, None]
        return plane.astype(np.float32)

    def coarse_pack(self):
        parts = [self.x_forward(), thirds(self.y_both()), tower(three(self.y_both()), np)]
        parts += [self.y_ends(), self.x_backward()]
        width = max(part.shape[1] for part in parts)
        self.places, rows = [], 0
        for part in parts:
            self.places.append((rows, part.shape))
            rows = up(rows + part.shape[0], 16)
        table = np.zeros((rows, width), ml_dtypes.bfloat16)
        for (row, shape), part in zip(self.places, parts):
            table[row : row + shape[0], : shape[1]] = part
        return table

    def fine_pack(self):
        parts = [self.plane(), self.y_sources(), self.joins()]
        return np.concatenate([part.reshape(-1, LANES) for part in parts], axis=0)

    def coarse(self, ref, which):
        row, shape = self.places[which]
        return ref[row : row + shape[0], : shape[1]]

    def join_rows(self, ref, row):
        me = lax.axis_index("gx") * self.gl + lax.axis_index("gl")
        size = (2 * HALO + 1) * self.kz
        start = 2 * self.ny + me * size + row * self.kz
        return ref[pl.ds(pl.multiple_of(start, 8), self.kz), :]

    def joins(self):
        lam_x = symbol_table(self.nx)[: self.mirror]
        lam_y, lam_z = symbol_table(self.ny), symbol_table(self.nz)
        total = EPS_PRECOND * (lam_z[:, None, None] + lam_x[None, :, None] + lam_y) + SHIFT_PRECOND
        green = np.real(np.fft.ifft(1.0 / total, axis=-1))
        i = np.arange(HALO)
        near = green[..., np.abs(i[:, None] - i[None, :])]
        far = green[..., i[:, None] + i[None, :] + 1]
        band = np.zeros((HALO, HALO))
        for row in range(HALO):
            for column in range(HALO - row):
                band[row, column] = STENCIL[row + column]
        eye = np.eye(HALO)
        even = np.linalg.inv(eye - 2.0 * (near + far) @ band)
        odd = np.linalg.inv(eye + 2.0 * (near - far) @ band)
        both = np.stack([even, odd], axis=2).reshape(self.ng, self.kz, self.mirror, 2 * HALO, HALO)
        both = both.transpose(0, 3, 1, 4, 2).reshape(self.ng, 2 * HALO, self.kz, HALO * self.mirror)
        table = np.zeros((self.ng, 2 * HALO + 1, self.kz, LANES), np.float32)
        table[:, : 2 * HALO, :, : HALO * self.mirror] = both
        table[:, 2 * HALO] = lam_z.reshape(self.ng, self.kz, 1)
        return table


VMEM_SPEC = pl.BlockSpec(memory_space=pltpu.VMEM)
ANY_SPEC = pl.BlockSpec(memory_space=pl.ANY)


def call(kernel, outs, args, scratch=(), specs=None, limit=VMEM_LIMIT):
    nbytes = sum(int(np.prod(a.shape)) * a.dtype.itemsize for a in (*args, *outs))
    return pl.pallas_call(
        kernel,
        out_shape=tuple(outs),
        in_specs=specs or [VMEM_SPEC] * len(args),
        out_specs=tuple([VMEM_SPEC] * len(outs)),
        scratch_shapes=list(scratch),
        compiler_params=pltpu.CompilerParams(vmem_limit_bytes=limit),
        cost_estimate=pl.CostEstimate(flops=0, bytes_accessed=nbytes, transcendentals=0),
    )(*args)


def lane_index(rows):
    return lax.broadcasted_iota(jnp.int32, (rows, LANES), 1)


def moved(values, shift):
    shift = shift % LANES
    return values if shift == 0 else pltpu.roll(values, shift, 1)


def within(lane, first, count):
    return (lane >= first) & (lane < first + count)


def between(lane, slot, width):
    return within(lane, slot * width, width)


def fetched(pairs, sems):
    copies = [
        pltpu.make_async_copy(source, target, sems.at[i])
        for i, (source, target) in enumerate(pairs)
    ]
    for copy in copies:
        copy.start()
    return copies


def forward_kernel(p, charge_in, high_in, low_in, out, charge, high_z, low_z, sems):
    copies = fetched(((charge_in, charge), (high_in, high_z), (low_in, low_z)), sems)
    copies[0].wait()
    lane = lane_index(p.xp)
    ready = False
    for part in range(2):
        ys = range(part * p.yq, (part + 1) * p.yq)
        high, low = split(jnp.concatenate([padded_rows(charge[y], p.xp) for y in ys], axis=0))
        if not ready:
            copies[1].wait()
        spec = mul(high, high_z[...]) + mul(low, high_z[...])
        if not ready:
            copies[2].wait()
            ready = True
        spec = spec + mul(high, low_z[...])
        for target in range(p.ng):
            chunk, slot = divmod(target, p.group)
            block = jnp.zeros((p.xp, LANES), jnp.float32)
            for i in range(p.yq):
                piece = spec[i * p.xp : (i + 1) * p.xp, chunk * LANES : (chunk + 1) * LANES]
                block = jnp.where(between(lane, i, p.kz), moved(piece, (i - slot) * p.kz), block)
            out[target, part * p.cx : (part + 1) * p.cx] = block[: p.cx]


def table_kernel(p, fine, out):
    plane = fine[: p.ny, :]
    waves = p.join_rows(fine, 2 * HALO)
    for k in range(p.kz):
        symbol = EPS_PRECOND * (plane + waves[k : k + 1]) + SHIFT_PRECOND
        out[:, k * LANES : (k + 1) * LANES] = 1.0 / (float(p.ny) * symbol)


def lanes_of(values, k):
    return values[:, k * LANES : (k + 1) * LANES]


def solve_kernel(p, blocks, coarse, table, spectrum_out, own, sent, turned, ends):
    x_fwd, y_both, y_ends = (p.coarse(coarse, i) for i in (0, 1, 3))
    columns = []
    for gl in range(p.gl):
        for part in range(2):
            pieces = [
                blocks[gx * p.gl + gl, part * p.cx : (part + 1) * p.cx] for gx in range(p.gx)
            ]
            columns.append(jnp.concatenate(pieces, axis=0))
    along_x = mul(x_fwd, stacked(jnp.concatenate(columns, axis=1), 0))
    for b in range(2 * p.gl):
        turned[pl.ds(b * p.step, LANES), :] = lanes_of(along_x, b).T
    field = jnp.concatenate(
        [turned[pl.ds(k, p.ny, stride=p.kz), :] for k in range(p.kz)], axis=1
    )
    along_y = mul(y_both, stacked(padded_rows(field, p.yp), 0))
    solved = along_y * table[...]
    spectrum_out[...] = solved
    at_ends = summed(mul(y_ends, spread(padded_rows(solved, p.yp), 0)))
    for k in range(p.kz):
        ends[pl.ds(k, 8, stride=p.kz), :] = lanes_of(at_ends, k)
    own[...] = ends[pl.ds(0, 2 * HALO * p.kz), :]
    piece = [ends[pl.ds(j * p.kz, p.kz), :] for j in range(2 * HALO)]
    lane = lane_index(p.kz)
    free = LANES - p.nx
    for i in range(4):
        spare = moved(piece[4 + i // 2], p.nx if i % 2 == 0 else p.nx - free)
        sent[pl.ds(i * p.kz, p.kz), :] = jnp.where(lane < p.nx, piece[i], spare)


def return_kernel(
    p, spectrum_in, own, received, table, fine, coarse,
    out, sources, planes,
):
    y_back, x_bwd = p.coarse(coarse, 2), p.coarse(coarse, 4)
    one, two, last = (x_bwd[:, i * LANES : (i + 1) * LANES] for i in range(3))
    columns = fine[p.ny : 2 * p.ny, :]
    y_sources = [jnp.broadcast_to(columns[:, j : j + 1], columns.shape) for j in range(2 * HALO)]
    lane = lane_index(p.kz)
    free = LANES - p.nx
    part = [received[pl.ds(i * p.kz, p.kz), :] for i in range(4)]
    other = [jnp.where(lane < p.nx, value, 0.0) for value in part]
    for i in range(2):
        first = moved(part[2 * i], -p.nx)
        second = moved(part[2 * i + 1], free - p.nx)
        other.append(jnp.where(lane < free, first, jnp.where(lane < p.nx, second, 0.0)))
    mine = [own[pl.ds(j * p.kz, p.kz), :] for j in range(2 * HALO)]
    jump = [mine[j] - other[j] for j in range(2 * HALO)]
    even = [jump[j] + jump[HALO + j] for j in range(HALO)]
    odd = [jump[j] - jump[HALO + j] for j in range(HALO)]

    def mixed(base, vector):
        results = []
        for i in range(HALO):
            packed = p.join_rows(fine, base + i)
            total = 0.0
            for j in range(HALO):
                first = moved(packed, -j * p.mirror)
                second = moved(packed, p.mirror - 1 - j * p.mirror)
                total = total + jnp.where(lane < p.mirror, first, second) * vector[j]
            results.append(total)
        return results

    even_full, odd_full = mixed(0, even), mixed(HALO, odd)
    low_full = [0.5 * (e + o) for e, o in zip(even_full, odd_full)]
    high_full = [0.5 * (e - o) for e, o in zip(even_full, odd_full)]
    far_low = [other[j] - 0.5 * (low_full[j] - jump[j]) for j in range(HALO)]
    far_high = [other[HALO + j] - 0.5 * (high_full[j] - jump[HALO + j]) for j in range(HALO)]
    for i in range(HALO):
        sources[pl.ds(i * p.kz, p.kz), :] = sum(
            STENCIL[i + j] * high_full[j] for j in range(HALO - i)
        )
        sources[pl.ds((HALO + i) * p.kz, p.kz), :] = sum(
            STENCIL[i + j] * low_full[j] for j in range(HALO - i)
        )
    whole = []
    for k in range(p.kz):
        added = sum(y_sources[j] * sources[pl.ds(j * p.kz + k, 1), :] for j in range(2 * HALO))
        whole.append(
            spectrum_in[:, k * LANES : (k + 1) * LANES]
            + added * table[:, k * LANES : (k + 1) * LANES]
        )
    back_y = summed(mul(y_back, spread(padded_rows(jnp.concatenate(whole, axis=1), p.yp), 0)))
    base = p.edge
    for k in range(p.kz):
        planes[pl.ds(base + k, p.ny, stride=p.kz), :] = lanes_of(back_y, k)
    after = base + p.ny * p.kz
    for i in range(HALO):
        planes[pl.ds(base - (i + 1) * p.kz, p.kz), :] = far_high[i]
        planes[pl.ds(after + i * p.kz, p.kz), :] = far_low[i]
    cut = p.gx * p.xw
    wide_rows = tower([part[:cut] for part in (one, two, last)], jnp)
    own_rows = tower([part[cut:] for part in (one, two, last)], jnp)
    rest = p.rows - 2 * p.xe - p.cx

    def filled(pieces, part):
        first = base + (gl + 1) * 2 * p.step + p.edge - p.kz + part * p.third
        pieces = [planes[pl.ds(at, count), :] for at, count in (*pieces, (first, p.third))]
        return padded_rows(jnp.concatenate(pieces, axis=0), LANES)

    for gl in range(p.gl):
        start = base + gl * 2 * p.step
        end = start + 2 * p.step
        both = [filled([(start + i * p.step, p.step)], i) for i in range(2)]
        wide = summed(mul_t(wide_rows, spread(jnp.concatenate(both, axis=0), 1)))
        sides = filled([(start - p.edge, p.edge), (end, p.edge - p.kz)], 2)
        side = summed(mul_t(own_rows, spread(sides, 1)))
        for gx in range(p.gx):
            target = gx * p.gl + gl
            for half in range(2):
                out[target, half * p.xe : (half + 1) * p.xe] = wide[
                    gx * p.xw : gx * p.xw + p.xe, half * LANES : (half + 1) * LANES
                ]
            at, line = 2 * p.xe, gx * p.xp
            out[target, at : at + p.cx] = side[line : line + p.cx]
            if rest:
                out[target, at + p.cx :] = jnp.zeros((rest, LANES), jnp.float32)


def faces_kernel(p, eps, ex_low, ex_high, ey_low, ey_high, faces_x, faces_y, faces_z, mass):
    for y in range(p.cy):
        here = eps[y]
        line = jnp.concatenate([ex_low[y], here, ex_high[y]], axis=0)
        faces_x[y, : p.cx + 3] = line[: p.cx + 3] + line[1 : p.cx + 4]
        faces_z[y] = here + pltpu.roll(here, p.nz - 1, 1)
        mass[y] = (KAPPA_SCALE / (EPS_SOLVENT - 1.0)) * (here - 1.0)
    planes = [ey_low[0], ey_low[1], *[eps[y] for y in range(p.cy)], ey_high[0], ey_high[1]]
    for y in range(p.cy + 3):
        faces_y[y] = planes[y] + planes[y + 1]


def stencil_kernel(
    p, blocks, high_z, low_z, last_z, charge, faces_x, faces_y, faces_z, mass,
    pre, image, sums, field,
):
    lane = lane_index(p.xw)
    side = 2 * p.xe

    def line_of(chunk, first, rows, source_lane, skip, count):
        here = lane[:rows]
        line = jnp.zeros((rows, LANES), jnp.float32)
        for slot in range(min(p.group, p.ng - chunk * p.group)):
            part = blocks[chunk * p.group + slot, first : first + rows, :]
            at = slot * p.kz + skip
            line = jnp.where(within(here, at, count), moved(part, at - source_lane), line)
        return line

    def plain(first, rows, piece):
        return rows, lambda chunk: line_of(chunk, first, rows, piece * p.kz, 0, p.kz)

    def last_layer(chunk):
        total = 0.0
        for part, row in enumerate((HALO, p.xe + HALO, side)):
            first = max(0, row - HALO) // 8 * 8 if part < 2 else row // 8 * 8
            rows = p.xw if part < 2 else p.xp
            line = line_of(chunk, first, rows, p.step, part * p.third, p.third)
            total = total + line[row - first : row - first + p.cx]
        return padded_rows(total, p.xp)

    windows = [plain(y // p.yq * p.xe // 8 * 8, p.xw, y % p.yq) for y in range(p.cy)]
    windows += [plain(side // 8 * 8, p.xp, h) for h in range(2 * HALO - 1)]
    windows.append((p.xp, last_layer))
    one, two, last = high_z[...], low_z[...], last_z[...]
    six_z = jnp.concatenate([one, one, one, two, two, last], axis=1)

    def assembled(group):
        parts = []
        for chunk in range(p.chunks):
            parts.append(jnp.concatenate([make(chunk) for rows, make in group], axis=0))
        return jnp.concatenate(parts, axis=1)

    groups = [windows[: p.yq + 3], windows[p.yq + 3 :]]
    results = []
    for group in groups:
        value = assembled(group)
        rows = value.shape[0]
        parts, rest = [], value
        for _ in range(3):
            parts.append(rest.astype(jnp.bfloat16))
            rest = rest - parts[-1].astype(jnp.float32)
        tall = mul_t(jnp.concatenate(parts, axis=0), one)
        second = mul_t(jnp.concatenate(parts[:2], axis=0), two)
        small = tall[2 * rows :] + second[rows:] + mul_t(parts[0], last)
        results.append(tall[:rows] + ((tall[rows : 2 * rows] + second[:rows]) + small))
    whole = jnp.concatenate(results, axis=0)
    starts = np.cumsum([0] + [rows for rows, make in windows])
    for y in range(p.cy):
        at = int(starts[y]) + y // p.yq * p.xe % 8
        field[HALO + y, : p.xe] = whole[at : at + p.xe]
    for h in range(2 * HALO):
        at = int(starts[p.cy + h]) + (side % 8 if h < 2 * HALO - 1 else 0)
        y = h if h < HALO else h + p.cy
        field[y, HALO : HALO + p.cx] = whole[at : at + p.cx]

    def stretch(flux_at):
        return 27.0 * (flux_at(2) - flux_at(1)) - (flux_at(3) - flux_at(0))

    rz = jnp.zeros((p.cx, LANES), jnp.float32)
    dot = jnp.zeros((p.cx, LANES), jnp.float32)
    fluxes_y = {}

    def flux_y(y):
        if y not in fluxes_y:
            val = [field[y + i, HALO : HALO + p.cx, :] for i in range(4)]
            fluxes_y[y] = faces_y[y] * stretch(lambda i: val[i])
        return fluxes_y[y]

    n = p.nz
    for y in range(p.cy):
        line = field[HALO + y]
        flux = faces_x[y, : p.cx + 3] * stretch(lambda i: line[i : i + p.cx + 3])
        term = stretch(lambda i: flux[i : i + p.cx])
        term = term + stretch(lambda i: flux_y(y + i))
        here = line[HALO : HALO + p.cx]
        grad = 27.0 * (pltpu.roll(here, n - 1, 1) - here) - (
            pltpu.roll(here, n - 2, 1) - pltpu.roll(here, 1, 1)
        )
        flux = faces_z[y] * grad
        term = term + (
            27.0 * (flux - pltpu.roll(flux, 1, 1))
            - (pltpu.roll(flux, n - 1, 1) - pltpu.roll(flux, 2, 1))
        )
        result = mass[y] * here - term * (0.5 / 576.0)
        pre[y] = here
        image[y] = result
        one = charge[y] * here
        two = result * here
        for c in range(n // LANES):
            rz = rz + one[:, c * LANES : (c + 1) * LANES]
            dot = dot + two[:, c * LANES : (c + 1) * LANES]
    rz = jnp.sum(rz, axis=0, keepdims=True)
    dot = jnp.sum(dot, axis=0, keepdims=True)
    half = LANES // 2
    rz = rz + pltpu.roll(rz, half, 1)
    dot = dot + pltpu.roll(dot, half, 1)
    both = jnp.where(lane_index(1) < half, rz, dot)
    sums[...] = jnp.broadcast_to(both[None], sums.shape)


def update_kernel(p, sums, charge, pre, image, solution_field, residual):
    half = LANES // 2
    total = jnp.sum(sums[...], axis=0)
    lane = lane_index(1)
    rz = jnp.sum(jnp.where(lane < half, total, 0.0), axis=1, keepdims=True)
    dot = jnp.sum(jnp.where(lane < half, 0.0, total), axis=1, keepdims=True)
    alpha = jnp.broadcast_to((4.0 * math.pi) * rz / dot, (p.cx, p.nz))
    for y in range(p.cy):
        solution_field[y] = alpha * pre[y]
        residual[y] = (4.0 * math.pi) * charge[y] - alpha * image[y]


def local_planes(p, density, charge):
    group = ("gx", "gl")
    along_y = ("gh", "gl")
    f32 = jnp.float32

    def shape(*dims):
        return jax.ShapeDtypeStruct(dims, f32)

    def pairs(count, first):
        low = range(first, count, 2)
        near = [(i, (i + 1) % count) for i in low]
        return near + [(target, source) for source, target in near]

    even_x = lax.axis_index("gx") % 2 == 0
    even_y = lax.axis_index("gl") % 2 == 0

    density = density.transpose(1, 0, 2)
    charge = charge.transpose(1, 0, 2)
    high_z, low_z, last_z = (jnp.asarray(part) for part in p.z_forward())
    coarse, fine = jnp.asarray(p.coarse_pack()), jnp.asarray(p.fine_pack())
    (blocks,) = call(
        lambda *refs: forward_kernel(p, *refs),
        [shape(p.ng, 2 * p.cx, LANES)],
        [charge, high_z, low_z],
        [
            pltpu.VMEM((p.cy, p.cx, p.nz), f32),
            pltpu.VMEM((p.nz, p.deep), jnp.bfloat16),
            pltpu.VMEM((p.nz, p.deep), jnp.bfloat16),
            pltpu.SemaphoreType.DMA((3,)),
        ],
        specs=[ANY_SPEC] * 3,
        limit=None,
    )
    blocks = lax.all_to_all(blocks, group, 0, 0)
    (table,) = call(
        lambda *refs: table_kernel(p, *refs), [shape(p.ny, p.kz * LANES)], [fine]
    )
    eps = permittivity(density)
    swap_by = lax.ppermute(
        jnp.where(even_y, eps[:2], eps[p.cy - 2 :]), along_y, pairs(2 * p.gl, 1)
    )
    swap_bx = lax.ppermute(
        jnp.where(even_x, eps[:, :2], eps[:, p.cx - 2 :]), "gx", pairs(p.gx, 1)
    )
    swap_ay = lax.ppermute(
        jnp.where(even_y, eps[p.cy - 2 :], eps[:2]), along_y, pairs(2 * p.gl, 0)
    )
    swap_ax = lax.ppermute(
        jnp.where(even_x, eps[:, p.cx - 2 :], eps[:, :2]), "gx", pairs(p.gx, 0)
    )
    blocks, eps, table = lax.optimization_barrier(
        (blocks, eps, table)
    )
    spectrum_half, own, sent = call(
        lambda *refs: solve_kernel(p, *refs),
        [shape(p.ny, p.kz * LANES), shape(2 * HALO * p.kz, LANES), shape(4 * p.kz, LANES)],
        [blocks, coarse, table],
        [pltpu.VMEM((p.ny * p.kz + LANES, LANES), f32), pltpu.VMEM((8 * p.kz, LANES), f32)],
    )
    received = lax.ppermute(sent, "gh", [(0, 1), (1, 0)])
    ex_low, ex_high = jnp.where(even_x, swap_bx, swap_ax), jnp.where(even_x, swap_ax, swap_bx)
    ey_low, ey_high = jnp.where(even_y, swap_by, swap_ay), jnp.where(even_y, swap_ay, swap_by)
    brick = (p.cy, p.cx, p.nz)
    faces = call(
        lambda *refs: faces_kernel(p, *refs),
        [
            shape(p.cy, p.xp, p.nz), shape(p.cy + 3, p.cx, p.nz), shape(*brick), shape(*brick),
        ],
        [eps, ex_low, ex_high, ey_low, ey_high],
    )
    received, *faces = lax.optimization_barrier((received, *faces))
    (blocks,) = call(
        lambda *refs: return_kernel(p, *refs),
        [shape(p.ng, p.rows, LANES)],
        [
            spectrum_half, own, received, table, fine, coarse,
        ],
        [
            pltpu.VMEM((2 * HALO * p.kz, LANES), f32),
            pltpu.VMEM((p.ny * p.kz + 2 * p.edge, LANES), f32),
        ],
    )
    blocks = lax.all_to_all(blocks, group, 0, 0)
    pre, image, sums = call(
        lambda *refs: stencil_kernel(p, *refs),
        [shape(*brick), shape(*brick), shape(2 * p.ng, 1, LANES)],
        [blocks, high_z, low_z, last_z, charge, *faces],
        [
            pltpu.VMEM((p.cy + 2 * HALO, p.xw, p.nz), f32),
        ],
    )
    sums = lax.all_to_all(sums, ("gx", "gh", "gl"), 0, 0)
    solution_field, residual = call(
        lambda *refs: update_kernel(p, *refs),
        [shape(*brick), shape(*brick)],
        [sums, charge, pre, image],
    )
    return solution_field.transpose(1, 0, 2), residual.transpose(1, 0, 2)


def solution(mesh):
    count_x, count_y = mesh.shape["gx"], mesh.shape["gy"]

    def run(density, charge):
        plan = Plan(charge.shape, count_x, count_y)
        if plan.fits():
            split_mesh = jax.sharding.Mesh(
                mesh.devices.reshape(count_x, 2, count_y // 2), ("gx", "gh", "gl")
            )
            spec = P("gx", ("gh", "gl"), None)
            body, over = (lambda *args: local_planes(plan, *args)), split_mesh
        else:
            spec = P("gx", "gy", None)
            body, over = local_lines, mesh
        return jax.shard_map(
            body, mesh=over, in_specs=(spec, spec), out_specs=(spec, spec), check_vma=False
        )(density, charge)

    return run
```
